32 devices in a mesh: member: 8 (over z, x), section: 4 (over y, core).
Axes of the slice: x: 2, y: 2, z: 4, core: 2. Of those that a mesh axis runs over, the one named last changes fastest.
Arguments:
- inputs: bfloat16 [8, 2, 1, 14, 14, 512], P('member'), may hold values from -6 to 6
- cotangent: bfloat16 [8, 2, 1, 14, 14, 512], P('member'), may hold values from -6 to 6
- probe: bfloat16 [8, 1, 14, 14, 512], P('member'), may hold values from -6 to 6
- dw_kernel: float32 [8, 4, 7, 7, 512], P('member', 'section'), may hold values from -0.875 to 0.875
- dw_bias: float32 [8, 4, 512], P('member', 'section'), may hold values from -3 to 3
- norm_gain: float32 [8, 4, 512], P('member', 'section'), may hold values from 0.5 to 1.5
- norm_bias: float32 [8, 4, 512], P('member', 'section'), may hold values from -3 to 3
- w_in: float32 [8, 4, 512, 2048], P('member', 'section'), may hold values from -0.25 to 0.25
- b_in: float32 [8, 4, 2048], P('member', 'section'), may hold values from -3 to 3
- w_out: float32 [8, 4, 2048, 512], P('member', 'section'), may hold values from -0.125 to 0.125
- b_out: float32 [8, 4, 512], P('member', 'section'), may hold values from -3 to 3
- layer_scale: float32 [8, 4, 512], P('member', 'section'), may hold values from 0.3 to 1.5
- shuffle_mask: int32 [4, 32], P('section'), may hold values from 0 to 1, as said below
- source_member: int32 [4, 32, 8], P('section'), may hold values from 0 to 7, as said below
Outputs:
- new_w_in: float32 [8, 4, 512, 2048], P('member', 'section')
- new_w_out: float32 [8, 4, 2048, 512], P('member', 'section')
- features: bfloat16 [8, 4, 1, 14, 14, 512], P('member', 'section')
The draws below stay inside these ranges and needn't reach their ends.
Inputs may be any that keep to these rules, and one draw needn't show every extreme that they name: `shuffle_mask`: each section marks exactly 16 of its 32 blocks. Each source_member[s, k] is a permutation of the members. For the marked blocks of a section no member is its own source, and no member is the source of more than 3 of another member's blocks; some pair of members reaches 3 in every section.
All inputs are finite; a program needn't handle non-finite values.
Results may differ from the reference program's by a relative error of at most 0.014.
Values may be sent and summed in bfloat16 or wider, within the bound.
No kernel may reach another device: no remote copies, remote signals or barrier semaphores. Data moves between devices by JAX's collectives and lax.ppermute only.
A program may use at most 192 MiB of HBM per device.

```python
import math
import jax
import jax.numpy as jnp
from jax import lax

D = 512
HID = 2048
TILE = 128
SIDE = 14
MICRO = 2
IMGS = 1
MEMBERS = 8
SECTIONS = 4
BLOCKS = 32
SHUFFLED = 16


def shuffle_tables(key):
    masks = []
    tables = []
    for section in range(SECTIONS):
        base = jax.random.fold_in(key, 7919 + section)
        key_blocks, key_shifts, key_labels = jax.random.split(base, 3)
        order_blocks = jax.random.permutation(key_blocks, BLOCKS)
        ranking = jnp.argsort(order_blocks).astype(jnp.int32)
        masks.append((ranking < SHUFFLED).astype(jnp.int32))
        shifts = (jax.random.permutation(key_shifts, MEMBERS - 1) + 1).astype(jnp.int32)
        offsets = shifts[ranking % (MEMBERS - 1)]
        labels = jax.random.permutation(key_labels, MEMBERS).astype(jnp.int32)
        inverse = jnp.argsort(labels).astype(jnp.int32)
        tables.append(inverse[(labels[None, :] - offsets[:, None]) % MEMBERS])
    return (jnp.stack(masks).astype(jnp.int32), jnp.stack(tables).astype(jnp.int32))


def draw_shuffle_mask(key, part):
    return shuffle_tables(jax.random.fold_in(key, 31))[0]


def draw_source_member(key, part):
    return shuffle_tables(jax.random.fold_in(key, 31))[1]


def steps_of(rng, shape, pieces, smallest, top_value):
    level = 1.0
    for axis_at, shards_of in pieces:
        heights = jax.random.uniform(jax.random.fold_in(jax.random.fold_in(rng, 6), axis_at), (shards_of,), jnp.float32, smallest / len(pieces), top_value / len(pieces))
        level = level * jnp.repeat(jnp.exp(heights), shape[axis_at] // shards_of).reshape((-1,) + (1,) * (len(shape) - 1 - axis_at))
    return level


def gaussian(key, shape, width, most, pieces=(), held_as=jnp.bfloat16):
    values = width * jax.random.normal(key, shape, jnp.float32)
    if pieces:
        values = values * steps_of(key, shape, pieces, -0.22, 0.18)
    return jnp.clip(values, -most, most).astype(held_as)


def setup_inputs(seed: int = 0) -> dict:
    splits = jax.random.split(jax.random.key(seed), 15)
    inputs = gaussian(splits[0], (MEMBERS, MICRO, IMGS, SIDE, SIDE, D), 1.0, 6.0, ((0, 8),))
    cotangent = gaussian(splits[1], (MEMBERS, MICRO, IMGS, SIDE, SIDE, D), 1.0, 6.0, ((0, 8),))
    probe = gaussian(splits[2], (MEMBERS, IMGS, SIDE, SIDE, D), 1.0, 6.0, ((0, 8),))
    dw_kernel = gaussian(splits[3], (MEMBERS, SECTIONS, 7, 7, D), 49 ** -0.5, 0.875, ((0, 8), (1, 4)), jnp.float32)
    dw_bias = gaussian(splits[4], (MEMBERS, SECTIONS, D), 0.5, 3.0, ((0, 8), (1, 4)), jnp.float32)
    norm_gain = jnp.clip(1.0 + 0.1 * jax.random.normal(splits[5], (MEMBERS, SECTIONS, D), jnp.float32), 0.5, 1.5)
    norm_bias = gaussian(splits[6], (MEMBERS, SECTIONS, D), 0.5, 3.0, ((0, 8), (1, 4)), jnp.float32)
    w_in = gaussian(splits[7], (MEMBERS, SECTIONS, D, HID), D ** -0.5, 0.25, ((0, 8), (1, 4)), jnp.float32)
    b_in = gaussian(splits[8], (MEMBERS, SECTIONS, HID), 0.5, 3.0, ((0, 8), (1, 4)), jnp.float32)
    w_out = gaussian(splits[9], (MEMBERS, SECTIONS, HID, D), HID ** -0.5, 0.125, ((0, 8), (1, 4)), jnp.float32)
    b_out = gaussian(splits[10], (MEMBERS, SECTIONS, D), 0.5, 3.0, ((0, 8), (1, 4)), jnp.float32)
    layer_scale = jnp.clip(jnp.exp(math.log(1.5) - 1.60943787 * jax.random.uniform(splits[11], (MEMBERS, SECTIONS, D), jnp.float32) ** steps_of(splits[11], (MEMBERS, SECTIONS, D), ((0, 8), (1, 4)), -0.2, 0.2)), 0.3, 1.5)
    shuffle_mask = draw_shuffle_mask(jax.random.fold_in(splits[14], 71), 0)
    source_member = draw_source_member(jax.random.fold_in(splits[14], 71), 0)
    return dict(inputs=inputs, cotangent=cotangent, probe=probe, dw_kernel=dw_kernel, dw_bias=dw_bias, norm_gain=norm_gain, norm_bias=norm_bias, w_in=w_in, b_in=b_in, w_out=w_out, b_out=b_out, layer_scale=layer_scale, shuffle_mask=shuffle_mask, source_member=source_member)


learning_rate = 0.001
norm_epsilon = 1e-06

def block(params, incoming):
    kernel, conv_bias, gain, shift_bias, first_weight, first_bias, second_weight, second_bias, scale = params
    widened = incoming.astype(jnp.float32)
    channels = widened.shape[-1]
    spread = lax.conv_general_dilated(widened, kernel.reshape(kernel.shape[0], kernel.shape[1], 1, channels), (1, 1), 'SAME', dimension_numbers=('NHWC', 'HWIO', 'NHWC'), feature_group_count=channels, precision=lax.Precision.HIGHEST) + conv_bias
    center = lax.optimization_barrier(jnp.mean(spread, axis=-1, keepdims=True))
    offset = spread - center
    variance = lax.optimization_barrier(jnp.mean(offset * offset, axis=-1, keepdims=True))
    normed = (offset * lax.rsqrt(variance + norm_epsilon) * gain + shift_bias).astype(jnp.bfloat16)
    rows = normed.reshape(-1, channels)
    hidden = jax.nn.gelu(jnp.dot(rows, first_weight, preferred_element_type=jnp.float32) + first_bias, approximate=False).astype(jnp.bfloat16)
    mixed = jnp.dot(hidden, second_weight, preferred_element_type=jnp.float32) + second_bias
    return (widened + scale * mixed.reshape(widened.shape)).astype(jnp.bfloat16)

def lowered(params):
    return tuple((leaf.astype(jnp.bfloat16) if position in (4, 6) else leaf for position, leaf in enumerate(params)))

def train_member(member_data):
    images = member_data[0]
    slopes = member_data[1]
    stacked = member_data[2:]
    initials = [tuple((leaf[section] for leaf in stacked)) for section in range(SECTIONS)]
    section_params = [lowered(initial) for initial in initials]
    totals = [tuple((jnp.zeros(leaf.shape, jnp.float32) for leaf in params)) for params in section_params]
    for micro in range(MICRO):
        stored = []
        current = images[micro]
        for section in range(SECTIONS):
            stored.append(current)
            current = block(section_params[section], current)
        slope = slopes[micro]
        for section in reversed(range(SECTIONS)):
            unused, pull = jax.vjp(block, section_params[section], stored[section])
            delta, slope = pull(slope)
            totals[section] = tuple((total + piece.astype(jnp.float32) for total, piece in zip(totals[section], delta)))
    updated = [tuple((leaf - learning_rate * total for leaf, total in zip(initials[section], totals[section]))) for section in range(SECTIONS)]
    return tuple((jnp.stack([updated[section][position] for section in range(SECTIONS)]) for position in range(9)))

def probe_member(member_data):
    current = member_data[0]
    stacked = member_data[1:]
    outputs = []
    for section in range(SECTIONS):
        params = lowered(tuple((leaf[section] for leaf in stacked)))
        current = block(params, current)
        outputs.append(current)
    return jnp.stack(outputs)

def reference(inputs, cotangent, probe, dw_kernel, dw_bias, norm_gain, norm_bias, w_in, b_in, w_out, b_out, layer_scale, shuffle_mask, source_member):
    updated = lax.map(train_member, (inputs, cotangent, dw_kernel, dw_bias, norm_gain, norm_bias, w_in, b_in, w_out, b_out, layer_scale))
    tile_count = HID // TILE
    row_groups = HID // D
    column_tiles = D // TILE
    sources = jnp.transpose(source_member, (2, 0, 1))
    section_index = jnp.arange(SECTIONS, dtype=jnp.int32)
    first_view = updated[4].reshape(MEMBERS, SECTIONS, D, tile_count, TILE)
    moved_first = first_view[sources[:, :, :tile_count], section_index[None, :, None], :, jnp.arange(tile_count, dtype=jnp.int32)[None, None, :], :]
    moved_first = jnp.transpose(moved_first, (0, 1, 3, 2, 4))
    marked_first = shuffle_mask[:, :tile_count][None, :, None, :, None] == 1
    new_first = jnp.where(marked_first, moved_first, first_view).reshape(MEMBERS, SECTIONS, D, HID)
    second_view = updated[6].reshape(MEMBERS, SECTIONS, row_groups, D, column_tiles, TILE)
    second_sources = sources[:, :, tile_count:].reshape(MEMBERS, SECTIONS, column_tiles, row_groups)
    moved_second = second_view[second_sources, section_index[None, :, None, None], jnp.arange(row_groups, dtype=jnp.int32)[None, None, None, :], :, jnp.arange(column_tiles, dtype=jnp.int32)[None, None, :, None], :]
    moved_second = jnp.transpose(moved_second, (0, 1, 3, 4, 2, 5))
    marked_second = jnp.transpose(shuffle_mask[:, tile_count:].reshape(SECTIONS, column_tiles, row_groups), (0, 2, 1))[None, :, :, None, :, None] == 1
    new_second = jnp.where(marked_second, moved_second, second_view).reshape(MEMBERS, SECTIONS, HID, D)
    features = lax.map(probe_member, (probe, updated[0], updated[1], updated[2], updated[3], new_first, updated[5], new_second, updated[7], updated[8]))
    return (new_first, new_second, features)
```

```python
import functools
import math

import jax
import jax.numpy as jnp
from jax import lax
from jax.experimental import pallas as pl
from jax.experimental.pallas import tpu as pltpu
from jax.sharding import PartitionSpec as P

TILE = 128
learning_rate = 0.001
norm_epsilon = 1e-06
F32 = jnp.float32
BF16 = jnp.bfloat16
EDGE = 8
REACH = 3
TAPS = 2 * REACH + 1
VMEM_LIMIT = 40 * 1024 * 1024

ERF_TOP = (
    0.00022905065861350646,
    0.0034082910107109506,
    0.050955695062380861,
    0.18520832239976145,
    1.128379143519084,
)
ERF_LOW = (
    -1.1791602954361697e-7,
    0.000023547966471313185,
    0.0010179625278914885,
    0.014070470171167667,
    0.11098505178285362,
    0.49746925110067538,
    1.0,
)


def erf(value):
    value = jnp.clip(value, -3.832506856900711, 3.832506856900711)
    square = value * value
    top = jnp.full_like(square, ERF_TOP[0])
    for term in ERF_TOP[1:]:
        top = top * square + term
    low = jnp.full_like(square, ERF_LOW[0])
    for term in ERF_LOW[1:]:
        low = low * square + term
    return value * top / low


def whole(array):
    rank = len(array.shape)
    return pl.BlockSpec(array.shape, lambda *args: (0,) * rank)


def lanes(index):
    return pl.ds(pl.multiple_of(index * TILE, TILE), TILE)


def shaped(shape, dtype):
    return jax.ShapeDtypeStruct(shape, dtype)


def convolve(padded, chunk, kernel_ref, height, width, flip, store):
    totals = [None] * height
    for col in range(TAPS):
        taps = []
        for row in range(TAPS):
            at = row * TAPS + col
            if flip:
                at = TAPS * TAPS - 1 - at
            taps.append(kernel_ref[at : at + 1, lanes(chunk)])
        for line in range(height + TAPS - 1):
            values = padded[chunk, line, pl.ds(EDGE - REACH + col, width), :]
            for row in range(TAPS):
                out = line - row
                if 0 <= out < height:
                    term = values * taps[row]
                    totals[out] = term if totals[out] is None else totals[out] + term
    for out in range(height):
        store(out, totals[out])


def fill_padded(padded, maps):
    height, width, channels = maps.shape
    padded[...] = jnp.zeros(padded.shape, F32)
    for chunk in range(channels // TILE):
        padded[chunk, REACH : REACH + height, EDGE : EDGE + width, :] = maps[
            :, :, chunk * TILE : (chunk + 1) * TILE
        ]


def real_columns(shape, side):
    return lax.broadcasted_iota(jnp.int32, shape, 1) < side


def normalise(spread):
    center = jnp.mean(spread, axis=-1, keepdims=True)
    offset = spread - center
    variance = jnp.mean(offset * offset, axis=-1, keepdims=True)
    inverse = lax.rsqrt(variance + norm_epsilon)
    return offset * inverse, inverse


def forward_core(side, vectors, widened, padded, spread, total, weights, n_ref, hidden_store):
    kernel_ref, bias_ref, gain_ref, shift_ref, first_bias_ref, second_bias_ref, scale_ref = vectors
    height, width, channels = widened.shape
    rows = height * width
    hid = first_bias_ref.shape[1]
    fill_padded(padded, widened)

    def conv_body(chunk, carry):
        bias = bias_ref[0:1, lanes(chunk)]

        def store(out, value):
            spread[out * width : (out + 1) * width, lanes(chunk)] = value + bias

        convolve(padded, chunk, kernel_ref, height, width, False, store)
        return carry

    lax.fori_loop(0, channels // TILE, conv_body, 0)
    hat, inverse = normalise(spread[...])
    n_ref[...] = (hat * gain_ref[...] + shift_ref[...]).astype(BF16)
    total[...] = jnp.zeros(total.shape, F32)

    def mix_body(piece, carry):
        first, second = weights(piece)
        at = pl.ds(pl.multiple_of(piece * channels, channels), channels)
        pre = jnp.dot(n_ref[...], first, preferred_element_type=F32) + first_bias_ref[:, at]
        below = 0.5 + 0.5 * erf(pre * math.sqrt(0.5))
        hidden = (pre * below).astype(BF16)
        hidden_store(at, hidden, pre, below)
        total[...] += jnp.dot(hidden, second, preferred_element_type=F32)
        return carry

    lax.fori_loop(0, hid // channels, mix_body, 0)
    mixed = total[...] + second_bias_ref[...]
    result = widened + (scale_ref[...] * mixed).reshape(height, width, channels)
    result = jnp.where(real_columns(result.shape, side), result, 0.0)
    return result, mixed, hat, inverse


def is_active(sec_ref, tick, count):
    which = tick - sec_ref[0]
    return (which >= 0) & (which < count)


def slot_of(which, count):
    return jnp.where((which >= 0) & (which < count), which, count)


def train_kernel(tick, micro, side, kept, sec_ref, image_ref, received_ref, *refs):
    vectors, (first_ref, second_ref) = refs[:7], refs[7:9]
    refs = refs[9 + kept :]
    y_ref, x_ref, hat_ref, inverse_ref, n_ref, h_ref, slope_ref, mixed_ref = refs[:8]
    padded, spread, total = refs[8:]

    @pl.when(is_active(sec_ref, tick, micro))
    def _():
        channels = x_ref.shape[-1]
        entry = jnp.where(sec_ref[0] == 0, image_ref[0].astype(F32), received_ref[...].astype(F32))
        x_ref[0] = entry.astype(BF16)

        def weights(piece):
            at = pl.ds(pl.multiple_of(piece * channels, channels), channels)
            return first_ref[:, at], second_ref[at, :]

        def hidden_store(at, hidden, pre, below):
            h_ref[0, :, at] = hidden
            density = jnp.exp(-0.5 * pre * pre) * (1.0 / math.sqrt(2.0 * math.pi))
            slope_ref[0, :, at] = (below + pre * density).astype(BF16)

        result, mixed, hat, inverse = forward_core(
            side, vectors, entry, padded, spread, total, weights, n_ref.at[0], hidden_store
        )
        y_ref[...] = result.astype(BF16)
        hat_ref[0] = hat
        inverse_ref[0] = jnp.broadcast_to(inverse, inverse_ref.shape[1:])
        mixed_ref[0] = mixed


def probe_kernel(tick, side, sec_ref, marked_ref, slot_ref, image_ref, received_ref, *refs):
    vectors, (own_ref, arrived_ref) = refs[:7], refs[7:9]
    y_ref, padded, spread, total, n_ref = refs[9:]

    @pl.when(sec_ref[0] == tick)
    def _():
        channels = y_ref.shape[-1]
        tiles = channels // TILE
        groups = vectors[4].shape[1] // channels
        entry = image_ref[...] if tick == 0 else received_ref[...]

        def tile(block):
            taken = marked_ref[block] == 1
            return jnp.where(taken, arrived_ref[slot_ref[block]], own_ref[block])

        def weights(piece):
            first = [tile(piece * tiles + item) for item in range(tiles)]
            second = [tile(groups * tiles + item * groups + piece) for item in range(tiles)]
            return jnp.concatenate(first, axis=1), jnp.concatenate(second, axis=1)

        result, mixed, hat, inverse = forward_core(
            side,
            vectors,
            entry.astype(F32),
            padded,
            spread,
            total,
            weights,
            n_ref,
            lambda at, hidden, pre, below: None,
        )
        y_ref[...] = result.astype(BF16)


def back_kernel(tick, micro, side, sections, kept, sec_ref, slope_in_ref, returned_ref, *refs):
    kernel_ref, gain_ref, scale_ref, first_ref, second_ref = refs[:5]
    hat_ref, inverse_ref, slope_ref = refs[5:8]
    refs = refs[8 + kept :]
    dx_ref, dy_ref, dmix_ref, dpre_ref, dn_ref, dspread_ref = refs[:6]
    padded, total, conv_out = refs[6:]
    which = tick - (sections - 1 - sec_ref[0])

    @pl.when((which >= 0) & (which < micro))
    def _():
        height, width, channels = dx_ref.shape
        rows = height * width
        hid = slope_ref.shape[-1]
        dy = jnp.where(
            sec_ref[0] == sections - 1, slope_in_ref[0].astype(F32), returned_ref[...].astype(F32)
        )
        flat = dy.reshape(rows, channels)
        dy_ref[0] = flat.astype(BF16)
        dmix_ref[0] = (flat * scale_ref[...]).astype(BF16)
        total[...] = jnp.zeros(total.shape, F32)
        contract = (((1,), (1,)), ((), ()))

        def body(piece, carry):
            at = pl.ds(pl.multiple_of(piece * channels, channels), channels)
            dh = lax.dot_general(dmix_ref[0], second_ref[at, :], contract, preferred_element_type=F32)
            dpre = (dh * slope_ref[0, :, at].astype(F32)).astype(BF16)
            dpre_ref[0, :, at] = dpre
            total[...] += lax.dot_general(
                dpre, first_ref[:, at], contract, preferred_element_type=F32
            )
            return carry

        lax.fori_loop(0, hid // channels, body, 0)
        dn = total[...]
        dn_ref[0] = dn.astype(BF16)
        hat = hat_ref[0]
        dhat = dn * gain_ref[...]
        mean = jnp.mean(dhat, axis=-1, keepdims=True)
        along = jnp.mean(dhat * hat, axis=-1, keepdims=True)
        dspread = inverse_ref[0, :, 0:1] * (dhat - mean - hat * along)
        dspread_ref[0] = dspread
        if tick < micro + sections - 2:
            fill_padded(padded, dspread.reshape(height, width, channels))

            def conv_body(chunk, carry):
                def store(out, value):
                    conv_out[out, :, lanes(chunk)] = value

                convolve(padded, chunk, kernel_ref, height, width, True, store)
                return carry

            lax.fori_loop(0, channels // TILE, conv_body, 0)
            dx = dy + conv_out[...]
            dx = jnp.where(real_columns(dx.shape, side), dx, 0.0)
            dx_ref[...] = dx.astype(BF16)


def small_kernel(micro, *refs):
    (kernel_ref, bias_ref, gain_ref, shift_ref, first_bias_ref, second_bias_ref, scale_ref) = refs[:7]
    x_ref, hat_ref, mixed_ref, dy_ref, dpre_ref, dn_ref, dspread_ref = refs[7:14]
    outs = refs[14:21]
    padded = refs[21]
    height, width, channels = x_ref.shape[1:]

    def total(values):
        return jnp.sum(values, axis=0, keepdims=True)

    def chunk_body(chunk, carry):
        at = lanes(chunk)
        scale = scale_ref[0:1, at]
        sums = [0.0] * 5
        for item in range(micro):
            dy = dy_ref[item, :, at].astype(F32)
            dn = dn_ref[item, :, at].astype(F32)
            sums[0] += total(dspread_ref[item, :, at])
            sums[1] += total(dn * hat_ref[item, :, at])
            sums[2] += total(dn)
            sums[3] += total(dy)
            sums[4] += total(dy * mixed_ref[item, :, at])
        outs[1][0:1, at] = bias_ref[0:1, at] - learning_rate * sums[0]
        outs[2][0:1, at] = gain_ref[0:1, at] - learning_rate * sums[1]
        outs[3][0:1, at] = shift_ref[0:1, at] - learning_rate * sums[2]
        outs[5][0:1, at] = second_bias_ref[0:1, at] - learning_rate * (scale * sums[3])
        outs[6][0:1, at] = scale - learning_rate * sums[4]
        padded[...] = jnp.zeros(padded.shape, F32)
        for item in range(micro):
            padded[item, REACH : REACH + height, EDGE : EDGE + width, :] = x_ref[
                item, :, :, at
            ].astype(F32)
        for col in range(TAPS):
            for row in range(TAPS):
                acc = None
                for item in range(micro):
                    for out in range(height):
                        term = (
                            padded[item, out + row, pl.ds(EDGE - REACH + col, width), :]
                            * dspread_ref[item, out * width : (out + 1) * width, at]
                        )
                        acc = term if acc is None else acc + term
                tap = row * TAPS + col
                outs[0][tap : tap + 1, at] = kernel_ref[tap : tap + 1, at] - learning_rate * total(acc)
        return carry

    lax.fori_loop(0, channels // TILE, chunk_body, 0)
    hid = first_bias_ref.shape[1]

    def bias_body(piece, carry):
        at = lanes(piece)
        acc = 0.0
        for item in range(micro):
            acc += total(dpre_ref[item, :, at].astype(F32))
        outs[4][0:1, at] = first_bias_ref[0:1, at] - learning_rate * acc
        return carry

    lax.fori_loop(0, hid // TILE, bias_body, 0)


def weight_step(first_tiles, groups, block, n_ref, dpre_ref, h_ref, dmix_ref, first_ref, second_ref, emit):
    rows = n_ref.shape[0] * n_ref.shape[1]
    channels = n_ref.shape[2]
    contract = (((0,), (0,)), ((), ()))

    @pl.when(block < first_tiles)
    def _():
        grad = lax.dot_general(
            n_ref[...].reshape(rows, channels),
            dpre_ref[...].reshape(rows, TILE),
            contract,
            preferred_element_type=F32,
        )
        emit(True, first_ref[...] - learning_rate * grad)

    @pl.when(block >= first_tiles)
    def _():
        group = lax.rem(block - first_tiles, groups)
        at = pl.ds(pl.multiple_of(group * channels, channels), channels)
        grad = lax.dot_general(
            h_ref[:, :, at].reshape(rows, channels),
            dmix_ref[...].reshape(rows, TILE),
            contract,
            preferred_element_type=F32,
        )
        emit(False, second_ref[...] - learning_rate * grad)


def send_kernel(first_tiles, groups, order_ref, slot_ref, n, dpre, h, dmix, first, second, send_ref):
    step = pl.program_id(0)

    def emit(is_first, updated):
        send_ref[0] = updated.astype(BF16)

    weight_step(first_tiles, groups, order_ref[step], n, dpre, h, dmix, first, second, emit)


def keep_kernel(
    first_tiles, groups, order_ref, edge_ref, n, dpre, h, dmix, first, second, own_ref, new_first, new_second
):
    step = pl.program_id(0)

    def emit(is_first, updated):
        own_ref[0] = updated.astype(BF16)
        if is_first:
            new_first[...] = updated
        else:
            new_second[...] = updated

    weight_step(first_tiles, groups, order_ref[step], n, dpre, h, dmix, first, second, emit)


def place_kernel(
    first_tiles, order_ref, edge_ref, slot_ref, arrived_ref, old_first, old_second, new_first, new_second
):
    step = pl.program_id(0)
    block = order_ref[step]

    @pl.when(step == 0)
    def _():
        new_first[...] = old_first[...]
        new_second[...] = old_second[...]

    @pl.when(block < first_tiles)
    def _():
        new_first[...] = arrived_ref[0].astype(F32)

    @pl.when(block >= first_tiles)
    def _():
        new_second[...] = arrived_ref[0].astype(F32)


def params_of(limit=VMEM_LIMIT):
    return pltpu.CompilerParams(vmem_limit_bytes=limit)


def cost(flops, read):
    return pl.CostEstimate(flops=flops, bytes_accessed=read, transcendentals=0)


def any_spec():
    return pl.BlockSpec(memory_space=pl.ANY)


def train_step(tick, micro, side, sec, images, received, vectors, weights, saved):
    height, width, channels = received.shape
    rows = height * width
    hid = vectors[4].shape[1]

    def slotted(*shape):
        rank = len(shape)
        return pl.BlockSpec(
            (1,) + shape, lambda i, s: (slot_of(tick - s[0], micro),) + (0,) * rank
        )

    saved_shapes = [
        ((height, width, channels), BF16),
        ((rows, channels), F32),
        ((rows, TILE), F32),
        ((rows, channels), BF16),
        ((rows, hid), BF16),
        ((rows, hid), BF16),
        ((rows, channels), F32),
    ]
    kept = 0 if saved is None else len(saved)
    at = min(tick, micro - 1)
    operands = [images, received, *vectors, *weights] + ([] if saved is None else list(saved))
    in_specs = [pl.BlockSpec((1, height, width, channels), lambda i, s: (at, 0, 0, 0))]
    in_specs += [whole(item) for item in operands[1 : len(operands) - kept]]
    in_specs += [any_spec()] * kept
    outs = pl.pallas_call(
        functools.partial(train_kernel, tick, micro, side, kept),
        grid_spec=pltpu.PrefetchScalarGridSpec(
            num_scalar_prefetch=1,
            grid=(1,),
            in_specs=in_specs,
            out_specs=[whole(received)] + [slotted(*shape) for shape, _ in saved_shapes],
            scratch_shapes=[
                pltpu.VMEM((channels // TILE, height + 2 * REACH, width + 2 * EDGE, TILE), F32),
                pltpu.VMEM((rows, channels), F32),
                pltpu.VMEM((rows, channels), F32),
            ],
        ),
        out_shape=[shaped(received.shape, BF16)]
        + [shaped((micro + 1,) + shape, dtype) for shape, dtype in saved_shapes],
        input_output_aliases={1 + len(operands) - kept + i: 1 + i for i in range(kept)},
        compiler_params=params_of(),
        cost_estimate=cost(4 * rows * channels * hid, 8 << 20),
        name=f"train{tick}",
    )(sec, *operands)
    return outs[0], outs[1:]


def back_step(tick, micro, side, sections, sec, slopes, returned, params, saved, kept_out):
    height, width, channels = returned.shape
    rows = height * width
    kernel, gain, scale, first, second = params
    hat, inverse, slope = saved
    hid = slope.shape[-1]

    def which(s):
        return tick - (sections - 1 - s[0])

    def slotted(*shape):
        rank = len(shape)
        return pl.BlockSpec((1,) + shape, lambda i, s: (slot_of(which(s), micro),) + (0,) * rank)

    def held(*shape):
        rank = len(shape)
        return pl.BlockSpec(
            (1,) + shape, lambda i, s: (jnp.clip(which(s), 0, micro - 1),) + (0,) * rank
        )

    shapes = [
        ((rows, channels), BF16),
        ((rows, channels), BF16),
        ((rows, hid), BF16),
        ((rows, channels), BF16),
        ((rows, channels), F32),
    ]
    kept = 0 if kept_out is None else len(kept_out)
    operands = [slopes, returned, kernel, gain, scale, first, second, hat, inverse, slope]
    at = min(tick, micro - 1)
    in_specs = [pl.BlockSpec((1, height, width, channels), lambda i, s: (at, 0, 0, 0))]
    in_specs += [whole(item) for item in operands[1:7]]
    in_specs += [held(rows, channels), held(rows, TILE), held(rows, hid)]
    in_specs += [any_spec()] * kept
    base = len(operands)
    operands += [] if kept_out is None else list(kept_out)
    outs = pl.pallas_call(
        functools.partial(back_kernel, tick, micro, side, sections, kept),
        grid_spec=pltpu.PrefetchScalarGridSpec(
            num_scalar_prefetch=1,
            grid=(1,),
            in_specs=in_specs,
            out_specs=[whole(returned)] + [slotted(*shape) for shape, _ in shapes],
            scratch_shapes=[
                pltpu.VMEM((channels // TILE, height + 2 * REACH, width + 2 * EDGE, TILE), F32),
                pltpu.VMEM((rows, channels), F32),
                pltpu.VMEM((height, width, channels), F32),
            ],
        ),
        out_shape=[shaped(returned.shape, BF16)]
        + [shaped((micro + 1,) + shape, dtype) for shape, dtype in shapes],
        input_output_aliases={1 + base + i: 1 + i for i in range(kept)},
        compiler_params=params_of(),
        cost_estimate=cost(4 * rows * channels * hid, 8 << 20),
        name=f"back{tick}",
    )(sec, *operands)
    return outs[0], outs[1:]


def small_step(micro, vectors, grads):
    x = grads[0]
    height, width, channels = x.shape[1:]

    def first_ones(array):
        rank = len(array.shape)
        return pl.BlockSpec((micro,) + array.shape[1:], lambda i: (0,) * rank)

    return pl.pallas_call(
        functools.partial(small_kernel, micro),
        grid=(1,),
        in_specs=[whole(item) for item in vectors] + [first_ones(item) for item in grads],
        out_specs=[whole(item) for item in vectors],
        out_shape=[shaped(item.shape, F32) for item in vectors],
        scratch_shapes=[pltpu.VMEM((micro, height + 2 * REACH, width + 2 * EDGE, TILE), F32)],
        compiler_params=params_of(),
        cost_estimate=cost(1 << 28, 8 << 20),
        name="small",
    )(*vectors, *grads)


def tables(marked, sources, first_tiles):
    member = lax.axis_index("member")
    members = sources.shape[1]
    blocks = marked.shape[0]
    taken = blocks // 2
    capacity = (taken + members - 2) // (members - 1)
    ids = jnp.arange(blocks, dtype=jnp.int32)
    member_ids = jnp.arange(members, dtype=jnp.int32)
    target = jnp.sum(jnp.where(sources == member, member_ids[None, :], 0), axis=1)
    anchor = jnp.sum(jnp.where(member_ids[None, :] == member, sources, 0), axis=1)
    earlier = ids[:, None] > ids[None, :]
    counted = marked[None, :] == 1
    out_rank = jnp.sum(earlier & (target[:, None] == target[None, :]) & counted, axis=1)
    in_rank = jnp.sum(earlier & (anchor[:, None] == anchor[None, :]) & counted, axis=1)
    out_slot = (target * capacity + out_rank).astype(jnp.int32)
    in_slot = (anchor * capacity + in_rank).astype(jnp.int32)
    steps = jnp.arange(taken, dtype=jnp.int32)
    top = members * capacity - 1

    def listed(flags):
        place = jnp.sum(earlier & flags[None, :], axis=1)
        hits = flags[None, :] & (place[None, :] == steps[:, None])
        return hits, jnp.sum(jnp.where(hits, ids[None, :], 0), axis=1)

    def edges(flags):
        low = jnp.max(jnp.where(flags & (ids < first_tiles), ids, -1))
        low = jnp.where(low < 0, first_tiles - 1, low)
        high = jnp.min(jnp.where(flags & (ids >= first_tiles), ids, blocks))
        high = jnp.where(high >= blocks, first_tiles, high)
        return jnp.stack([low, high]).astype(jnp.int32)

    is_marked = marked == 1
    hits, marked_order = listed(is_marked)
    send_slots = jnp.clip(jnp.sum(jnp.where(hits, out_slot[None, :], 0), axis=1), 0, top)
    take_slots = jnp.clip(jnp.sum(jnp.where(hits, in_slot[None, :], 0), axis=1), 0, top)
    _, plain_order = listed(~is_marked)
    return dict(
        slots=members * capacity,
        in_slot=jnp.clip(in_slot, 0, top),
        marked_order=marked_order.astype(jnp.int32),
        plain_order=plain_order.astype(jnp.int32),
        send_slots=send_slots.astype(jnp.int32),
        take_slots=take_slots.astype(jnp.int32),
        marked_edges=edges(is_marked),
        plain_edges=edges(~is_marked),
    )


def weight_specs(micro, rows, channels, hid, first_tiles, groups):
    def low(block):
        return jnp.minimum(block, first_tiles - 1)

    def high(block):
        return jnp.maximum(block - first_tiles, 0)

    return [
        pl.BlockSpec((micro, rows, channels), lambda i, o, e: (0, 0, 0)),
        pl.BlockSpec((micro, rows, TILE), lambda i, o, e: (0, 0, low(o[i]))),
        pl.BlockSpec((micro, rows, hid), lambda i, o, e: (0, 0, 0)),
        pl.BlockSpec((micro, rows, TILE), lambda i, o, e: (0, 0, high(o[i]) // groups)),
        pl.BlockSpec((channels, TILE), lambda i, o, e: (0, low(o[i]))),
        pl.BlockSpec((channels, TILE), lambda i, o, e: (high(o[i]) % groups, high(o[i]) // groups)),
    ]


def local(
    inputs,
    cotangent,
    probe,
    dw_kernel,
    dw_bias,
    norm_gain,
    norm_bias,
    w_in,
    b_in,
    w_out,
    b_out,
    layer_scale,
    shuffle_mask,
    source_member,
):
    sections = lax.axis_size("section")
    sec = lax.axis_index("section").astype(jnp.int32).reshape(1)
    micro = inputs.shape[1]
    height, side, channels = inputs.shape[3:]
    width = (side + 15) // 16 * 16
    rows = height * width
    hid = w_in.shape[3]
    first_tiles = hid // TILE
    groups = hid // channels
    vectors = [
        dw_kernel.reshape(TAPS * TAPS, channels),
        dw_bias[0],
        norm_gain[0],
        norm_bias[0],
        b_in[0],
        b_out[0],
        layer_scale[0],
    ]
    first = w_in[0, 0]
    second = w_out[0, 0]
    lowered = [first.astype(BF16), second.astype(BF16)]

    def padded(maps):
        return jnp.pad(maps, ((0, 0), (0, 0), (0, width - side), (0, 0)))

    images = padded(inputs[0, :, 0])
    slopes = padded(cotangent[0, :, 0])
    trial = padded(probe[0])[0]
    ticks = micro + sections - 1
    received = images[0]
    saved = None
    for tick in range(ticks):
        current, saved = train_step(
            tick, micro, side, sec, images, received, vectors, lowered, saved
        )
        if tick < ticks - 1:
            pairs = [(s, s + 1) for s in range(sections - 1) if 0 <= tick - s < micro]
            received = lax.ppermute(current, "section", pairs)
    xs, hats, inverses, ns, hs, gelu_slopes, mixes = saved
    kernel, gain, scale = vectors[0], vectors[2], vectors[6]
    returned = slopes[0]
    grads = None
    for tick in range(ticks):
        current, grads = back_step(
            tick,
            micro,
            side,
            sections,
            sec,
            slopes,
            returned,
            (kernel, gain, scale, *lowered),
            (hats, inverses, gelu_slopes),
            grads,
        )
        if tick < ticks - 1:
            pairs = [
                (s, s - 1) for s in range(1, sections) if 0 <= tick - (sections - 1 - s) < micro
            ]
            returned = lax.ppermute(current, "section", pairs)
    dys, dmixes, dpres, dns, dspreads = grads

    table = tables(shuffle_mask[0], source_member[0], first_tiles)
    taken = table["marked_order"].shape[0]
    blocks = shuffle_mask.shape[1]
    weight_ins = (ns, dpres, hs, dmixes, first, second)
    specs = weight_specs(micro, rows, channels, hid, first_tiles, groups)
    tile = (1, channels, TILE)
    outgoing = pl.pallas_call(
        functools.partial(send_kernel, first_tiles, groups),
        grid_spec=pltpu.PrefetchScalarGridSpec(
            num_scalar_prefetch=2,
            grid=(taken,),
            in_specs=specs,
            out_specs=pl.BlockSpec(tile, lambda i, o, e: (e[i], 0, 0)),
        ),
        out_shape=shaped((table["slots"], channels, TILE), BF16),
        compiler_params=params_of(),
        cost_estimate=cost(1 << 30, 8 << 20),
        name="send",
    )(table["marked_order"], table["send_slots"], *weight_ins)
    arrived = lax.all_to_all(outgoing, "member", split_axis=0, concat_axis=0, tiled=True)

    def low_at(i, o, e):
        return (0, jnp.minimum(o[i], e[0]))

    def high_at(i, o, e):
        at = jnp.maximum(o[i], e[1]) - first_tiles
        return (at % groups, at // groups)

    own, new_first, new_second = pl.pallas_call(
        functools.partial(keep_kernel, first_tiles, groups),
        grid_spec=pltpu.PrefetchScalarGridSpec(
            num_scalar_prefetch=2,
            grid=(blocks - taken,),
            in_specs=specs,
            out_specs=[
                pl.BlockSpec(tile, lambda i, o, e: (o[i], 0, 0)),
                pl.BlockSpec((channels, TILE), low_at),
                pl.BlockSpec((channels, TILE), high_at),
            ],
        ),
        out_shape=[
            shaped((blocks, channels, TILE), BF16),
            shaped(first.shape, F32),
            shaped(second.shape, F32),
        ],
        compiler_params=params_of(),
        cost_estimate=cost(1 << 30, 8 << 20),
        name="keep",
    )(table["plain_order"], table["plain_edges"], *weight_ins)
    vectors = small_step(micro, vectors, (xs, hats, mixes, dys, dpres, dns, dspreads))

    new_first, new_second = pl.pallas_call(
        functools.partial(place_kernel, first_tiles),
        grid_spec=pltpu.PrefetchScalarGridSpec(
            num_scalar_prefetch=3,
            grid=(taken,),
            in_specs=[
                pl.BlockSpec(tile, lambda i, o, e, s: (s[i], 0, 0)),
                pl.BlockSpec((channels, TILE), lambda i, o, e, s: low_at(0, o, e)),
                pl.BlockSpec((channels, TILE), lambda i, o, e, s: high_at(0, o, e)),
            ],
            out_specs=[
                pl.BlockSpec((channels, TILE), lambda i, o, e, s: low_at(i, o, e)),
                pl.BlockSpec((channels, TILE), lambda i, o, e, s: high_at(i, o, e)),
            ],
        ),
        out_shape=[shaped(first.shape, F32), shaped(second.shape, F32)],
        input_output_aliases={4: 0, 5: 1},
        compiler_params=params_of(),
        cost_estimate=cost(0, 8 << 20),
        name="place",
    )(
        table["marked_order"],
        table["marked_edges"],
        table["take_slots"],
        arrived,
        new_first,
        new_second,
    )

    received = trial
    kept_out = None
    for tick in range(sections):
        operands = [trial, received, *vectors, own, arrived]
        result = pl.pallas_call(
            functools.partial(probe_kernel, tick, side),
            grid_spec=pltpu.PrefetchScalarGridSpec(
                num_scalar_prefetch=3,
                grid=(1,),
                in_specs=[whole(item) for item in operands],
                out_specs=whole(trial),
                scratch_shapes=[
                    pltpu.VMEM(
                        (channels // TILE, height + 2 * REACH, width + 2 * EDGE, TILE), F32
                    ),
                    pltpu.VMEM((rows, channels), F32),
                    pltpu.VMEM((rows, channels), F32),
                    pltpu.VMEM((rows, channels), BF16),
                ],
            ),
            out_shape=shaped(trial.shape, BF16),
            compiler_params=params_of(),
            cost_estimate=cost(4 * rows * channels * hid, 8 << 20),
            name=f"probe{tick}",
        )(sec, shuffle_mask[0], table["in_slot"], *operands)
        kept_out = result if tick == 0 else jnp.where(sec[0] == tick, result, kept_out)
        if tick < sections - 1:
            received = lax.ppermute(result, "section", [(tick, tick + 1)])
    features = kept_out[:, :side, :]
    return (new_first[None, None], new_second[None, None], features[None, None, None])


def solution(mesh):
    return jax.shard_map(
        local,
        mesh=mesh,
        in_specs=(
            P("member", None, None, None, None, None),
            P("member", None, None, None, None, None),
            P("member", None, None, None, None),
            P("member", "section", None, None, None),
            P("member", "section", None),
            P("member", "section", None),
            P("member", "section", None),
            P("member", "section", None, None),
            P("member", "section", None),
            P("member", "section", None, None),
            P("member", "section", None),
            P("member", "section", None),
            P("section", None),
            P("section", None, None),
        ),
        out_specs=(
            P("member", "section", None, None),
            P("member", "section", None, None),
            P("member", "section", None, None, None, None),
        ),
        check_vma=False,
    )
```

```python
import functools
import math

import jax
import jax.numpy as jnp
from jax import lax
from jax.experimental import pallas as pl
from jax.experimental.pallas import tpu as pltpu
from jax.sharding import PartitionSpec as P

TILE = 128
learning_rate = 0.001
norm_epsilon = 1e-06
F32 = jnp.float32
BF16 = jnp.bfloat16
EDGE = 8
REACH = 3
TAPS = 2 * REACH + 1
VMEM_LIMIT = 44 * 1024 * 1024

ERF_TOP = (
    0.00022905065861350646,
    0.0034082910107109506,
    0.050955695062380861,
    0.18520832239976145,
    1.128379143519084,
)
ERF_LOW = (
    -1.1791602954361697e-7,
    0.000023547966471313185,
    0.0010179625278914885,
    0.014070470171167667,
    0.11098505178285362,
    0.49746925110067538,
    1.0,
)


def erf(value):
    value = jnp.clip(value, -3.832506856900711, 3.832506856900711)
    square = value * value
    top = jnp.full_like(square, ERF_TOP[0])
    for term in ERF_TOP[1:]:
        top = top * square + term
    low = jnp.full_like(square, ERF_LOW[0])
    for term in ERF_LOW[1:]:
        low = low * square + term
    return value * top / low


def whole(array):
    rank = len(array.shape)
    return pl.BlockSpec(array.shape, lambda *args: (0,) * rank)


def lanes(index):
    return pl.ds(pl.multiple_of(index * TILE, TILE), TILE)


def shaped(shape, dtype):
    return jax.ShapeDtypeStruct(shape, dtype)


def convolve(padded, chunk, kernel_ref, height, width, flip, store):
    totals = [None] * height
    for col in range(TAPS):
        taps = []
        for row in range(TAPS):
            at = row * TAPS + col
            if flip:
                at = TAPS * TAPS - 1 - at
            taps.append(kernel_ref[at, 0:1, lanes(chunk)])
        for line in range(height + TAPS - 1):
            values = padded[chunk, line, pl.ds(EDGE - REACH + col, width), :]
            for row in range(TAPS):
                out = line - row
                if 0 <= out < height:
                    term = values * taps[row]
                    totals[out] = term if totals[out] is None else totals[out] + term
    for out in range(height):
        store(out, totals[out])


def fill_padded(padded, maps):
    height, width, channels = maps.shape
    padded[...] = jnp.zeros(padded.shape, F32)
    for chunk in range(channels // TILE):
        padded[chunk, REACH : REACH + height, EDGE : EDGE + width, :] = maps[
            :, :, chunk * TILE : (chunk + 1) * TILE
        ]


def real_columns(shape, side):
    return lax.broadcasted_iota(jnp.int32, shape, 1) < side


def normalise(spread):
    center = jnp.mean(spread, axis=-1, keepdims=True)
    offset = spread - center
    variance = jnp.mean(offset * offset, axis=-1, keepdims=True)
    inverse = lax.rsqrt(variance + norm_epsilon)
    return offset * inverse, inverse


def forward_core(
    side, vectors, widened, padded, spread, total, weights, n_ref, hat_store, hidden_store
):
    kernel_ref, bias_ref, gain_ref, shift_ref, first_bias_ref, second_bias_ref, scale_ref = vectors
    height, width, channels = widened.shape
    hid = first_bias_ref.shape[1]
    fill_padded(padded, widened)

    def conv_body(chunk, carry):
        bias = bias_ref[0:1, lanes(chunk)]

        def store(out, value):
            spread[out * width : (out + 1) * width, lanes(chunk)] = value + bias

        convolve(padded, chunk, kernel_ref, height, width, False, store)
        return carry

    lax.fori_loop(0, channels // TILE, conv_body, 0)
    hat, inverse = normalise(spread[...])
    n_ref[...] = (hat * gain_ref[...] + shift_ref[...]).astype(BF16)
    hat_store(hat, inverse)
    total[...] = jnp.zeros(total.shape, F32)

    def mix_body(piece, carry):
        first, second = weights(piece)
        at = pl.ds(pl.multiple_of(piece * channels, channels), channels)
        pre = jnp.dot(n_ref[...], first, preferred_element_type=F32) + first_bias_ref[:, at]
        below = 0.5 + 0.5 * erf(pre * math.sqrt(0.5))
        hidden = (pre * below).astype(BF16)
        hidden_store(piece, hidden, pre, below)
        total[...] += jnp.dot(hidden, second, preferred_element_type=F32)
        return carry

    lax.fori_loop(0, hid // channels, mix_body, 0)
    mixed = total[...] + second_bias_ref[...]
    result = widened + (scale_ref[...] * mixed).reshape(height, width, channels)
    result = jnp.where(real_columns(result.shape, side), result, 0.0)
    return result, mixed


def is_active(sec_ref, tick, count):
    which = tick - sec_ref[0]
    return (which >= 0) & (which < count)


def columns(piece, channels):
    return pl.ds(pl.multiple_of(piece * channels, channels), channels)


def train_kernel(tick, micro, side, kept, sec_ref, image_ref, received_ref, *refs):
    vectors, (first_ref, second_ref) = refs[:7], refs[7:9]
    refs = refs[9 + kept :]
    y_ref, outs, bufs = refs[0], refs[1:8], refs[8:15]
    padded, spread, total, sems, piece_sems = refs[15:]
    x_buf, hat_buf, inverse_buf, n_buf, mixed_buf, h_buf, slope_buf = bufs
    h_out, slope_out = outs[5:]

    @pl.when(is_active(sec_ref, tick, micro))
    def _():
        slot = tick - sec_ref[0]
        channels = x_buf.shape[-1]
        pieces = h_buf.shape[-1] // channels
        entry = jnp.where(sec_ref[0] == 0, image_ref[0].astype(F32), received_ref[...].astype(F32))
        x_buf[...] = entry.astype(BF16)

        def weights(piece):
            at = columns(piece, channels)
            return first_ref[:, at], second_ref[at, :]

        def piece_copies(piece):
            at = columns(piece, channels)
            return [
                pltpu.make_async_copy(h_buf.at[:, at], h_out.at[slot, :, at], piece_sems.at[0, piece]),
                pltpu.make_async_copy(
                    slope_buf.at[:, at], slope_out.at[slot, :, at], piece_sems.at[1, piece]
                ),
            ]

        def hidden_store(piece, hidden, pre, below):
            at = columns(piece, channels)
            h_buf[:, at] = hidden
            density = jnp.exp(-0.5 * pre * pre) * (1.0 / math.sqrt(2.0 * math.pi))
            slope_buf[:, at] = (below + pre * density).astype(BF16)
            for copy in piece_copies(piece):
                copy.start()

        copies = [
            pltpu.make_async_copy(buf, out.at[slot], sems.at[index])
            for index, (buf, out) in enumerate(zip(bufs[:5], outs[:5]))
        ]

        def hat_store(hat, inverse):
            hat_buf[...] = hat
            inverse_buf[...] = jnp.broadcast_to(inverse, inverse_buf.shape)
            for copy in copies[:4]:
                copy.start()

        result, mixed = forward_core(
            side, vectors, entry, padded, spread, total, weights, n_buf, hat_store, hidden_store
        )
        y_ref[...] = result.astype(BF16)
        mixed_buf[...] = mixed
        copies[4].start()
        for copy in copies:
            copy.wait()
        for piece in range(pieces):
            for copy in piece_copies(piece):
                copy.wait()


def probe_kernel(tick, side, kept, sec_ref, marked_ref, slot_ref, image_ref, received_ref, *refs):
    vectors, (own_ref, arrived_ref) = refs[:7], refs[7:9]
    refs = refs[9 + kept :]
    y_ref, feature_ref, feature_buf, tiles_buf, padded, spread, total, n_ref, sems, end_sem = refs

    @pl.when(sec_ref[0] == tick)
    def _():
        channels = y_ref.shape[-1]
        tiles = channels // TILE
        blocks = tiles_buf.shape[0]
        groups = vectors[4].shape[1] // channels
        for block in range(blocks):
            taken = marked_ref[block] == 1

            @pl.when(taken)
            def _():
                pltpu.make_async_copy(
                    arrived_ref.at[slot_ref[block]], tiles_buf.at[block], sems.at[block]
                ).start()

            @pl.when(jnp.logical_not(taken))
            def _():
                pltpu.make_async_copy(
                    own_ref.at[block], tiles_buf.at[block], sems.at[block]
                ).start()

        entry = image_ref[...] if tick == 0 else received_ref[...]

        def tile(block):
            pltpu.make_async_copy(own_ref.at[block], tiles_buf.at[block], sems.at[block]).wait()
            return tiles_buf[block]

        def weights(piece):
            first = [tile(piece * tiles + item) for item in range(tiles)]
            second = [tile(groups * tiles + item * groups + piece) for item in range(tiles)]
            return jnp.concatenate(first, axis=1), jnp.concatenate(second, axis=1)

        result, mixed = forward_core(
            side,
            vectors,
            entry.astype(F32),
            padded,
            spread,
            total,
            weights,
            n_ref,
            lambda hat, inverse: None,
            lambda piece, hidden, pre, below: None,
        )
        output = result.astype(BF16)
        y_ref[...] = output
        feature_buf[...] = output[:, :side, :]
        done = pltpu.make_async_copy(feature_buf, feature_ref, end_sem)
        done.start()
        done.wait()


def back_kernel(tick, micro, side, sections, kept, turns, sec_ref, slope_in_ref, returned_ref, *refs):
    kernel_ref, gain_ref, scale_ref, first_ref, second_ref = refs[:5]
    hat_ref, inverse_ref, slope_ref, n_ref, h_ref = refs[5:10]
    refs = refs[10 + kept :]
    dx_ref, outs, turned_ref = refs[0], refs[1:5], refs[5]
    dy_buf, dn_buf, dspread_buf, both_buf, turned_buf = refs[6:11]
    hat_buf, inverse_buf, slope_buf, n_buf, h_buf = refs[11:16]
    padded, total, conv_out, sems, piece_sems, in_sems = refs[16:]
    both_out = outs[3]
    which = tick - (sections - 1 - sec_ref[0])
    channels = dx_ref.shape[-1]
    hid = h_buf.shape[-1]
    pieces = hid // channels

    @pl.when((which >= 0) & (which < micro))
    def _():
        height, width, _ = dx_ref.shape
        rows = height * width
        ins = [
            pltpu.make_async_copy(
                slope_ref.at[which, :, columns(piece, channels)],
                slope_buf.at[:, columns(piece, channels)],
                in_sems.at[piece],
            )
            for piece in range(pieces)
        ]
        ins.append(pltpu.make_async_copy(hat_ref.at[which], hat_buf, in_sems.at[pieces]))
        ins.append(pltpu.make_async_copy(inverse_ref.at[which], inverse_buf, in_sems.at[pieces + 1]))
        for copy in ins:
            copy.start()
        dy = jnp.where(
            sec_ref[0] == sections - 1, slope_in_ref[0].astype(F32), returned_ref[...].astype(F32)
        )
        flat = dy.reshape(rows, channels)
        dy_buf[...] = flat.astype(BF16)
        mix_at = columns(pieces, channels)
        both_buf[:, mix_at] = (flat * scale_ref[...]).astype(BF16)
        total[...] = jnp.zeros(total.shape, F32)
        contract = (((1,), (1,)), ((), ()))
        copies = [
            pltpu.make_async_copy(buf, out.at[which], sems.at[index])
            for index, (buf, out) in enumerate(zip((dy_buf, dn_buf, dspread_buf), outs))
        ]
        copies[0].start()

        def both_copy(piece):
            at = columns(piece, channels)
            return pltpu.make_async_copy(
                both_buf.at[:, at], both_out.at[which, :, at], piece_sems.at[piece]
            )

        both_copy(pieces).start()

        def body(piece, carry):
            at = columns(piece, channels)
            dh = lax.dot_general(
                both_buf[:, mix_at], second_ref[at, :], contract, preferred_element_type=F32
            )
            pltpu.make_async_copy(
                slope_ref.at[which, :, at], slope_buf.at[:, at], in_sems.at[piece]
            ).wait()
            dpre = (dh * slope_buf[:, at].astype(F32)).astype(BF16)
            both_buf[:, at] = dpre
            both_copy(piece).start()
            total[...] += lax.dot_general(
                dpre, first_ref[:, at], contract, preferred_element_type=F32
            )
            return carry

        lax.fori_loop(0, pieces, body, 0)
        ins[pieces].wait()
        ins[pieces + 1].wait()
        dn = total[...]
        dn_buf[...] = dn.astype(BF16)
        copies[1].start()
        hat = hat_buf[...]
        dhat = dn * gain_ref[...]
        mean = jnp.mean(dhat, axis=-1, keepdims=True)
        along = jnp.mean(dhat * hat, axis=-1, keepdims=True)
        dspread = inverse_buf[:, 0:1] * (dhat - mean - hat * along)
        dspread_buf[...] = dspread
        copies[2].start()
        if tick < micro + sections - 2:
            fill_padded(padded, dspread.reshape(height, width, channels))

            def conv_body(chunk, carry):
                def store(out, value):
                    conv_out[out, :, lanes(chunk)] = value

                convolve(padded, chunk, kernel_ref, height, width, True, store)
                return carry

            lax.fori_loop(0, channels // TILE, conv_body, 0)
            dx = dy + conv_out[...]
            dx = jnp.where(real_columns(dx.shape, side), dx, 0.0)
            dx_ref[...] = dx.astype(BF16)
        for copy in copies:
            copy.wait()
        for piece in range(pieces + 1):
            both_copy(piece).wait()

    if turns:
        wanted = which == -1
        if tick == micro:
            wanted = wanted | (sec_ref[0] == sections - 1)

        @pl.when(wanted)
        def _():
            get_n = pltpu.make_async_copy(n_ref, n_buf, sems.at[0])
            get_h = pltpu.make_async_copy(h_ref, h_buf, sems.at[1])
            get_n.start()
            get_h.start()
            get_h.wait()
            get_n.wait()
            depth = turned_buf.shape[1]

            def turn(piece, carry):
                at = columns(piece, channels)
                turned_buf[at, :] = h_buf[:, :, at].reshape(depth, channels).T
                return carry

            lax.fori_loop(0, pieces, turn, 0)
            turned_buf[columns(pieces, channels), :] = n_buf[...].reshape(depth, channels).T
            put = pltpu.make_async_copy(turned_buf, turned_ref, sems.at[2])
            put.start()
            put.wait()


def small_kernel(micro, *refs):
    (kernel_ref, bias_ref, gain_ref, shift_ref, first_bias_ref, second_bias_ref, scale_ref) = refs[:7]
    x_ref, hat_ref, mixed_ref, dy_ref, dn_ref, dspread_ref, both_ref = refs[7:14]
    outs = refs[14:21]
    padded = refs[21]
    height, width, channels = x_ref.shape[1:]

    def total(values):
        return jnp.sum(values, axis=0, keepdims=True)

    def chunk_body(chunk, carry):
        at = lanes(chunk)
        scale = scale_ref[0:1, at]
        sums = [0.0] * 5
        for item in range(micro):
            dy = dy_ref[item, :, at].astype(F32)
            dn = dn_ref[item, :, at].astype(F32)
            sums[0] += total(dspread_ref[item, :, at])
            sums[1] += total(dn * hat_ref[item, :, at])
            sums[2] += total(dn)
            sums[3] += total(dy)
            sums[4] += total(dy * mixed_ref[item, :, at])
        outs[1][0:1, at] = bias_ref[0:1, at] - learning_rate * sums[0]
        outs[2][0:1, at] = gain_ref[0:1, at] - learning_rate * sums[1]
        outs[3][0:1, at] = shift_ref[0:1, at] - learning_rate * sums[2]
        outs[5][0:1, at] = second_bias_ref[0:1, at] - learning_rate * (scale * sums[3])
        outs[6][0:1, at] = scale - learning_rate * sums[4]
        padded[...] = jnp.zeros(padded.shape, F32)
        for item in range(micro):
            padded[item, REACH : REACH + height, EDGE : EDGE + width, :] = x_ref[
                item, :, :, at
            ].astype(F32)
        for col in range(TAPS):
            for row in range(TAPS):
                acc = None
                for item in range(micro):
                    for out in range(height):
                        term = (
                            padded[item, out + row, pl.ds(EDGE - REACH + col, width), :]
                            * dspread_ref[item, out * width : (out + 1) * width, at]
                        )
                        acc = term if acc is None else acc + term
                tap = row * TAPS + col
                outs[0][tap, 0:1, at] = kernel_ref[tap, 0:1, at] - learning_rate * total(acc)
        return carry

    lax.fori_loop(0, channels // TILE, chunk_body, 0)
    hid = first_bias_ref.shape[1]

    def bias_body(piece, carry):
        at = lanes(piece)
        acc = 0.0
        for item in range(micro):
            acc += total(both_ref[item, :, at].astype(F32))
        outs[4][0:1, at] = first_bias_ref[0:1, at] - learning_rate * acc
        return carry

    lax.fori_loop(0, hid // TILE, bias_body, 0)


def block_views(block, first_tiles, groups, channels, first_ref, second_ref, act):
    @pl.when(block < first_tiles)
    def _():
        act(first_ref.at[:, lanes(block)])

    @pl.when(block >= first_tiles)
    def _():
        place = block - first_tiles
        group = lax.rem(place, groups)
        act(second_ref.at[columns(group, channels), lanes(lax.div(place, groups))])


def update_kernel(
    first_tiles, groups, sending, order_ref, slot_ref, turned_ref, both_ref, first_ref, second_ref, *refs
):
    if sending:
        (send_ref, wide_buf, slim_buf, in_sems, out_sems) = refs
    else:
        (own_ref, new_first, new_second, wide_buf, slim_buf, in_sems, out_sems, wide_sems) = refs
    count = wide_buf.shape[0]
    channels = wide_buf.shape[1]
    micro, rows, _ = both_ref.shape

    def fetch(step, carry):
        def act(view):
            pltpu.make_async_copy(view, wide_buf.at[step], in_sems.at[step]).start()

        block_views(order_ref[step], first_tiles, groups, channels, first_ref, second_ref, act)
        return carry

    lax.fori_loop(0, count, fetch, 0)

    def slim_copy(step):
        target = send_ref.at[slot_ref[step]] if sending else own_ref.at[order_ref[step]]
        return pltpu.make_async_copy(slim_buf.at[step], target, out_sems.at[step])

    def body(step, carry):
        block = order_ref[step]
        is_first = block < first_tiles
        place = jnp.maximum(block - first_tiles, 0)
        group = jnp.where(is_first, groups, lax.rem(place, groups))
        column = jnp.where(is_first, block, first_tiles + lax.div(place, groups))
        grad = jnp.dot(
            turned_ref[columns(group, channels), :],
            both_ref[:, :, lanes(column)].reshape(micro * rows, TILE),
            preferred_element_type=F32,
        )
        pltpu.make_async_copy(
            first_ref.at[:, lanes(0)], wide_buf.at[step], in_sems.at[step]
        ).wait()
        updated = wide_buf[step] - learning_rate * grad
        slim_buf[step] = updated.astype(BF16)
        slim_copy(step).start()
        if not sending:
            wide_buf[step] = updated

            def act(view):
                pltpu.make_async_copy(wide_buf.at[step], view, wide_sems.at[step]).start()

            block_views(block, first_tiles, groups, channels, new_first, new_second, act)
        return carry

    lax.fori_loop(0, count, body, 0)

    def drain(step, carry):
        slim_copy(step).wait()
        if not sending:
            pltpu.make_async_copy(
                wide_buf.at[step], new_first.at[:, lanes(0)], wide_sems.at[step]
            ).wait()
        return carry

    lax.fori_loop(0, count, drain, 0)


def place_kernel(
    first_tiles, groups, order_ref, slot_ref, arrived_ref, old_first, old_second, new_first, new_second, *refs
):
    wide_buf, slim_buf, in_sems, out_sems = refs
    count, channels, _ = wide_buf.shape

    def fetch(step, carry):
        pltpu.make_async_copy(
            arrived_ref.at[slot_ref[step]], slim_buf.at[step], in_sems.at[step]
        ).start()
        return carry

    lax.fori_loop(0, count, fetch, 0)

    def body(step, carry):
        pltpu.make_async_copy(arrived_ref.at[0], slim_buf.at[step], in_sems.at[step]).wait()
        wide_buf[step] = slim_buf[step].astype(F32)

        def act(view):
            pltpu.make_async_copy(wide_buf.at[step], view, out_sems.at[step]).start()

        block_views(order_ref[step], first_tiles, groups, channels, new_first, new_second, act)
        return carry

    lax.fori_loop(0, count, body, 0)

    def drain(step, carry):
        pltpu.make_async_copy(
            wide_buf.at[step], new_first.at[:, lanes(0)], out_sems.at[step]
        ).wait()
        return carry

    lax.fori_loop(0, count, drain, 0)


def params_of(limit=VMEM_LIMIT):
    return pltpu.CompilerParams(vmem_limit_bytes=limit)


def cost(flops, read):
    return pl.CostEstimate(flops=flops, bytes_accessed=read, transcendentals=0)


def hbm_spec():
    return pl.BlockSpec(memory_space=pltpu.HBM)


def train_step(tick, micro, side, sec, images, received, vectors, weights, saved):
    height, width, channels = received.shape
    rows = height * width
    hid = vectors[4].shape[1]
    saved_shapes = [
        ((height, width, channels), BF16),
        ((rows, channels), F32),
        ((rows, TILE), F32),
        ((rows, channels), BF16),
        ((rows, channels), F32),
        ((rows, hid), BF16),
        ((rows, hid), BF16),
    ]
    kept = 0 if saved is None else len(saved)
    at = min(tick, micro - 1)
    operands = [images, received, *vectors, *weights] + ([] if saved is None else list(saved))
    in_specs = [pl.BlockSpec((1, height, width, channels), lambda i, s: (at, 0, 0, 0))]
    in_specs += [whole(item) for item in operands[1 : len(operands) - kept]]
    in_specs += [hbm_spec()] * kept
    outs = pl.pallas_call(
        functools.partial(train_kernel, tick, micro, side, kept),
        grid_spec=pltpu.PrefetchScalarGridSpec(
            num_scalar_prefetch=1,
            grid=(1,),
            in_specs=in_specs,
            out_specs=[whole(received)] + [hbm_spec() for _ in saved_shapes],
            scratch_shapes=[pltpu.VMEM(shape, dtype) for shape, dtype in saved_shapes]
            + [
                pltpu.VMEM((channels // TILE, height + 2 * REACH, width + 2 * EDGE, TILE), F32),
                pltpu.VMEM((rows, channels), F32),
                pltpu.VMEM((rows, channels), F32),
                pltpu.SemaphoreType.DMA((5,)),
                pltpu.SemaphoreType.DMA((2, hid // channels)),
            ],
        ),
        out_shape=[shaped(received.shape, BF16)]
        + [pltpu.HBM((micro,) + shape, dtype) for shape, dtype in saved_shapes],
        input_output_aliases={1 + len(operands) - kept + i: 1 + i for i in range(kept)},
        compiler_params=params_of(),
        cost_estimate=cost(4 * rows * channels * hid, 8 << 20),
        name=f"train{tick}",
    )(sec, *operands)
    return outs[0], outs[1:]


def back_step(tick, micro, side, sections, sec, slopes, returned, params, saved, kept_out):
    height, width, channels = returned.shape
    rows = height * width
    hid = saved[2].shape[-1]
    shapes = [
        ((rows, channels), BF16),
        ((rows, channels), BF16),
        ((rows, channels), F32),
        ((rows, hid + channels), BF16),
    ]
    turned = ((hid + channels, micro * rows), BF16)
    kept = 0 if kept_out is None else len(kept_out)
    operands = [slopes, returned, *params, *saved]
    at = min(tick, micro - 1)
    in_specs = [pl.BlockSpec((1, height, width, channels), lambda i, s: (at, 0, 0, 0))]
    in_specs += [whole(item) for item in operands[1:7]]
    in_specs += [hbm_spec()] * (len(saved) + kept)
    base = len(operands)
    operands += [] if kept_out is None else list(kept_out)
    turns = tick <= max(sections - 2, micro)
    outs = pl.pallas_call(
        functools.partial(back_kernel, tick, micro, side, sections, kept, turns),
        grid_spec=pltpu.PrefetchScalarGridSpec(
            num_scalar_prefetch=1,
            grid=(1,),
            in_specs=in_specs,
            out_specs=[whole(returned)] + [hbm_spec()] * (len(shapes) + 1),
            scratch_shapes=[pltpu.VMEM(shape, dtype) for shape, dtype in shapes]
            + [
                pltpu.VMEM(*turned),
                pltpu.VMEM((rows, channels), F32),
                pltpu.VMEM((rows, TILE), F32),
                pltpu.VMEM((rows, hid), BF16),
                pltpu.VMEM((micro, rows, channels), BF16),
                pltpu.VMEM((micro, rows, hid), BF16),
                pltpu.VMEM((channels // TILE, height + 2 * REACH, width + 2 * EDGE, TILE), F32),
                pltpu.VMEM((rows, channels), F32),
                pltpu.VMEM((height, width, channels), F32),
                pltpu.SemaphoreType.DMA((3,)),
                pltpu.SemaphoreType.DMA((hid // channels + 1,)),
                pltpu.SemaphoreType.DMA((hid // channels + 2,)),
            ],
        ),
        out_shape=[shaped(returned.shape, BF16)]
        + [pltpu.HBM((micro,) + shape, dtype) for shape, dtype in shapes]
        + [pltpu.HBM(*turned)],
        input_output_aliases={1 + base + i: 1 + i for i in range(kept)},
        compiler_params=params_of(),
        cost_estimate=cost(4 * rows * channels * hid, 8 << 20),
        name=f"back{tick}",
    )(sec, *operands)
    return outs[0], outs[1:]


def small_step(micro, vectors, grads):
    x = grads[0]
    height, width, channels = x.shape[1:]
    return pl.pallas_call(
        functools.partial(small_kernel, micro),
        grid=(1,),
        in_specs=[whole(item) for item in vectors] + [whole(item) for item in grads],
        out_specs=[whole(item) for item in vectors],
        out_shape=[shaped(item.shape, F32) for item in vectors],
        scratch_shapes=[pltpu.VMEM((micro, height + 2 * REACH, width + 2 * EDGE, TILE), F32)],
        compiler_params=params_of(),
        cost_estimate=cost(1 << 28, 8 << 20),
        name="small",
    )(*vectors, *grads)


def tables(marked, sources):
    member = lax.axis_index("member")
    members = sources.shape[1]
    blocks = marked.shape[0]
    taken = blocks // 2
    capacity = (taken + members - 2) // (members - 1)
    ids = jnp.arange(blocks, dtype=jnp.int32)
    member_ids = jnp.arange(members, dtype=jnp.int32)
    target = jnp.sum(jnp.where(sources == member, member_ids[None, :], 0), axis=1)
    anchor = jnp.sum(jnp.where(member_ids[None, :] == member, sources, 0), axis=1)
    earlier = ids[:, None] > ids[None, :]
    counted = marked[None, :] == 1
    out_rank = jnp.sum(earlier & (target[:, None] == target[None, :]) & counted, axis=1)
    in_rank = jnp.sum(earlier & (anchor[:, None] == anchor[None, :]) & counted, axis=1)
    out_slot = (target * capacity + out_rank).astype(jnp.int32)
    in_slot = (anchor * capacity + in_rank).astype(jnp.int32)
    steps = jnp.arange(taken, dtype=jnp.int32)
    top = members * capacity - 1

    def listed(flags):
        place = jnp.sum(earlier & flags[None, :], axis=1)
        hits = flags[None, :] & (place[None, :] == steps[:, None])
        return hits, jnp.sum(jnp.where(hits, ids[None, :], 0), axis=1)

    is_marked = marked == 1
    hits, marked_order = listed(is_marked)
    send_slots = jnp.clip(jnp.sum(jnp.where(hits, out_slot[None, :], 0), axis=1), 0, top)
    take_slots = jnp.clip(jnp.sum(jnp.where(hits, in_slot[None, :], 0), axis=1), 0, top)
    _, plain_order = listed(~is_marked)
    return dict(
        slots=members * capacity,
        in_slot=jnp.clip(in_slot, 0, top),
        marked_order=marked_order.astype(jnp.int32),
        plain_order=plain_order.astype(jnp.int32),
        send_slots=send_slots.astype(jnp.int32),
        take_slots=take_slots.astype(jnp.int32),
    )


def update_step(sending, order, slots, turned, both, first, second, out_shape):
    count = order.shape[0]
    channels = first.shape[0]
    first_tiles = first.shape[1] // TILE
    groups = second.shape[0] // channels
    sems = [pltpu.SemaphoreType.DMA((count,))] * (2 if sending else 3)
    return pl.pallas_call(
        functools.partial(update_kernel, first_tiles, groups, sending),
        grid_spec=pltpu.PrefetchScalarGridSpec(
            num_scalar_prefetch=2,
            grid=(1,),
            in_specs=[whole(turned), whole(both), hbm_spec(), hbm_spec()],
            out_specs=[hbm_spec() for _ in out_shape],
            scratch_shapes=[
                pltpu.VMEM((count, channels, TILE), F32),
                pltpu.VMEM((count, channels, TILE), BF16),
                *sems,
            ],
        ),
        out_shape=out_shape,
        compiler_params=params_of(),
        cost_estimate=cost(1 << 30, 8 << 20),
        name="send" if sending else "keep",
    )(order, slots, turned, both, first, second)


def local(
    inputs,
    cotangent,
    probe,
    dw_kernel,
    dw_bias,
    norm_gain,
    norm_bias,
    w_in,
    b_in,
    w_out,
    b_out,
    layer_scale,
    shuffle_mask,
    source_member,
):
    sections = lax.axis_size("section")
    sec = lax.axis_index("section").astype(jnp.int32).reshape(1)
    micro = inputs.shape[1]
    height, side, channels = inputs.shape[3:]
    width = (side + 15) // 16 * 16
    rows = height * width
    hid = w_in.shape[3]
    first_tiles = hid // TILE
    groups = hid // channels
    vectors = [
        dw_kernel.reshape(TAPS * TAPS, 1, channels),
        dw_bias[0],
        norm_gain[0],
        norm_bias[0],
        b_in[0],
        b_out[0],
        layer_scale[0],
    ]
    first = w_in[0, 0]
    second = w_out[0, 0]
    lowered = [first.astype(BF16), second.astype(BF16)]

    def padded(maps):
        return jnp.pad(maps, ((0, 0), (0, 0), (0, width - side), (0, 0)))

    images = padded(inputs[0, :, 0])
    slopes = padded(cotangent[0, :, 0])
    trial = padded(probe[0])[0]
    ticks = micro + sections - 1
    received = images[0]
    saved = None
    for tick in range(ticks):
        current, saved = train_step(
            tick, micro, side, sec, images, received, vectors, lowered, saved
        )
        if tick < ticks - 1:
            pairs = [(s, s + 1) for s in range(sections - 1) if 0 <= tick - s < micro]
            received = lax.ppermute(current, "section", pairs)
    xs, hats, inverses, ns, mixes, hs, gelu_slopes = saved
    kernel, gain, scale = vectors[0], vectors[2], vectors[6]
    returned = slopes[0]
    grads = None
    for tick in range(ticks):
        current, grads = back_step(
            tick,
            micro,
            side,
            sections,
            sec,
            slopes,
            returned,
            (kernel, gain, scale, *lowered),
            (hats, inverses, gelu_slopes, ns, hs),
            grads,
        )
        if tick < ticks - 1:
            pairs = [
                (s, s - 1) for s in range(1, sections) if 0 <= tick - (sections - 1 - s) < micro
            ]
            returned = lax.ppermute(current, "section", pairs)
    dys, dns, dspreads, boths, turned = grads

    table = tables(shuffle_mask[0], source_member[0])
    taken = table["marked_order"].shape[0]
    blocks = shuffle_mask.shape[1]
    (outgoing,) = update_step(
        True,
        table["marked_order"],
        table["send_slots"],
        turned,
        boths,
        first,
        second,
        [pltpu.HBM((table["slots"], channels, TILE), BF16)],
    )
    arrived = lax.all_to_all(outgoing, "member", split_axis=0, concat_axis=0, tiled=True)
    own, new_first, new_second = update_step(
        False,
        table["plain_order"],
        table["plain_order"],
        turned,
        boths,
        first,
        second,
        [
            pltpu.HBM((blocks, channels, TILE), BF16),
            pltpu.HBM(first.shape, F32),
            pltpu.HBM(second.shape, F32),
        ],
    )
    vectors = small_step(micro, vectors, (xs, hats, mixes, dys, dns, dspreads, boths))

    new_first, new_second = pl.pallas_call(
        functools.partial(place_kernel, first_tiles, groups),
        grid_spec=pltpu.PrefetchScalarGridSpec(
            num_scalar_prefetch=2,
            grid=(1,),
            in_specs=[hbm_spec()] * 3,
            out_specs=[hbm_spec()] * 2,
            scratch_shapes=[
                pltpu.VMEM((taken, channels, TILE), F32),
                pltpu.VMEM((taken, channels, TILE), BF16),
                pltpu.SemaphoreType.DMA((taken,)),
                pltpu.SemaphoreType.DMA((taken,)),
            ],
        ),
        out_shape=[pltpu.HBM(first.shape, F32), pltpu.HBM(second.shape, F32)],
        input_output_aliases={3: 0, 4: 1},
        compiler_params=params_of(),
        cost_estimate=cost(0, 8 << 20),
        name="place",
    )(table["marked_order"], table["take_slots"], arrived, new_first, new_second)

    received = trial
    features = None
    for tick in range(sections):
        operands = [trial, received, *vectors, own, arrived]
        in_specs = [whole(item) for item in operands[:-2]] + [hbm_spec(), hbm_spec()]
        kept = 0 if features is None else 1
        if kept:
            operands.append(features)
            in_specs.append(hbm_spec())
        result, features = pl.pallas_call(
            functools.partial(probe_kernel, tick, side, kept),
            grid_spec=pltpu.PrefetchScalarGridSpec(
                num_scalar_prefetch=3,
                grid=(1,),
                in_specs=in_specs,
                out_specs=[whole(trial), hbm_spec()],
                scratch_shapes=[
                    pltpu.VMEM((height, side, channels), BF16),
                    pltpu.VMEM((blocks, channels, TILE), BF16),
                    pltpu.VMEM(
                        (channels // TILE, height + 2 * REACH, width + 2 * EDGE, TILE), F32
                    ),
                    pltpu.VMEM((rows, channels), F32),
                    pltpu.VMEM((rows, channels), F32),
                    pltpu.VMEM((rows, channels), BF16),
                    pltpu.SemaphoreType.DMA((blocks,)),
                    pltpu.SemaphoreType.DMA,
                ],
            ),
            out_shape=[shaped(trial.shape, BF16), pltpu.HBM((height, side, channels), BF16)],
            input_output_aliases={2 + len(operands): 1} if kept else {},
            compiler_params=params_of(),
            cost_estimate=cost(4 * rows * channels * hid, 8 << 20),
            name=f"probe{tick}",
        )(sec, shuffle_mask[0], table["in_slot"], *operands)
        if tick < sections - 1:
            received = lax.ppermute(result, "section", [(tick, tick + 1)])
    return (new_first[None, None], new_second[None, None], features[None, None, None])


def solution(mesh):
    return jax.shard_map(
        local,
        mesh=mesh,
        in_specs=(
            P("member", None, None, None, None, None),
            P("member", None, None, None, None, None),
            P("member", None, None, None, None),
            P("member", "section", None, None, None),
            P("member", "section", None),
            P("member", "section", None),
            P("member", "section", None),
            P("member", "section", None, None),
            P("member", "section", None),
            P("member", "section", None, None),
            P("member", "section", None),
            P("member", "section", None),
            P("section", None),
            P("section", None, None),
        ),
        out_specs=(
            P("member", "section", None, None),
            P("member", "section", None, None),
            P("member", "section", None, None, None, None),
        ),
        check_vma=False,
    )
```

```python
import functools
import math

import jax
import jax.numpy as jnp
from jax import lax
from jax.experimental import pallas as pl
from jax.experimental.pallas import tpu as pltpu
from jax.sharding import PartitionSpec as P

TILE = 128
learning_rate = 0.001
norm_epsilon = 1e-06
F32 = jnp.float32
BF16 = jnp.bfloat16
EDGE = 8
REACH = 3
TAPS = 2 * REACH + 1
VMEM_LIMIT = 30 * 1024 * 1024

ERF_TOP = (
    0.00022905065861350646,
    0.0034082910107109506,
    0.050955695062380861,
    0.18520832239976145,
    1.128379143519084,
)
ERF_LOW = (
    -1.1791602954361697e-7,
    0.000023547966471313185,
    0.0010179625278914885,
    0.014070470171167667,
    0.11098505178285362,
    0.49746925110067538,
    1.0,
)


def erf(value):
    value = jnp.clip(value, -3.832506856900711, 3.832506856900711)
    square = value * value
    top = jnp.full_like(square, ERF_TOP[0])
    for term in ERF_TOP[1:]:
        top = top * square + term
    low = jnp.full_like(square, ERF_LOW[0])
    for term in ERF_LOW[1:]:
        low = low * square + term
    return value * top / low


def whole(array):
    rank = len(array.shape)
    return pl.BlockSpec(array.shape, lambda *args: (0,) * rank)


def lanes(index):
    return pl.ds(pl.multiple_of(index * TILE, TILE), TILE)


def shaped(shape, dtype):
    return jax.ShapeDtypeStruct(shape, dtype)


def convolve(padded, chunk, kernel_ref, height, width, flip, store):
    totals = [None] * height
    for col in range(TAPS):
        taps = []
        for row in range(TAPS):
            at = row * TAPS + col
            if flip:
                at = TAPS * TAPS - 1 - at
            taps.append(kernel_ref[at, 0:1, lanes(chunk)])
        for line in range(height + TAPS - 1):
            values = padded[chunk, line, pl.ds(EDGE - REACH + col, width), :]
            for row in range(TAPS):
                out = line - row
                if 0 <= out < height:
                    term = values * taps[row]
                    totals[out] = term if totals[out] is None else totals[out] + term
    for out in range(height):
        store(out, totals[out])


def fill_padded(padded, maps):
    height, width, channels = maps.shape
    padded[...] = jnp.zeros(padded.shape, F32)
    for chunk in range(channels // TILE):
        padded[chunk, REACH : REACH + height, EDGE : EDGE + width, :] = maps[
            :, :, chunk * TILE : (chunk + 1) * TILE
        ]


def real_columns(shape, side):
    return lax.broadcasted_iota(jnp.int32, shape, 1) < side


def normalise(spread):
    center = jnp.mean(spread, axis=-1, keepdims=True)
    offset = spread - center
    variance = jnp.mean(offset * offset, axis=-1, keepdims=True)
    inverse = lax.rsqrt(variance + norm_epsilon)
    return offset * inverse, inverse


def forward_core(
    side, vectors, widened, padded, spread, total, weights, n_ref, hat_store, hidden_store
):
    kernel_ref, bias_ref, gain_ref, shift_ref, first_bias_ref, second_bias_ref, scale_ref = vectors
    height, width, channels = widened.shape
    hid = first_bias_ref.shape[1]
    fill_padded(padded, widened)

    def conv_body(chunk, carry):
        bias = bias_ref[0:1, lanes(chunk)]

        def store(out, value):
            spread[out * width : (out + 1) * width, lanes(chunk)] = value + bias

        convolve(padded, chunk, kernel_ref, height, width, False, store)
        return carry

    lax.fori_loop(0, channels // TILE, conv_body, 0)
    hat, inverse = normalise(spread[...])
    n_ref[...] = (hat * gain_ref[...] + shift_ref[...]).astype(BF16)
    hat_store(hat, inverse)
    total[...] = jnp.zeros(total.shape, F32)

    def mix_body(piece, carry):
        first, second = weights(piece)
        at = pl.ds(pl.multiple_of(piece * channels, channels), channels)
        pre = jnp.dot(n_ref[...], first, preferred_element_type=F32) + first_bias_ref[:, at]
        below = 0.5 + 0.5 * erf(pre * math.sqrt(0.5))
        hidden = (pre * below).astype(BF16)
        hidden_store(piece, hidden, pre, below)
        total[...] += jnp.dot(hidden, second, preferred_element_type=F32)
        return carry

    lax.fori_loop(0, hid // channels, mix_body, 0)
    mixed = total[...] + second_bias_ref[...]
    result = widened + (scale_ref[...] * mixed).reshape(height, width, channels)
    result = jnp.where(real_columns(result.shape, side), result, 0.0)
    return result, mixed


def is_active(sec_ref, tick, count):
    which = tick - sec_ref[0]
    return (which >= 0) & (which < count)


def columns(piece, channels):
    return pl.ds(pl.multiple_of(piece * channels, channels), channels)


def train_kernel(tick, micro, side, kept, sec_ref, image_ref, received_ref, *refs):
    vectors, (first_ref, second_ref) = refs[:7], refs[7:9]
    refs = refs[9 + kept :]
    y_ref, outs, bufs = refs[0], refs[1:8], refs[8:15]
    padded, spread, total, sems, piece_sems = refs[15:]
    x_buf, hat_buf, inverse_buf, n_buf, mixed_buf, h_buf, slope_buf = bufs
    h_out, slope_out = outs[5:]

    @pl.when(is_active(sec_ref, tick, micro))
    def _():
        slot = tick - sec_ref[0]
        channels = x_buf.shape[-1]
        pieces = h_buf.shape[-1] // channels
        entry = jnp.where(sec_ref[0] == 0, image_ref[0].astype(F32), received_ref[...].astype(F32))
        x_buf[...] = entry.astype(BF16)

        def weights(piece):
            at = columns(piece, channels)
            return first_ref[:, at], second_ref[at, :]

        def piece_copies(piece):
            at = columns(piece, channels)
            return [
                pltpu.make_async_copy(h_buf.at[:, at], h_out.at[slot, :, at], piece_sems.at[0, piece]),
                pltpu.make_async_copy(
                    slope_buf.at[:, at], slope_out.at[slot, :, at], piece_sems.at[1, piece]
                ),
            ]

        def hidden_store(piece, hidden, pre, below):
            at = columns(piece, channels)
            h_buf[:, at] = hidden
            density = jnp.exp(-0.5 * pre * pre) * (1.0 / math.sqrt(2.0 * math.pi))
            slope_buf[:, at] = (below + pre * density).astype(BF16)
            for copy in piece_copies(piece):
                copy.start()

        copies = [
            pltpu.make_async_copy(buf, out.at[slot], sems.at[index])
            for index, (buf, out) in enumerate(zip(bufs[:5], outs[:5]))
        ]

        def hat_store(hat, inverse):
            hat_buf[...] = hat
            inverse_buf[...] = jnp.broadcast_to(inverse, inverse_buf.shape)
            for copy in copies[:4]:
                copy.start()

        result, mixed = forward_core(
            side, vectors, entry, padded, spread, total, weights, n_buf, hat_store, hidden_store
        )
        y_ref[...] = result.astype(BF16)
        mixed_buf[...] = mixed
        copies[4].start()
        for copy in copies:
            copy.wait()
        for piece in range(pieces):
            for copy in piece_copies(piece):
                copy.wait()


def probe_kernel(tick, side, kept, sec_ref, marked_ref, slot_ref, image_ref, received_ref, *refs):
    vectors, (own_ref, arrived_ref) = refs[:7], refs[7:9]
    refs = refs[9 + kept :]
    y_ref, feature_ref, feature_buf, tiles_buf, padded, spread, total, n_ref, sems, end_sem = refs

    @pl.when(sec_ref[0] == tick)
    def _():
        channels = y_ref.shape[-1]
        tiles = channels // TILE
        blocks = tiles_buf.shape[0]
        groups = vectors[4].shape[1] // channels
        for block in range(blocks):
            taken = marked_ref[block] == 1

            @pl.when(taken)
            def _():
                pltpu.make_async_copy(
                    arrived_ref.at[slot_ref[block]], tiles_buf.at[block], sems.at[block]
                ).start()

            @pl.when(jnp.logical_not(taken))
            def _():
                pltpu.make_async_copy(
                    own_ref.at[block], tiles_buf.at[block], sems.at[block]
                ).start()

        entry = image_ref[...] if tick == 0 else received_ref[...]

        def tile(block):
            pltpu.make_async_copy(own_ref.at[block], tiles_buf.at[block], sems.at[block]).wait()
            return tiles_buf[block]

        def weights(piece):
            first = [tile(piece * tiles + item) for item in range(tiles)]
            second = [tile(groups * tiles + item * groups + piece) for item in range(tiles)]
            return jnp.concatenate(first, axis=1), jnp.concatenate(second, axis=1)

        result, mixed = forward_core(
            side,
            vectors,
            entry.astype(F32),
            padded,
            spread,
            total,
            weights,
            n_ref,
            lambda hat, inverse: None,
            lambda piece, hidden, pre, below: None,
        )
        output = result.astype(BF16)
        y_ref[...] = output
        feature_buf[...] = output[:, :side, :]
        done = pltpu.make_async_copy(feature_buf, feature_ref, end_sem)
        done.start()
        done.wait()


def back_kernel(tick, micro, side, sections, kept, turns, sec_ref, slope_in_ref, returned_ref, *refs):
    kernel_ref, gain_ref, scale_ref, first_ref, second_ref = refs[:5]
    hat_ref, inverse_ref, slope_ref, n_ref, h_ref = refs[5:10]
    refs = refs[10 + kept :]
    dx_ref, outs, turned_ref = refs[0], refs[1:5], refs[5]
    dy_buf, dn_buf, dspread_buf, both_buf, turned_buf = refs[6:11]
    hat_buf, inverse_buf, slope_buf, n_buf, h_buf = refs[11:16]
    padded, total, conv_out, sems, piece_sems, in_sems = refs[16:]
    both_out = outs[3]
    which = tick - (sections - 1 - sec_ref[0])
    channels = dx_ref.shape[-1]
    hid = h_buf.shape[-1]
    pieces = hid // channels

    @pl.when((which >= 0) & (which < micro))
    def _():
        height, width, _ = dx_ref.shape
        rows = height * width
        ins = [
            pltpu.make_async_copy(
                slope_ref.at[which, :, columns(piece, channels)],
                slope_buf.at[:, columns(piece, channels)],
                in_sems.at[piece],
            )
            for piece in range(pieces)
        ]
        ins.append(pltpu.make_async_copy(hat_ref.at[which], hat_buf, in_sems.at[pieces]))
        ins.append(pltpu.make_async_copy(inverse_ref.at[which], inverse_buf, in_sems.at[pieces + 1]))
        for copy in ins:
            copy.start()
        dy = jnp.where(
            sec_ref[0] == sections - 1, slope_in_ref[0].astype(F32), returned_ref[...].astype(F32)
        )
        flat = dy.reshape(rows, channels)
        dy_buf[...] = flat.astype(BF16)
        mix_at = columns(pieces, channels)
        both_buf[:, mix_at] = (flat * scale_ref[...]).astype(BF16)
        total[...] = jnp.zeros(total.shape, F32)
        contract = (((1,), (1,)), ((), ()))
        copies = [
            pltpu.make_async_copy(buf, out.at[which], sems.at[index])
            for index, (buf, out) in enumerate(zip((dy_buf, dn_buf, dspread_buf), outs))
        ]
        copies[0].start()

        def both_copy(piece):
            at = columns(piece, channels)
            return pltpu.make_async_copy(
                both_buf.at[:, at], both_out.at[which, :, at], piece_sems.at[piece]
            )

        both_copy(pieces).start()

        def body(piece, carry):
            at = columns(piece, channels)
            dh = lax.dot_general(
                both_buf[:, mix_at], second_ref[at, :], contract, preferred_element_type=F32
            )
            pltpu.make_async_copy(
                slope_ref.at[which, :, at], slope_buf.at[:, at], in_sems.at[piece]
            ).wait()
            dpre = (dh * slope_buf[:, at].astype(F32)).astype(BF16)
            both_buf[:, at] = dpre
            both_copy(piece).start()
            total[...] += lax.dot_general(
                dpre, first_ref[:, at], contract, preferred_element_type=F32
            )
            return carry

        lax.fori_loop(0, pieces, body, 0)
        ins[pieces].wait()
        ins[pieces + 1].wait()
        dn = total[...]
        dn_buf[...] = dn.astype(BF16)
        copies[1].start()
        hat = hat_buf[...]
        dhat = dn * gain_ref[...]
        mean = jnp.mean(dhat, axis=-1, keepdims=True)
        along = jnp.mean(dhat * hat, axis=-1, keepdims=True)
        dspread = inverse_buf[:, 0:1] * (dhat - mean - hat * along)
        dspread_buf[...] = dspread
        copies[2].start()
        if tick < micro + sections - 2:
            fill_padded(padded, dspread.reshape(height, width, channels))

            def conv_body(chunk, carry):
                def store(out, value):
                    conv_out[out, :, lanes(chunk)] = value

                convolve(padded, chunk, kernel_ref, height, width, True, store)
                return carry

            lax.fori_loop(0, channels // TILE, conv_body, 0)
            dx = dy + conv_out[...]
            dx = jnp.where(real_columns(dx.shape, side), dx, 0.0)
            dx_ref[...] = dx.astype(BF16)
        for copy in copies:
            copy.wait()
        for piece in range(pieces + 1):
            both_copy(piece).wait()

    if turns:
        wanted = which == -1
        if tick == micro:
            wanted = wanted | (sec_ref[0] == sections - 1)

        @pl.when(wanted)
        def _():
            get_n = pltpu.make_async_copy(n_ref, n_buf, sems.at[0])
            get_h = pltpu.make_async_copy(h_ref, h_buf, sems.at[1])
            get_n.start()
            get_h.start()
            get_h.wait()
            get_n.wait()
            depth = turned_buf.shape[1]

            def turn(piece, carry):
                at = columns(piece, channels)
                turned_buf[at, :] = h_buf[:, :, at].reshape(depth, channels).T
                return carry

            lax.fori_loop(0, pieces, turn, 0)
            turned_buf[columns(pieces, channels), :] = n_buf[...].reshape(depth, channels).T
            put = pltpu.make_async_copy(turned_buf, turned_ref, sems.at[2])
            put.start()
            put.wait()


def small_kernel(micro, *refs):
    (kernel_ref, bias_ref, gain_ref, shift_ref, first_bias_ref, second_bias_ref, scale_ref) = refs[:7]
    x_ref, hat_ref, mixed_ref, dy_ref, dn_ref, dspread_ref, both_ref = refs[7:14]
    outs = refs[14:21]
    padded = refs[21]
    height, width, channels = x_ref.shape[1:]

    def total(values):
        return jnp.sum(values, axis=0, keepdims=True)

    def chunk_body(chunk, carry):
        at = lanes(chunk)
        scale = scale_ref[0:1, at]
        sums = [0.0] * 5
        for item in range(micro):
            dy = dy_ref[item, :, at].astype(F32)
            dn = dn_ref[item, :, at].astype(F32)
            sums[0] += total(dspread_ref[item, :, at])
            sums[1] += total(dn * hat_ref[item, :, at])
            sums[2] += total(dn)
            sums[3] += total(dy)
            sums[4] += total(dy * mixed_ref[item, :, at])
        outs[1][0:1, at] = bias_ref[0:1, at] - learning_rate * sums[0]
        outs[2][0:1, at] = gain_ref[0:1, at] - learning_rate * sums[1]
        outs[3][0:1, at] = shift_ref[0:1, at] - learning_rate * sums[2]
        outs[5][0:1, at] = second_bias_ref[0:1, at] - learning_rate * (scale * sums[3])
        outs[6][0:1, at] = scale - learning_rate * sums[4]
        padded[...] = jnp.zeros(padded.shape, F32)
        for item in range(micro):
            padded[item, REACH : REACH + height, EDGE : EDGE + width, :] = x_ref[
                item, :, :, at
            ].astype(F32)
        for col in range(TAPS):
            for row in range(TAPS):
                acc = None
                for item in range(micro):
                    for out in range(height):
                        term = (
                            padded[item, out + row, pl.ds(EDGE - REACH + col, width), :]
                            * dspread_ref[item, out * width : (out + 1) * width, at]
                        )
                        acc = term if acc is None else acc + term
                tap = row * TAPS + col
                outs[0][tap, 0:1, at] = kernel_ref[tap, 0:1, at] - learning_rate * total(acc)
        return carry

    lax.fori_loop(0, channels // TILE, chunk_body, 0)
    hid = first_bias_ref.shape[1]

    def bias_body(piece, carry):
        at = lanes(piece)
        acc = 0.0
        for item in range(micro):
            acc += total(both_ref[item, :, at].astype(F32))
        outs[4][0:1, at] = first_bias_ref[0:1, at] - learning_rate * acc
        return carry

    lax.fori_loop(0, hid // TILE, bias_body, 0)


def block_views(block, first_tiles, groups, channels, first_ref, second_ref, act):
    @pl.when(block < first_tiles)
    def _():
        act(first_ref.at[:, lanes(block)])

    @pl.when(block >= first_tiles)
    def _():
        place = block - first_tiles
        group = lax.rem(place, groups)
        act(second_ref.at[columns(group, channels), lanes(lax.div(place, groups))])


def update_kernel(
    first_tiles, groups, sending, order_ref, slot_ref, turned_ref, both_ref, first_ref, second_ref, *refs
):
    if sending:
        (send_ref, wide_buf, slim_buf, in_sems, out_sems) = refs
    else:
        (own_ref, new_first, new_second, wide_buf, slim_buf, in_sems, out_sems, wide_sems) = refs
    count = wide_buf.shape[0]
    channels = wide_buf.shape[1]
    micro, rows, _ = both_ref.shape

    def fetch(step, carry):
        def act(view):
            pltpu.make_async_copy(view, wide_buf.at[step], in_sems.at[step]).start()

        block_views(order_ref[step], first_tiles, groups, channels, first_ref, second_ref, act)
        return carry

    lax.fori_loop(0, count, fetch, 0)

    def slim_copy(step):
        target = send_ref.at[slot_ref[step]] if sending else own_ref.at[order_ref[step]]
        return pltpu.make_async_copy(slim_buf.at[step], target, out_sems.at[step])

    def body(step, carry):
        block = order_ref[step]
        is_first = block < first_tiles
        place = jnp.maximum(block - first_tiles, 0)
        group = jnp.where(is_first, groups, lax.rem(place, groups))
        column = jnp.where(is_first, block, first_tiles + lax.div(place, groups))
        grad = jnp.dot(
            turned_ref[columns(group, channels), :],
            both_ref[:, :, lanes(column)].reshape(micro * rows, TILE),
            preferred_element_type=F32,
        )
        pltpu.make_async_copy(
            first_ref.at[:, lanes(0)], wide_buf.at[step], in_sems.at[step]
        ).wait()
        updated = wide_buf[step] - learning_rate * grad
        slim_buf[step] = updated.astype(BF16)
        slim_copy(step).start()
        if not sending:
            wide_buf[step] = updated

            def act(view):
                pltpu.make_async_copy(wide_buf.at[step], view, wide_sems.at[step]).start()

            block_views(block, first_tiles, groups, channels, new_first, new_second, act)
        return carry

    lax.fori_loop(0, count, body, 0)

    def drain(step, carry):
        slim_copy(step).wait()
        if not sending:
            pltpu.make_async_copy(
                wide_buf.at[step], new_first.at[:, lanes(0)], wide_sems.at[step]
            ).wait()
        return carry

    lax.fori_loop(0, count, drain, 0)


def place_kernel(
    first_tiles, groups, order_ref, slot_ref, arrived_ref, old_first, old_second, new_first, new_second, *refs
):
    wide_buf, slim_buf, in_sems, out_sems = refs
    count, channels, _ = wide_buf.shape

    def fetch(step, carry):
        pltpu.make_async_copy(
            arrived_ref.at[slot_ref[step]], slim_buf.at[step], in_sems.at[step]
        ).start()
        return carry

    lax.fori_loop(0, count, fetch, 0)

    def body(step, carry):
        pltpu.make_async_copy(arrived_ref.at[0], slim_buf.at[step], in_sems.at[step]).wait()
        wide_buf[step] = slim_buf[step].astype(F32)

        def act(view):
            pltpu.make_async_copy(wide_buf.at[step], view, out_sems.at[step]).start()

        block_views(order_ref[step], first_tiles, groups, channels, new_first, new_second, act)
        return carry

    lax.fori_loop(0, count, body, 0)

    def drain(step, carry):
        pltpu.make_async_copy(
            wide_buf.at[step], new_first.at[:, lanes(0)], out_sems.at[step]
        ).wait()
        return carry

    lax.fori_loop(0, count, drain, 0)


def params_of(limit=VMEM_LIMIT):
    return pltpu.CompilerParams(vmem_limit_bytes=limit)


def cost(flops, read):
    return pl.CostEstimate(flops=flops, bytes_accessed=read, transcendentals=0)


def pinned(arrays):
    return [pltpu.with_memory_space_constraint(item, pltpu.HBM) for item in arrays]


def hbm_spec():
    return pl.BlockSpec(memory_space=pltpu.HBM)


def train_step(tick, micro, side, sec, images, received, vectors, weights, saved):
    height, width, channels = received.shape
    rows = height * width
    hid = vectors[4].shape[1]
    saved_shapes = [
        ((height, width, channels), BF16),
        ((rows, channels), F32),
        ((rows, TILE), F32),
        ((rows, channels), BF16),
        ((rows, channels), F32),
        ((rows, hid), BF16),
        ((rows, hid), BF16),
    ]
    kept = 0 if saved is None else len(saved)
    at = min(tick, micro - 1)
    operands = [images, received, *vectors, *weights] + ([] if saved is None else pinned(saved))
    in_specs = [pl.BlockSpec((1, height, width, channels), lambda i, s: (at, 0, 0, 0))]
    in_specs += [whole(item) for item in operands[1 : len(operands) - kept]]
    in_specs += [hbm_spec()] * kept
    outs = pl.pallas_call(
        functools.partial(train_kernel, tick, micro, side, kept),
        grid_spec=pltpu.PrefetchScalarGridSpec(
            num_scalar_prefetch=1,
            grid=(1,),
            in_specs=in_specs,
            out_specs=[whole(received)] + [hbm_spec() for _ in saved_shapes],
            scratch_shapes=[pltpu.VMEM(shape, dtype) for shape, dtype in saved_shapes]
            + [
                pltpu.VMEM((channels // TILE, height + 2 * REACH, width + 2 * EDGE, TILE), F32),
                pltpu.VMEM((rows, channels), F32),
                pltpu.VMEM((rows, channels), F32),
                pltpu.SemaphoreType.DMA((5,)),
                pltpu.SemaphoreType.DMA((2, hid // channels)),
            ],
        ),
        out_shape=[shaped(received.shape, BF16)]
        + [pltpu.HBM((micro,) + shape, dtype) for shape, dtype in saved_shapes],
        input_output_aliases={1 + len(operands) - kept + i: 1 + i for i in range(kept)},
        compiler_params=params_of(),
        cost_estimate=cost(4 * rows * channels * hid, 8 << 20),
        name=f"train{tick}",
    )(sec, *operands)
    return outs[0], outs[1:]


def back_step(tick, micro, side, sections, sec, slopes, returned, params, saved, kept_out):
    height, width, channels = returned.shape
    rows = height * width
    hid = saved[2].shape[-1]
    shapes = [
        ((rows, channels), BF16),
        ((rows, channels), BF16),
        ((rows, channels), F32),
        ((rows, hid + channels), BF16),
    ]
    turned = ((hid + channels, micro * rows), BF16)
    kept = 0 if kept_out is None else len(kept_out)
    operands = [slopes, returned, *params, *pinned(saved)]
    at = min(tick, micro - 1)
    in_specs = [pl.BlockSpec((1, height, width, channels), lambda i, s: (at, 0, 0, 0))]
    in_specs += [whole(item) for item in operands[1:7]]
    in_specs += [hbm_spec()] * (len(saved) + kept)
    base = len(operands)
    operands += [] if kept_out is None else pinned(kept_out)
    turns = tick <= max(sections - 2, micro)
    outs = pl.pallas_call(
        functools.partial(back_kernel, tick, micro, side, sections, kept, turns),
        grid_spec=pltpu.PrefetchScalarGridSpec(
            num_scalar_prefetch=1,
            grid=(1,),
            in_specs=in_specs,
            out_specs=[whole(returned)] + [hbm_spec()] * (len(shapes) + 1),
            scratch_shapes=[pltpu.VMEM(shape, dtype) for shape, dtype in shapes]
            + [
                pltpu.VMEM(*turned),
                pltpu.VMEM((rows, channels), F32),
                pltpu.VMEM((rows, TILE), F32),
                pltpu.VMEM((rows, hid), BF16),
                pltpu.VMEM((micro, rows, channels), BF16),
                pltpu.VMEM((micro, rows, hid), BF16),
                pltpu.VMEM((channels // TILE, height + 2 * REACH, width + 2 * EDGE, TILE), F32),
                pltpu.VMEM((rows, channels), F32),
                pltpu.VMEM((height, width, channels), F32),
                pltpu.SemaphoreType.DMA((3,)),
                pltpu.SemaphoreType.DMA((hid // channels + 1,)),
                pltpu.SemaphoreType.DMA((hid // channels + 2,)),
            ],
        ),
        out_shape=[shaped(returned.shape, BF16)]
        + [pltpu.HBM((micro,) + shape, dtype) for shape, dtype in shapes]
        + [pltpu.HBM(*turned)],
        input_output_aliases={1 + base + i: 1 + i for i in range(kept)},
        compiler_params=params_of(),
        cost_estimate=cost(4 * rows * channels * hid, 8 << 20),
        name=f"back{tick}",
    )(sec, *operands)
    return outs[0], outs[1:]


def small_step(micro, vectors, grads):
    x = grads[0]
    height, width, channels = x.shape[1:]
    return pl.pallas_call(
        functools.partial(small_kernel, micro),
        grid=(1,),
        in_specs=[whole(item) for item in vectors] + [whole(item) for item in grads],
        out_specs=[whole(item) for item in vectors],
        out_shape=[shaped(item.shape, F32) for item in vectors],
        scratch_shapes=[pltpu.VMEM((micro, height + 2 * REACH, width + 2 * EDGE, TILE), F32)],
        compiler_params=params_of(),
        cost_estimate=cost(1 << 28, 8 << 20),
        name="small",
    )(*vectors, *pinned(grads))


def tables(marked, sources):
    member = lax.axis_index("member")
    members = sources.shape[1]
    blocks = marked.shape[0]
    taken = blocks // 2
    capacity = (taken + members - 2) // (members - 1)
    ids = jnp.arange(blocks, dtype=jnp.int32)
    member_ids = jnp.arange(members, dtype=jnp.int32)
    target = jnp.sum(jnp.where(sources == member, member_ids[None, :], 0), axis=1)
    anchor = jnp.sum(jnp.where(member_ids[None, :] == member, sources, 0), axis=1)
    earlier = ids[:, None] > ids[None, :]
    counted = marked[None, :] == 1
    out_rank = jnp.sum(earlier & (target[:, None] == target[None, :]) & counted, axis=1)
    in_rank = jnp.sum(earlier & (anchor[:, None] == anchor[None, :]) & counted, axis=1)
    out_slot = (target * capacity + out_rank).astype(jnp.int32)
    in_slot = (anchor * capacity + in_rank).astype(jnp.int32)
    steps = jnp.arange(taken, dtype=jnp.int32)
    top = members * capacity - 1

    def listed(flags):
        place = jnp.sum(earlier & flags[None, :], axis=1)
        hits = flags[None, :] & (place[None, :] == steps[:, None])
        return hits, jnp.sum(jnp.where(hits, ids[None, :], 0), axis=1)

    is_marked = marked == 1
    hits, marked_order = listed(is_marked)
    send_slots = jnp.clip(jnp.sum(jnp.where(hits, out_slot[None, :], 0), axis=1), 0, top)
    take_slots = jnp.clip(jnp.sum(jnp.where(hits, in_slot[None, :], 0), axis=1), 0, top)
    _, plain_order = listed(~is_marked)
    return dict(
        slots=members * capacity,
        in_slot=jnp.clip(in_slot, 0, top),
        marked_order=marked_order.astype(jnp.int32),
        plain_order=plain_order.astype(jnp.int32),
        send_slots=send_slots.astype(jnp.int32),
        take_slots=take_slots.astype(jnp.int32),
    )


def update_step(sending, order, slots, turned, both, first, second, out_shape):
    count = order.shape[0]
    channels = first.shape[0]
    first_tiles = first.shape[1] // TILE
    groups = second.shape[0] // channels
    sems = [pltpu.SemaphoreType.DMA((count,))] * (2 if sending else 3)
    return pl.pallas_call(
        functools.partial(update_kernel, first_tiles, groups, sending),
        grid_spec=pltpu.PrefetchScalarGridSpec(
            num_scalar_prefetch=2,
            grid=(1,),
            in_specs=[whole(turned), whole(both), hbm_spec(), hbm_spec()],
            out_specs=[hbm_spec() for _ in out_shape],
            scratch_shapes=[
                pltpu.VMEM((count, channels, TILE), F32),
                pltpu.VMEM((count, channels, TILE), BF16),
                *sems,
            ],
        ),
        out_shape=out_shape,
        compiler_params=params_of(),
        cost_estimate=cost(1 << 30, 8 << 20),
        name="send" if sending else "keep",
    )(order, slots, *pinned((turned, both, first, second)))


def local(
    inputs,
    cotangent,
    probe,
    dw_kernel,
    dw_bias,
    norm_gain,
    norm_bias,
    w_in,
    b_in,
    w_out,
    b_out,
    layer_scale,
    shuffle_mask,
    source_member,
):
    sections = lax.axis_size("section")
    sec = lax.axis_index("section").astype(jnp.int32).reshape(1)
    micro = inputs.shape[1]
    height, side, channels = inputs.shape[3:]
    width = (side + 15) // 16 * 16
    rows = height * width
    hid = w_in.shape[3]
    first_tiles = hid // TILE
    groups = hid // channels
    vectors = [
        dw_kernel.reshape(TAPS * TAPS, 1, channels),
        dw_bias[0],
        norm_gain[0],
        norm_bias[0],
        b_in[0],
        b_out[0],
        layer_scale[0],
    ]
    first = w_in[0, 0]
    second = w_out[0, 0]
    lowered = [first.astype(BF16), second.astype(BF16)]

    def padded(maps):
        return jnp.pad(maps, ((0, 0), (0, 0), (0, width - side), (0, 0)))

    images = padded(inputs[0, :, 0])
    slopes = padded(cotangent[0, :, 0])
    trial = padded(probe[0])[0]
    ticks = micro + sections - 1
    received = images[0]
    saved = None
    for tick in range(ticks):
        current, saved = train_step(
            tick, micro, side, sec, images, received, vectors, lowered, saved
        )
        if tick < ticks - 1:
            pairs = [(s, s + 1) for s in range(sections - 1) if 0 <= tick - s < micro]
            received = lax.ppermute(current, "section", pairs)
    xs, hats, inverses, ns, mixes, hs, gelu_slopes = saved
    kernel, gain, scale = vectors[0], vectors[2], vectors[6]
    returned = slopes[0]
    grads = None
    for tick in range(ticks):
        current, grads = back_step(
            tick,
            micro,
            side,
            sections,
            sec,
            slopes,
            returned,
            (kernel, gain, scale, *lowered),
            (hats, inverses, gelu_slopes, ns, hs),
            grads,
        )
        if tick < ticks - 1:
            pairs = [
                (s, s - 1) for s in range(1, sections) if 0 <= tick - (sections - 1 - s) < micro
            ]
            returned = lax.ppermute(current, "section", pairs)
    dys, dns, dspreads, boths, turned = grads

    table = tables(shuffle_mask[0], source_member[0])
    taken = table["marked_order"].shape[0]
    blocks = shuffle_mask.shape[1]
    (outgoing,) = update_step(
        True,
        table["marked_order"],
        table["send_slots"],
        turned,
        boths,
        first,
        second,
        [pltpu.HBM((table["slots"], channels, TILE), BF16)],
    )
    arrived = lax.all_to_all(outgoing, "member", split_axis=0, concat_axis=0, tiled=True)
    own, new_first, new_second = update_step(
        False,
        table["plain_order"],
        table["plain_order"],
        turned,
        boths,
        first,
        second,
        [
            pltpu.HBM((blocks, channels, TILE), BF16),
            pltpu.HBM(first.shape, F32),
            pltpu.HBM(second.shape, F32),
        ],
    )
    vectors = small_step(micro, vectors, (xs, hats, mixes, dys, dns, dspreads, boths))

    new_first, new_second = pl.pallas_call(
        functools.partial(place_kernel, first_tiles, groups),
        grid_spec=pltpu.PrefetchScalarGridSpec(
            num_scalar_prefetch=2,
            grid=(1,),
            in_specs=[hbm_spec()] * 3,
            out_specs=[hbm_spec()] * 2,
            scratch_shapes=[
                pltpu.VMEM((taken, channels, TILE), F32),
                pltpu.VMEM((taken, channels, TILE), BF16),
                pltpu.SemaphoreType.DMA((taken,)),
                pltpu.SemaphoreType.DMA((taken,)),
            ],
        ),
        out_shape=[pltpu.HBM(first.shape, F32), pltpu.HBM(second.shape, F32)],
        input_output_aliases={3: 0, 4: 1},
        compiler_params=params_of(),
        cost_estimate=cost(0, 8 << 20),
        name="place",
    )(table["marked_order"], table["take_slots"], *pinned((arrived, new_first, new_second)))

    received = trial
    features = None
    for tick in range(sections):
        operands = [trial, received, *vectors, *pinned((own, arrived))]
        in_specs = [whole(item) for item in operands[:-2]] + [hbm_spec(), hbm_spec()]
        kept = 0 if features is None else 1
        if kept:
            operands += pinned([features])
            in_specs.append(hbm_spec())
        result, features = pl.pallas_call(
            functools.partial(probe_kernel, tick, side, kept),
            grid_spec=pltpu.PrefetchScalarGridSpec(
                num_scalar_prefetch=3,
                grid=(1,),
                in_specs=in_specs,
                out_specs=[whole(trial), hbm_spec()],
                scratch_shapes=[
                    pltpu.VMEM((height, side, channels), BF16),
                    pltpu.VMEM((blocks, channels, TILE), BF16),
                    pltpu.VMEM(
                        (channels // TILE, height + 2 * REACH, width + 2 * EDGE, TILE), F32
                    ),
                    pltpu.VMEM((rows, channels), F32),
                    pltpu.VMEM((rows, channels), F32),
                    pltpu.VMEM((rows, channels), BF16),
                    pltpu.SemaphoreType.DMA((blocks,)),
                    pltpu.SemaphoreType.DMA,
                ],
            ),
            out_shape=[shaped(trial.shape, BF16), pltpu.HBM((height, side, channels), BF16)],
            input_output_aliases={2 + len(operands): 1} if kept else {},
            compiler_params=params_of(),
            cost_estimate=cost(4 * rows * channels * hid, 8 << 20),
            name=f"probe{tick}",
        )(sec, shuffle_mask[0], table["in_slot"], *operands)
        if tick < sections - 1:
            received = lax.ppermute(result, "section", [(tick, tick + 1)])
    return (new_first[None, None], new_second[None, None], features[None, None, None])


def solution(mesh):
    return jax.shard_map(
        local,
        mesh=mesh,
        in_specs=(
            P("member", None, None, None, None, None),
            P("member", None, None, None, None, None),
            P("member", None, None, None, None),
            P("member", "section", None, None, None),
            P("member", "section", None),
            P("member", "section", None),
            P("member", "section", None),
            P("member", "section", None, None),
            P("member", "section", None),
            P("member", "section", None, None),
            P("member", "section", None),
            P("member", "section", None),
            P("section", None),
            P("section", None, None),
        ),
        out_specs=(
            P("member", "section", None, None),
            P("member", "section", None, None),
            P("member", "section", None, None, None, None),
        ),
        check_vma=False,
    )
```

```python
import functools
import math

import jax
import jax.numpy as jnp
from jax import lax
from jax.experimental import pallas as pl
from jax.experimental.pallas import tpu as pltpu
from jax.sharding import PartitionSpec as P

TILE = 128
learning_rate = 0.001
norm_epsilon = 1e-06
F32 = jnp.float32
BF16 = jnp.bfloat16
EDGE = 8
REACH = 3
TAPS = 2 * REACH + 1
VMEM_LIMIT = 36 * 1024 * 1024

TURN = 0.3275911 * math.sqrt(0.5)
TERMS = (1.061405429, -1.453152027, 1.421413741, -0.284496736, 0.254829592)


def normal_below(pre):
    bell = jnp.exp2((pre * pre) * (-0.5 * math.log2(math.e)))
    turn = 1.0 / (1.0 + TURN * jnp.abs(pre))
    poly = jnp.full_like(turn, 0.5 * TERMS[0])
    for term in TERMS[1:]:
        poly = poly * turn + 0.5 * term
    tail = poly * turn * bell
    return jnp.where(pre >= 0.0, 1.0 - tail, tail), bell


def whole(array):
    rank = len(array.shape)
    return pl.BlockSpec(array.shape, lambda *args: (0,) * rank)


def lanes(index):
    return pl.ds(pl.multiple_of(index * TILE, TILE), TILE)


def shaped(shape, dtype):
    return jax.ShapeDtypeStruct(shape, dtype)


def convolve(padded, chunk, kernel_ref, height, width, flip, store):
    totals = [None] * height
    for col in range(TAPS):
        taps = []
        for row in range(TAPS):
            at = row * TAPS + col
            if flip:
                at = TAPS * TAPS - 1 - at
            taps.append(kernel_ref[at, 0:1, lanes(chunk)])
        for line in range(REACH, REACH + height):
            values = padded[chunk, line, pl.ds(EDGE - REACH + col, width), :]
            for row in range(TAPS):
                out = line - row
                if 0 <= out < height:
                    term = values * taps[row]
                    totals[out] = term if totals[out] is None else totals[out] + term
    for out in range(height):
        store(out, totals[out])


def fill_padded(padded, maps):
    height, width, channels = maps.shape
    padded[...] = jnp.zeros(padded.shape, F32)
    for chunk in range(channels // TILE):
        padded[chunk, REACH : REACH + height, EDGE : EDGE + width, :] = maps[
            :, :, chunk * TILE : (chunk + 1) * TILE
        ]


def real_columns(shape, side):
    return lax.broadcasted_iota(jnp.int32, shape, 1) < side


def normalise(spread):
    center = jnp.mean(spread, axis=-1, keepdims=True)
    offset = spread - center
    variance = jnp.mean(offset * offset, axis=-1, keepdims=True)
    inverse = lax.rsqrt(variance + norm_epsilon)
    return offset * inverse, inverse


def conv_norm(vectors, widened, padded, spread, n_ref, hat_store):
    kernel_ref, bias_ref, gain_ref, shift_ref = vectors[:4]
    height, width, channels = widened.shape
    fill_padded(padded, widened)

    def conv_body(chunk, carry):
        bias = bias_ref[0:1, lanes(chunk)]

        def store(out, value):
            spread[out * width : (out + 1) * width, lanes(chunk)] = value + bias

        convolve(padded, chunk, kernel_ref, height, width, False, store)
        return carry

    lax.fori_loop(0, channels // TILE, conv_body, 0)
    hat, inverse = normalise(spread[...])
    n_ref[...] = (hat * gain_ref[...] + shift_ref[...]).astype(BF16)
    hat_store(hat, inverse)


def mix(side, vectors, widened, total, weights, n_ref, hidden_store):
    first_bias_ref, second_bias_ref, scale_ref = vectors[4:]
    height, width, channels = widened.shape
    hid = first_bias_ref.shape[1]
    total[...] = jnp.zeros(total.shape, F32)

    def mix_body(piece, carry):
        first, second = weights(piece)
        at = columns(piece, channels)
        pre = jnp.dot(n_ref[...], first, preferred_element_type=F32) + first_bias_ref[:, at]
        below, bell = normal_below(pre)
        hidden = (pre * below).astype(BF16)
        hidden_store(piece, hidden, pre, below, bell)
        total[...] += jnp.dot(hidden, second, preferred_element_type=F32)
        return carry

    lax.fori_loop(0, hid // channels, mix_body, 0)
    mixed = total[...] + second_bias_ref[...]
    result = widened + (scale_ref[...] * mixed).reshape(height, width, channels)
    result = jnp.where(real_columns(result.shape, side), result, 0.0)
    return result, mixed


def is_active(sec_ref, tick, count):
    which = tick - sec_ref[0]
    return (which >= 0) & (which < count)


def columns(piece, channels):
    return pl.ds(pl.multiple_of(piece * channels, channels), channels)


def train_kernel(tick, micro, side, kept, sec_ref, image_ref, received_ref, *refs):
    vectors, (first_ref, second_ref) = refs[:7], refs[7:9]
    refs = refs[9 + kept :]
    y_ref, outs = refs[0], refs[1:8]
    refs = refs[8:]
    if tick == 0:
        low_first, low_second = refs[:2]
        refs = refs[2:]
        wide_first, wide_second, wide_sems = refs[12:]
    bufs = refs[:7]
    padded, spread, total, sems, piece_sems = refs[7:12]
    x_buf, hat_buf, inverse_buf, n_buf, mixed_buf, h_buf, slope_buf = bufs
    h_out, slope_out = outs[5:]
    channels = x_buf.shape[-1]
    pieces = h_buf.shape[-1] // channels
    active = is_active(sec_ref, tick, micro)

    def wide_copies(piece):
        at = columns(piece, channels)
        return [
            pltpu.make_async_copy(first_ref.at[:, at], wide_first.at[piece], wide_sems.at[0, piece]),
            pltpu.make_async_copy(second_ref.at[at, :], wide_second.at[piece], wide_sems.at[1, piece]),
        ]

    def weights(piece):
        at = columns(piece, channels)
        if tick > 0:
            return first_ref[:, at], second_ref[at, :]
        for copy in wide_copies(piece):
            copy.wait()
        first = wide_first[piece].astype(BF16)
        second = wide_second[piece].astype(BF16)
        low_first[:, at] = first
        low_second[at, :] = second
        return first, second

    if tick == 0:
        for piece in range(pieces):
            for copy in wide_copies(piece):
                copy.start()

        @pl.when(jnp.logical_not(active))
        def _():
            def body(piece, carry):
                weights(piece)
                return carry

            lax.fori_loop(0, pieces, body, 0)

    @pl.when(active)
    def _():
        slot = tick - sec_ref[0]
        entry = jnp.where(sec_ref[0] == 0, image_ref[0].astype(F32), received_ref[...].astype(F32))
        x_buf[...] = entry.astype(BF16)

        def piece_copies(piece):
            at = columns(piece, channels)
            return [
                pltpu.make_async_copy(h_buf.at[:, at], h_out.at[slot, :, at], piece_sems.at[0, piece]),
                pltpu.make_async_copy(
                    slope_buf.at[:, at], slope_out.at[slot, :, at], piece_sems.at[1, piece]
                ),
            ]

        def hidden_store(piece, hidden, pre, below, bell):
            at = columns(piece, channels)
            h_buf[:, at] = hidden
            slope_buf[:, at] = (below + pre * (bell * (1.0 / math.sqrt(2.0 * math.pi)))).astype(BF16)
            for copy in piece_copies(piece):
                copy.start()

        copies = [
            pltpu.make_async_copy(buf, out.at[slot], sems.at[index])
            for index, (buf, out) in enumerate(zip(bufs[:5], outs[:5]))
        ]

        def hat_store(hat, inverse):
            hat_buf[...] = hat
            inverse_buf[...] = jnp.broadcast_to(inverse, inverse_buf.shape)
            for copy in copies[:4]:
                copy.start()

        conv_norm(vectors, entry, padded, spread, n_buf, hat_store)
        result, mixed = mix(side, vectors, entry, total, weights, n_buf, hidden_store)
        y_ref[...] = result.astype(BF16)
        mixed_buf[...] = mixed
        copies[4].start()
        for copy in copies:
            copy.wait()
        for piece in range(pieces):
            for copy in piece_copies(piece):
                copy.wait()


def early_kernel(sec_ref, image_ref, *refs):
    vectors = refs[:4]
    n_ref, padded, spread = refs[4:]

    @pl.when(sec_ref[0] == 0)
    def _():
        conv_norm(
            vectors, image_ref[...].astype(F32), padded, spread, n_ref, lambda hat, inverse: None
        )


def probe_kernel(tick, side, kept, sec_ref, marked_ref, slot_ref, received_ref, early_ref, *refs):
    vectors, (own_ref, arrived_ref) = refs[:7], refs[7:9]
    refs = refs[9 + kept :]
    y_ref, feature_ref, feature_buf, tiles_buf, padded, spread, total, n_buf, sems, end_sem = refs

    @pl.when(sec_ref[0] == tick)
    def _():
        channels = y_ref.shape[-1]
        tiles = channels // TILE
        groups = vectors[4].shape[1] // channels

        def start(block):
            taken = marked_ref[block] == 1

            @pl.when(taken)
            def _():
                pltpu.make_async_copy(
                    arrived_ref.at[slot_ref[block]], tiles_buf.at[block], sems.at[block]
                ).start()

            @pl.when(jnp.logical_not(taken))
            def _():
                pltpu.make_async_copy(
                    own_ref.at[block], tiles_buf.at[block], sems.at[block]
                ).start()

        for piece in range(groups):
            for item in range(tiles):
                start(piece * tiles + item)
            for item in range(tiles):
                start(groups * tiles + item * groups + piece)

        entry = received_ref[...].astype(F32)

        def wait(block):
            pltpu.make_async_copy(own_ref.at[block], tiles_buf.at[block], sems.at[block]).wait()

        def weights(piece):
            first = [piece * tiles + item for item in range(tiles)]
            second = [groups * tiles + item * groups + piece for item in range(tiles)]
            for block in first + second:
                wait(block)
            return (
                jnp.concatenate([tiles_buf[block] for block in first], axis=1),
                jnp.concatenate([tiles_buf[block] for block in second], axis=1),
            )

        if tick > 0:
            conv_norm(vectors, entry, padded, spread, n_buf, lambda hat, inverse: None)
        result, mixed = mix(
            side,
            vectors,
            entry,
            total,
            weights,
            early_ref if tick == 0 else n_buf,
            lambda piece, hidden, pre, below, bell: None,
        )
        output = result.astype(BF16)
        y_ref[...] = output
        feature_buf[...] = output[:, :side, :]
        done = pltpu.make_async_copy(feature_buf, feature_ref, end_sem)
        done.start()
        done.wait()


def back_kernel(tick, micro, side, sections, kept, turns, sec_ref, slope_in_ref, returned_ref, *refs):
    kernel_ref, gain_ref, scale_ref, first_ref, second_ref = refs[:5]
    hat_ref, inverse_ref, slope_ref, n_ref, h_ref = refs[5:10]
    refs = refs[10 + kept :]
    dx_ref, outs, turned_ref = refs[0], refs[1:5], refs[5]
    dy_buf, dn_buf, dspread_buf, both_buf, turned_buf = refs[6:11]
    hat_buf, inverse_buf, slope_buf, n_buf, h_buf = refs[11:16]
    padded, total, conv_out, sems, piece_sems, in_sems = refs[16:]
    both_out = outs[3]
    which = tick - (sections - 1 - sec_ref[0])
    channels = dx_ref.shape[-1]
    hid = h_buf.shape[-1]
    pieces = hid // channels

    @pl.when((which >= 0) & (which < micro))
    def _():
        height, width, _ = dx_ref.shape
        rows = height * width
        ins = [
            pltpu.make_async_copy(
                slope_ref.at[which, :, columns(piece, channels)],
                slope_buf.at[:, columns(piece, channels)],
                in_sems.at[piece],
            )
            for piece in range(pieces)
        ]
        ins.append(pltpu.make_async_copy(hat_ref.at[which], hat_buf, in_sems.at[pieces]))
        ins.append(pltpu.make_async_copy(inverse_ref.at[which], inverse_buf, in_sems.at[pieces + 1]))
        for copy in ins:
            copy.start()
        dy = jnp.where(
            sec_ref[0] == sections - 1, slope_in_ref[0].astype(F32), returned_ref[...].astype(F32)
        )
        flat = dy.reshape(rows, channels)
        dy_buf[...] = flat.astype(BF16)
        mix_at = columns(pieces, channels)
        both_buf[:, mix_at] = (flat * scale_ref[...]).astype(BF16)
        total[...] = jnp.zeros(total.shape, F32)
        contract = (((1,), (1,)), ((), ()))
        copies = [
            pltpu.make_async_copy(buf, out.at[which], sems.at[index])
            for index, (buf, out) in enumerate(zip((dy_buf, dn_buf, dspread_buf), outs))
        ]
        copies[0].start()

        def both_copy(piece):
            at = columns(piece, channels)
            return pltpu.make_async_copy(
                both_buf.at[:, at], both_out.at[which, :, at], piece_sems.at[piece]
            )

        both_copy(pieces).start()

        def body(piece, carry):
            at = columns(piece, channels)
            dh = lax.dot_general(
                both_buf[:, mix_at], second_ref[at, :], contract, preferred_element_type=F32
            )
            pltpu.make_async_copy(
                slope_ref.at[which, :, at], slope_buf.at[:, at], in_sems.at[piece]
            ).wait()
            dpre = (dh * slope_buf[:, at].astype(F32)).astype(BF16)
            both_buf[:, at] = dpre
            both_copy(piece).start()
            total[...] += lax.dot_general(
                dpre, first_ref[:, at], contract, preferred_element_type=F32
            )
            return carry

        lax.fori_loop(0, pieces, body, 0)
        ins[pieces].wait()
        ins[pieces + 1].wait()
        dn = total[...]
        dn_buf[...] = dn.astype(BF16)
        copies[1].start()
        hat = hat_buf[...]
        dhat = dn * gain_ref[...]
        mean = jnp.mean(dhat, axis=-1, keepdims=True)
        along = jnp.mean(dhat * hat, axis=-1, keepdims=True)
        dspread = inverse_buf[:, 0:1] * (dhat - mean - hat * along)
        dspread_buf[...] = dspread
        copies[2].start()
        if tick < micro + sections - 2:
            fill_padded(padded, dspread.reshape(height, width, channels))

            def conv_body(chunk, carry):
                def store(out, value):
                    conv_out[out, :, lanes(chunk)] = value

                convolve(padded, chunk, kernel_ref, height, width, True, store)
                return carry

            lax.fori_loop(0, channels // TILE, conv_body, 0)
            dx = dy + conv_out[...]
            dx = jnp.where(real_columns(dx.shape, side), dx, 0.0)
            dx_ref[...] = dx.astype(BF16)
        for copy in copies:
            copy.wait()
        for piece in range(pieces + 1):
            both_copy(piece).wait()

    if turns:
        wanted = which == -1
        if tick == micro:
            wanted = wanted | (sec_ref[0] == sections - 1)

        @pl.when(wanted)
        def _():
            get_n = pltpu.make_async_copy(n_ref, n_buf, sems.at[0])
            get_h = pltpu.make_async_copy(h_ref, h_buf, sems.at[1])
            get_n.start()
            get_h.start()
            get_h.wait()
            get_n.wait()
            depth = turned_buf.shape[1]

            def turn(piece, carry):
                at = columns(piece, channels)
                turned_buf[at, :] = h_buf[:, :, at].reshape(depth, channels).T
                return carry

            lax.fori_loop(0, pieces, turn, 0)
            turned_buf[columns(pieces, channels), :] = n_buf[...].reshape(depth, channels).T
            put = pltpu.make_async_copy(turned_buf, turned_ref, sems.at[2])
            put.start()
            put.wait()


def small_kernel(micro, *refs):
    (kernel_ref, bias_ref, gain_ref, shift_ref, first_bias_ref, second_bias_ref, scale_ref) = refs[:7]
    x_ref, hat_ref, mixed_ref, dy_ref, dn_ref, dspread_ref, both_ref = refs[7:14]
    outs = refs[14:21]
    padded = refs[21]
    height, width, channels = x_ref.shape[1:]

    def total(values):
        return jnp.sum(values, axis=0, keepdims=True)

    def chunk_body(chunk, carry):
        at = lanes(chunk)
        scale = scale_ref[0:1, at]
        sums = [0.0] * 5
        for item in range(micro):
            dy = dy_ref[item, :, at].astype(F32)
            dn = dn_ref[item, :, at].astype(F32)
            sums[0] += total(dspread_ref[item, :, at])
            sums[1] += total(dn * hat_ref[item, :, at])
            sums[2] += total(dn)
            sums[3] += total(dy)
            sums[4] += total(dy * mixed_ref[item, :, at])
        outs[1][0:1, at] = bias_ref[0:1, at] - learning_rate * sums[0]
        outs[2][0:1, at] = gain_ref[0:1, at] - learning_rate * sums[1]
        outs[3][0:1, at] = shift_ref[0:1, at] - learning_rate * sums[2]
        outs[5][0:1, at] = second_bias_ref[0:1, at] - learning_rate * (scale * sums[3])
        outs[6][0:1, at] = scale - learning_rate * sums[4]
        padded[...] = jnp.zeros(padded.shape, F32)
        for item in range(micro):
            padded[item, REACH : REACH + height, EDGE : EDGE + width, :] = x_ref[
                item, :, :, at
            ].astype(F32)
        for col in range(TAPS):
            for row in range(TAPS):
                acc = None
                for item in range(micro):
                    for out in range(max(0, REACH - row), min(height, height + REACH - row)):
                        term = (
                            padded[item, out + row, pl.ds(EDGE - REACH + col, width), :]
                            * dspread_ref[item, out * width : (out + 1) * width, at]
                        )
                        acc = term if acc is None else acc + term
                tap = row * TAPS + col
                outs[0][tap, 0:1, at] = kernel_ref[tap, 0:1, at] - learning_rate * total(acc)
        return carry

    lax.fori_loop(0, channels // TILE, chunk_body, 0)
    hid = first_bias_ref.shape[1]

    def bias_body(piece, carry):
        at = lanes(piece)
        acc = 0.0
        for item in range(micro):
            acc += total(both_ref[item, :, at].astype(F32))
        outs[4][0:1, at] = first_bias_ref[0:1, at] - learning_rate * acc
        return carry

    lax.fori_loop(0, hid // TILE, bias_body, 0)


def block_views(block, first_tiles, groups, channels, first_ref, second_ref, act):
    @pl.when(block < first_tiles)
    def _():
        act(first_ref.at[:, lanes(block)])

    @pl.when(block >= first_tiles)
    def _():
        place = block - first_tiles
        group = lax.rem(place, groups)
        act(second_ref.at[columns(group, channels), lanes(lax.div(place, groups))])


def update_kernel(
    first_tiles, groups, sending, order_ref, slot_ref, turned_ref, both_ref, first_ref, second_ref, *refs
):
    if sending:
        (send_ref, wide_buf, slim_buf, in_sems, out_sems) = refs
    else:
        (own_ref, new_first, new_second, wide_buf, slim_buf, in_sems, out_sems, wide_sems) = refs
    count = wide_buf.shape[0]
    channels = wide_buf.shape[1]
    micro, rows, _ = both_ref.shape
    batch = math.gcd(count, 4)

    def fetch(step, carry):
        def act(view):
            pltpu.make_async_copy(view, wide_buf.at[step], in_sems.at[step]).start()

        block_views(order_ref[step], first_tiles, groups, channels, first_ref, second_ref, act)
        return carry

    lax.fori_loop(0, count, fetch, 0)

    def slim_copy(step):
        target = send_ref.at[slot_ref[step]] if sending else own_ref.at[order_ref[step]]
        return pltpu.make_async_copy(slim_buf.at[step], target, out_sems.at[step])

    def body(turn, carry):
        steps = [turn * batch + item for item in range(batch)]
        for step in steps:
            pltpu.make_async_copy(
                first_ref.at[:, lanes(0)], wide_buf.at[step], in_sems.at[step]
            ).wait()
        for step in steps:
            block = order_ref[step]
            is_first = block < first_tiles
            place = jnp.maximum(block - first_tiles, 0)
            group = jnp.where(is_first, groups, lax.rem(place, groups))
            column = jnp.where(is_first, block, first_tiles + lax.div(place, groups))
            grad = jnp.dot(
                turned_ref[columns(group, channels), :],
                both_ref[:, :, lanes(column)].reshape(micro * rows, TILE),
                preferred_element_type=F32,
            )
            updated = wide_buf[step] - learning_rate * grad
            slim_buf[step] = updated.astype(BF16)
            if not sending:
                wide_buf[step] = updated
        for step in steps:
            slim_copy(step).start()
            if not sending:

                def act(view, step=step):
                    pltpu.make_async_copy(wide_buf.at[step], view, wide_sems.at[step]).start()

                block_views(
                    order_ref[step], first_tiles, groups, channels, new_first, new_second, act
                )
        return carry

    lax.fori_loop(0, count // batch, body, 0)

    def drain(step, carry):
        slim_copy(step).wait()
        if not sending:
            pltpu.make_async_copy(
                wide_buf.at[step], new_first.at[:, lanes(0)], wide_sems.at[step]
            ).wait()
        return carry

    lax.fori_loop(0, count, drain, 0)


def place_kernel(
    first_tiles, groups, order_ref, slot_ref, arrived_ref, old_first, old_second, new_first, new_second, *refs
):
    wide_buf, slim_buf, in_sems, out_sems = refs
    count, channels, _ = wide_buf.shape

    def fetch(step, carry):
        pltpu.make_async_copy(
            arrived_ref.at[slot_ref[step]], slim_buf.at[step], in_sems.at[step]
        ).start()
        return carry

    lax.fori_loop(0, count, fetch, 0)

    def body(step, carry):
        pltpu.make_async_copy(arrived_ref.at[0], slim_buf.at[step], in_sems.at[step]).wait()
        wide_buf[step] = slim_buf[step].astype(F32)

        def act(view):
            pltpu.make_async_copy(wide_buf.at[step], view, out_sems.at[step]).start()

        block_views(order_ref[step], first_tiles, groups, channels, new_first, new_second, act)
        return carry

    lax.fori_loop(0, count, body, 0)

    def drain(step, carry):
        pltpu.make_async_copy(
            wide_buf.at[step], new_first.at[:, lanes(0)], out_sems.at[step]
        ).wait()
        return carry

    lax.fori_loop(0, count, drain, 0)


def params_of(limit=VMEM_LIMIT):
    return pltpu.CompilerParams(vmem_limit_bytes=limit)


def cost(flops, read):
    return pl.CostEstimate(flops=flops, bytes_accessed=read, transcendentals=0)


def pinned(arrays):
    return [pltpu.with_memory_space_constraint(item, pltpu.HBM) for item in arrays]


def hbm_spec():
    return pl.BlockSpec(memory_space=pltpu.HBM)


def train_step(tick, micro, side, sec, images, received, vectors, weights, saved):
    height, width, channels = received.shape
    rows = height * width
    hid = vectors[4].shape[1]
    saved_shapes = [
        ((height, width, channels), BF16),
        ((rows, channels), F32),
        ((rows, TILE), F32),
        ((rows, channels), BF16),
        ((rows, channels), F32),
        ((rows, hid), BF16),
        ((rows, hid), BF16),
    ]
    kept = 0 if saved is None else len(saved)
    at = min(tick, micro - 1)
    operands = [images, received, *vectors, *weights] + ([] if saved is None else pinned(saved))
    in_specs = [pl.BlockSpec((1, height, width, channels), lambda i, s: (at, 0, 0, 0))]
    in_specs += [whole(item) for item in operands[1 : len(operands) - kept]]
    in_specs += [hbm_spec()] * kept
    more_specs, more_shapes, more_scratch = [], [], []
    if tick == 0:
        operands[9:11] = pinned(weights)
        in_specs[9:11] = [hbm_spec()] * 2
        more_specs = [whole(item) for item in weights]
        more_shapes = [shaped(item.shape, BF16) for item in weights]
        wide = pltpu.VMEM((hid // channels, channels, channels), F32)
        more_scratch = [wide, wide, pltpu.SemaphoreType.DMA((2, hid // channels))]
    outs = pl.pallas_call(
        functools.partial(train_kernel, tick, micro, side, kept),
        grid_spec=pltpu.PrefetchScalarGridSpec(
            num_scalar_prefetch=1,
            grid=(1,),
            in_specs=in_specs,
            out_specs=[whole(received)] + [hbm_spec() for _ in saved_shapes] + more_specs,
            scratch_shapes=[pltpu.VMEM(shape, dtype) for shape, dtype in saved_shapes]
            + [
                pltpu.VMEM((channels // TILE, height + 2 * REACH, width + 2 * EDGE, TILE), F32),
                pltpu.VMEM((rows, channels), F32),
                pltpu.VMEM((rows, channels), F32),
                pltpu.SemaphoreType.DMA((5,)),
                pltpu.SemaphoreType.DMA((2, hid // channels)),
            ]
            + more_scratch,
        ),
        out_shape=[shaped(received.shape, BF16)]
        + [pltpu.HBM((micro,) + shape, dtype) for shape, dtype in saved_shapes]
        + more_shapes,
        input_output_aliases={1 + len(operands) - kept + i: 1 + i for i in range(kept)},
        compiler_params=params_of(),
        cost_estimate=cost(4 * rows * channels * hid, 8 << 20),
        name=f"train{tick}",
    )(sec, *operands)
    return outs[0], outs[1:8], outs[8:] if tick == 0 else weights


def back_step(tick, micro, side, sections, sec, slopes, returned, params, saved, kept_out):
    height, width, channels = returned.shape
    rows = height * width
    hid = saved[2].shape[-1]
    shapes = [
        ((rows, channels), BF16),
        ((rows, channels), BF16),
        ((rows, channels), F32),
        ((rows, hid + channels), BF16),
    ]
    turned = ((hid + channels, micro * rows), BF16)
    kept = 0 if kept_out is None else len(kept_out)
    operands = [slopes, returned, *params, *pinned(saved)]
    at = min(tick, micro - 1)
    in_specs = [pl.BlockSpec((1, height, width, channels), lambda i, s: (at, 0, 0, 0))]
    in_specs += [whole(item) for item in operands[1:7]]
    in_specs += [hbm_spec()] * (len(saved) + kept)
    base = len(operands)
    operands += [] if kept_out is None else pinned(kept_out)
    turns = tick <= max(sections - 2, micro)
    outs = pl.pallas_call(
        functools.partial(back_kernel, tick, micro, side, sections, kept, turns),
        grid_spec=pltpu.PrefetchScalarGridSpec(
            num_scalar_prefetch=1,
            grid=(1,),
            in_specs=in_specs,
            out_specs=[whole(returned)] + [hbm_spec()] * (len(shapes) + 1),
            scratch_shapes=[pltpu.VMEM(shape, dtype) for shape, dtype in shapes]
            + [
                pltpu.VMEM(*turned),
                pltpu.VMEM((rows, channels), F32),
                pltpu.VMEM((rows, TILE), F32),
                pltpu.VMEM((rows, hid), BF16),
                pltpu.VMEM((micro, rows, channels), BF16),
                pltpu.VMEM((micro, rows, hid), BF16),
                pltpu.VMEM((channels // TILE, height + 2 * REACH, width + 2 * EDGE, TILE), F32),
                pltpu.VMEM((rows, channels), F32),
                pltpu.VMEM((height, width, channels), F32),
                pltpu.SemaphoreType.DMA((3,)),
                pltpu.SemaphoreType.DMA((hid // channels + 1,)),
                pltpu.SemaphoreType.DMA((hid // channels + 2,)),
            ],
        ),
        out_shape=[shaped(returned.shape, BF16)]
        + [pltpu.HBM((micro,) + shape, dtype) for shape, dtype in shapes]
        + [pltpu.HBM(*turned)],
        input_output_aliases={1 + base + i: 1 + i for i in range(kept)},
        compiler_params=params_of(),
        cost_estimate=cost(4 * rows * channels * hid, 8 << 20),
        name=f"back{tick}",
    )(sec, *operands)
    return outs[0], outs[1:]


def small_step(micro, vectors, grads):
    x = grads[0]
    height, width, channels = x.shape[1:]
    return pl.pallas_call(
        functools.partial(small_kernel, micro),
        grid=(1,),
        in_specs=[whole(item) for item in vectors] + [whole(item) for item in grads],
        out_specs=[whole(item) for item in vectors],
        out_shape=[shaped(item.shape, F32) for item in vectors],
        scratch_shapes=[pltpu.VMEM((micro, height + 2 * REACH, width + 2 * EDGE, TILE), F32)],
        compiler_params=params_of(),
        cost_estimate=cost(1 << 28, 8 << 20),
        name="small",
    )(*vectors, *pinned(grads))


def tables(marked, sources):
    member = lax.axis_index("member")
    members = sources.shape[1]
    blocks = marked.shape[0]
    taken = blocks // 2
    capacity = (taken + members - 2) // (members - 1)
    ids = jnp.arange(blocks, dtype=jnp.int32)
    member_ids = jnp.arange(members, dtype=jnp.int32)
    target = jnp.sum(jnp.where(sources == member, member_ids[None, :], 0), axis=1)
    anchor = jnp.sum(jnp.where(member_ids[None, :] == member, sources, 0), axis=1)
    earlier = ids[:, None] > ids[None, :]
    counted = marked[None, :] == 1
    out_rank = jnp.sum(earlier & (target[:, None] == target[None, :]) & counted, axis=1)
    in_rank = jnp.sum(earlier & (anchor[:, None] == anchor[None, :]) & counted, axis=1)
    out_slot = (target * capacity + out_rank).astype(jnp.int32)
    in_slot = (anchor * capacity + in_rank).astype(jnp.int32)
    steps = jnp.arange(taken, dtype=jnp.int32)
    top = members * capacity - 1

    def listed(flags):
        place = jnp.sum(earlier & flags[None, :], axis=1)
        hits = flags[None, :] & (place[None, :] == steps[:, None])
        return hits, jnp.sum(jnp.where(hits, ids[None, :], 0), axis=1)

    is_marked = marked == 1
    hits, marked_order = listed(is_marked)
    send_slots = jnp.clip(jnp.sum(jnp.where(hits, out_slot[None, :], 0), axis=1), 0, top)
    take_slots = jnp.clip(jnp.sum(jnp.where(hits, in_slot[None, :], 0), axis=1), 0, top)
    _, plain_order = listed(~is_marked)
    return dict(
        slots=members * capacity,
        in_slot=jnp.clip(in_slot, 0, top),
        marked_order=marked_order.astype(jnp.int32),
        plain_order=plain_order.astype(jnp.int32),
        send_slots=send_slots.astype(jnp.int32),
        take_slots=take_slots.astype(jnp.int32),
    )


def update_step(sending, order, slots, turned, both, first, second, out_shape):
    count = order.shape[0]
    channels = first.shape[0]
    first_tiles = first.shape[1] // TILE
    groups = second.shape[0] // channels
    sems = [pltpu.SemaphoreType.DMA((count,))] * (2 if sending else 3)
    return pl.pallas_call(
        functools.partial(update_kernel, first_tiles, groups, sending),
        grid_spec=pltpu.PrefetchScalarGridSpec(
            num_scalar_prefetch=2,
            grid=(1,),
            in_specs=[whole(turned), whole(both), hbm_spec(), hbm_spec()],
            out_specs=[hbm_spec() for _ in out_shape],
            scratch_shapes=[
                pltpu.VMEM((count, channels, TILE), F32),
                pltpu.VMEM((count, channels, TILE), BF16),
                *sems,
            ],
        ),
        out_shape=out_shape,
        compiler_params=params_of(),
        cost_estimate=cost(1 << 30, 8 << 20),
        name="send" if sending else "keep",
    )(order, slots, *pinned((turned, both, first, second)))


def local(
    inputs,
    cotangent,
    probe,
    dw_kernel,
    dw_bias,
    norm_gain,
    norm_bias,
    w_in,
    b_in,
    w_out,
    b_out,
    layer_scale,
    shuffle_mask,
    source_member,
):
    sections = lax.axis_size("section")
    sec = lax.axis_index("section").astype(jnp.int32).reshape(1)
    micro = inputs.shape[1]
    height, side, channels = inputs.shape[3:]
    width = (side + 15) // 16 * 16
    rows = height * width
    hid = w_in.shape[3]
    first_tiles = hid // TILE
    groups = hid // channels
    vectors = [
        dw_kernel.reshape(TAPS * TAPS, 1, channels),
        dw_bias[0],
        norm_gain[0],
        norm_bias[0],
        b_in[0],
        b_out[0],
        layer_scale[0],
    ]
    first = w_in[0, 0]
    second = w_out[0, 0]
    lowered = [first, second]

    def padded(maps):
        return jnp.pad(maps, ((0, 0), (0, 0), (0, width - side), (0, 0)))

    images = padded(inputs[0, :, 0])
    slopes = padded(cotangent[0, :, 0])
    trial = padded(probe[0])[0]
    ticks = micro + sections - 1
    received = images[0]
    saved = None
    for tick in range(ticks):
        current, saved, lowered = train_step(
            tick, micro, side, sec, images, received, vectors, lowered, saved
        )
        if tick < ticks - 1:
            pairs = [(s, s + 1) for s in range(sections - 1) if 0 <= tick - s < micro]
            received = lax.ppermute(current, "section", pairs)
    xs, hats, inverses, ns, mixes, hs, gelu_slopes = saved
    kernel, gain, scale = vectors[0], vectors[2], vectors[6]
    returned = slopes[0]
    grads = None
    for tick in range(ticks):
        current, grads = back_step(
            tick,
            micro,
            side,
            sections,
            sec,
            slopes,
            returned,
            (kernel, gain, scale, *lowered),
            (hats, inverses, gelu_slopes, ns, hs),
            grads,
        )
        if tick < ticks - 1:
            pairs = [
                (s, s - 1) for s in range(1, sections) if 0 <= tick - (sections - 1 - s) < micro
            ]
            returned = lax.ppermute(current, "section", pairs)
    dys, dns, dspreads, boths, turned = grads

    table = tables(shuffle_mask[0], source_member[0])
    taken = table["marked_order"].shape[0]
    blocks = shuffle_mask.shape[1]
    (outgoing,) = update_step(
        True,
        table["marked_order"],
        table["send_slots"],
        turned,
        boths,
        first,
        second,
        [pltpu.HBM((table["slots"], channels, TILE), BF16)],
    )
    arrived = lax.all_to_all(outgoing, "member", split_axis=0, concat_axis=0, tiled=True)
    own, new_first, new_second = update_step(
        False,
        table["plain_order"],
        table["plain_order"],
        turned,
        boths,
        first,
        second,
        [
            pltpu.HBM((blocks, channels, TILE), BF16),
            pltpu.HBM(first.shape, F32),
            pltpu.HBM(second.shape, F32),
        ],
    )
    vectors = small_step(micro, vectors, (xs, hats, mixes, dys, dns, dspreads, boths))

    new_first, new_second = pl.pallas_call(
        functools.partial(place_kernel, first_tiles, groups),
        grid_spec=pltpu.PrefetchScalarGridSpec(
            num_scalar_prefetch=2,
            grid=(1,),
            in_specs=[hbm_spec()] * 3,
            out_specs=[hbm_spec()] * 2,
            scratch_shapes=[
                pltpu.VMEM((taken, channels, TILE), F32),
                pltpu.VMEM((taken, channels, TILE), BF16),
                pltpu.SemaphoreType.DMA((taken,)),
                pltpu.SemaphoreType.DMA((taken,)),
            ],
        ),
        out_shape=[pltpu.HBM(first.shape, F32), pltpu.HBM(second.shape, F32)],
        input_output_aliases={3: 0, 4: 1},
        compiler_params=params_of(),
        cost_estimate=cost(0, 8 << 20),
        name="place",
    )(table["marked_order"], table["take_slots"], *pinned((arrived, new_first, new_second)))

    early = pl.pallas_call(
        early_kernel,
        grid_spec=pltpu.PrefetchScalarGridSpec(
            num_scalar_prefetch=1,
            grid=(1,),
            in_specs=[whole(trial)] + [whole(item) for item in vectors[:4]],
            out_specs=pl.BlockSpec((rows, channels), lambda i, s: (0, 0)),
            scratch_shapes=[
                pltpu.VMEM((channels // TILE, height + 2 * REACH, width + 2 * EDGE, TILE), F32),
                pltpu.VMEM((rows, channels), F32),
            ],
        ),
        out_shape=shaped((rows, channels), BF16),
        compiler_params=params_of(),
        cost_estimate=cost(1 << 26, 1 << 20),
        name="early",
    )(sec, trial, *vectors[:4])
    received = trial
    features = None
    for tick in range(sections):
        operands = [received, early, *vectors, *pinned((own, arrived))]
        in_specs = [whole(item) for item in operands[:-2]] + [hbm_spec(), hbm_spec()]
        kept = 0 if features is None else 1
        if kept:
            operands += pinned([features])
            in_specs.append(hbm_spec())
        result, features = pl.pallas_call(
            functools.partial(probe_kernel, tick, side, kept),
            grid_spec=pltpu.PrefetchScalarGridSpec(
                num_scalar_prefetch=3,
                grid=(1,),
                in_specs=in_specs,
                out_specs=[whole(trial), hbm_spec()],
                scratch_shapes=[
                    pltpu.VMEM((height, side, channels), BF16),
                    pltpu.VMEM((blocks, channels, TILE), BF16),
                    pltpu.VMEM(
                        (channels // TILE, height + 2 * REACH, width + 2 * EDGE, TILE), F32
                    ),
                    pltpu.VMEM((rows, channels), F32),
                    pltpu.VMEM((rows, channels), F32),
                    pltpu.VMEM((rows, channels), BF16),
                    pltpu.SemaphoreType.DMA((blocks,)),
                    pltpu.SemaphoreType.DMA,
                ],
            ),
            out_shape=[shaped(trial.shape, BF16), pltpu.HBM((height, side, channels), BF16)],
            input_output_aliases={2 + len(operands): 1} if kept else {},
            compiler_params=params_of(),
            cost_estimate=cost(4 * rows * channels * hid, 8 << 20),
            name=f"probe{tick}",
        )(sec, shuffle_mask[0], table["in_slot"], *operands)
        if tick < sections - 1:
            received = lax.ppermute(result, "section", [(tick, tick + 1)])
    return (new_first[None, None], new_second[None, None], features[None, None, None])


def solution(mesh):
    return jax.shard_map(
        local,
        mesh=mesh,
        in_specs=(
            P("member", None, None, None, None, None),
            P("member", None, None, None, None, None),
            P("member", None, None, None, None),
            P("member", "section", None, None, None),
            P("member", "section", None),
            P("member", "section", None),
            P("member", "section", None),
            P("member", "section", None, None),
            P("member", "section", None),
            P("member", "section", None, None),
            P("member", "section", None),
            P("member", "section", None),
            P("section", None),
            P("section", None, None),
        ),
        out_specs=(
            P("member", "section", None, None),
            P("member", "section", None, None),
            P("member", "section", None, None, None, None),
        ),
        check_vma=False,
    )
```

```python
import functools
import math

import jax
import jax.numpy as jnp
from jax import lax
from jax.experimental import pallas as pl
from jax.experimental.pallas import tpu as pltpu
from jax.sharding import PartitionSpec as P

TILE = 128
learning_rate = 0.001
norm_epsilon = 1e-06
F32 = jnp.float32
BF16 = jnp.bfloat16
EDGE = 8
REACH = 3
TAPS = 2 * REACH + 1
VMEM_LIMIT = 36 * 1024 * 1024

TURN = 0.3275911 * math.sqrt(0.5)
TERMS = (1.061405429, -1.453152027, 1.421413741, -0.284496736, 0.254829592)


def normal_below(pre):
    bell = jnp.exp2((pre * pre) * (-0.5 * math.log2(math.e)))
    turn = 1.0 / (1.0 + TURN * jnp.abs(pre))
    poly = jnp.full_like(turn, 0.5 * TERMS[0])
    for term in TERMS[1:]:
        poly = poly * turn + 0.5 * term
    tail = poly * turn * bell
    return jnp.where(pre >= 0.0, 1.0 - tail, tail), bell


def whole(array):
    rank = len(array.shape)
    return pl.BlockSpec(array.shape, lambda *args: (0,) * rank)


def lanes(index):
    return pl.ds(pl.multiple_of(index * TILE, TILE), TILE)


def shaped(shape, dtype):
    return jax.ShapeDtypeStruct(shape, dtype)


def convolve(padded, chunk, kernel_ref, height, width, flip, store):
    totals = [None] * height
    for col in range(TAPS):
        taps = []
        for row in range(TAPS):
            at = row * TAPS + col
            if flip:
                at = TAPS * TAPS - 1 - at
            taps.append(kernel_ref[at, 0:1, lanes(chunk)])
        for line in range(REACH, REACH + height):
            values = padded[chunk, line, pl.ds(EDGE - REACH + col, width), :]
            for row in range(TAPS):
                out = line - row
                if 0 <= out < height:
                    term = values * taps[row]
                    totals[out] = term if totals[out] is None else totals[out] + term
    for out in range(height):
        store(out, totals[out])


def fill_padded(padded, maps):
    height, width, channels = maps.shape
    padded[...] = jnp.zeros(padded.shape, F32)
    for chunk in range(channels // TILE):
        padded[chunk, REACH : REACH + height, EDGE : EDGE + width, :] = maps[
            :, :, chunk * TILE : (chunk + 1) * TILE
        ]


def real_columns(shape, side):
    return lax.broadcasted_iota(jnp.int32, shape, 1) < side


def normalise(spread):
    center = jnp.mean(spread, axis=-1, keepdims=True)
    offset = spread - center
    variance = jnp.mean(offset * offset, axis=-1, keepdims=True)
    inverse = lax.rsqrt(variance + norm_epsilon)
    return offset * inverse, inverse


def conv_norm(vectors, widened, padded, spread, n_ref, hat_store):
    kernel_ref, bias_ref, gain_ref, shift_ref = vectors[:4]
    height, width, channels = widened.shape
    fill_padded(padded, widened)

    def conv_body(chunk, carry):
        bias = bias_ref[0:1, lanes(chunk)]

        def store(out, value):
            spread[out * width : (out + 1) * width, lanes(chunk)] = value + bias

        convolve(padded, chunk, kernel_ref, height, width, False, store)
        return carry

    lax.fori_loop(0, channels // TILE, conv_body, 0)
    hat, inverse = normalise(spread[...])
    n_ref[...] = (hat * gain_ref[...] + shift_ref[...]).astype(BF16)
    hat_store(hat, inverse)


def mix(side, vectors, widened, total, weights, n_ref, hidden_store):
    first_bias_ref, second_bias_ref, scale_ref = vectors[4:]
    height, width, channels = widened.shape
    hid = first_bias_ref.shape[1]
    total[...] = jnp.zeros(total.shape, F32)

    def mix_body(piece, carry):
        first, second = weights(piece)
        at = columns(piece, channels)
        pre = jnp.dot(n_ref[...], first, preferred_element_type=F32) + first_bias_ref[:, at]
        below, bell = normal_below(pre)
        hidden = (pre * below).astype(BF16)
        hidden_store(piece, hidden, pre, below, bell)
        total[...] += jnp.dot(hidden, second, preferred_element_type=F32)
        return carry

    lax.fori_loop(0, hid // channels, mix_body, 0)
    mixed = total[...] + second_bias_ref[...]
    result = widened + (scale_ref[...] * mixed).reshape(height, width, channels)
    result = jnp.where(real_columns(result.shape, side), result, 0.0)
    return result, mixed


def columns(piece, channels):
    return pl.ds(pl.multiple_of(piece * channels, channels), channels)


def train_kernel(owner, slot, side, kept, sec_ref, entry_ref, *refs):
    vectors, (first_ref, second_ref) = refs[:7], refs[7:9]
    refs = refs[9 + kept :]
    y_ref, outs = refs[0], refs[1:8]
    refs = refs[8:]
    leading = kept == 0
    if leading:
        low_first, low_second = refs[:2]
        refs = refs[2:]
        wide_first, wide_second, wide_sems = refs[12:]
    bufs = refs[:7]
    padded, spread, total, sems, piece_sems = refs[7:12]
    x_buf, hat_buf, inverse_buf, n_buf, mixed_buf, h_buf, slope_buf = bufs
    h_out, slope_out = outs[5:]
    channels = x_buf.shape[-1]
    pieces = h_buf.shape[-1] // channels
    active = sec_ref[0] == owner

    def wide_copies(piece):
        at = columns(piece, channels)
        return [
            pltpu.make_async_copy(first_ref.at[:, at], wide_first.at[piece], wide_sems.at[0, piece]),
            pltpu.make_async_copy(second_ref.at[at, :], wide_second.at[piece], wide_sems.at[1, piece]),
        ]

    def weights(piece):
        at = columns(piece, channels)
        if not leading:
            return first_ref[:, at], second_ref[at, :]
        for copy in wide_copies(piece):
            copy.wait()
        first = wide_first[piece].astype(BF16)
        second = wide_second[piece].astype(BF16)
        low_first[:, at] = first
        low_second[at, :] = second
        return first, second

    if leading:
        for piece in range(pieces):
            for copy in wide_copies(piece):
                copy.start()

        @pl.when(jnp.logical_not(active))
        def _():
            def body(piece, carry):
                weights(piece)
                return carry

            lax.fori_loop(0, pieces, body, 0)

    @pl.when(active)
    def _():
        entry = entry_ref[...].astype(F32)
        x_buf[...] = entry_ref[...]

        def piece_copies(piece):
            at = columns(piece, channels)
            return [
                pltpu.make_async_copy(h_buf.at[:, at], h_out.at[slot, :, at], piece_sems.at[0, piece]),
                pltpu.make_async_copy(
                    slope_buf.at[:, at], slope_out.at[slot, :, at], piece_sems.at[1, piece]
                ),
            ]

        def hidden_store(piece, hidden, pre, below, bell):
            at = columns(piece, channels)
            h_buf[:, at] = hidden
            slope_buf[:, at] = (below + pre * (bell * (1.0 / math.sqrt(2.0 * math.pi)))).astype(BF16)
            for copy in piece_copies(piece):
                copy.start()

        copies = [
            pltpu.make_async_copy(buf, out.at[slot], sems.at[index])
            for index, (buf, out) in enumerate(zip(bufs[:5], outs[:5]))
        ]

        def hat_store(hat, inverse):
            hat_buf[...] = hat
            inverse_buf[...] = jnp.broadcast_to(inverse, inverse_buf.shape)
            for copy in copies[:4]:
                copy.start()

        conv_norm(vectors, entry, padded, spread, n_buf, hat_store)
        result, mixed = mix(side, vectors, entry, total, weights, n_buf, hidden_store)
        y_ref[...] = result.astype(BF16)
        mixed_buf[...] = mixed
        copies[4].start()
        for copy in copies:
            copy.wait()
        for piece in range(pieces):
            for copy in piece_copies(piece):
                copy.wait()


def early_kernel(sec_ref, image_ref, *refs):
    vectors = refs[:4]
    n_ref, padded, spread = refs[4:]

    @pl.when(sec_ref[0] == 0)
    def _():
        conv_norm(
            vectors, image_ref[...].astype(F32), padded, spread, n_ref, lambda hat, inverse: None
        )


def probe_kernel(tick, side, kept, sec_ref, marked_ref, slot_ref, received_ref, early_ref, *refs):
    vectors, (own_ref, arrived_ref) = refs[:7], refs[7:9]
    refs = refs[9 + kept :]
    y_ref, feature_ref, feature_buf, tiles_buf, padded, spread, total, n_buf, sems, end_sem = refs

    @pl.when(sec_ref[0] == tick)
    def _():
        channels = y_ref.shape[-1]
        tiles = channels // TILE
        groups = vectors[4].shape[1] // channels

        def start(block):
            taken = marked_ref[block] == 1

            @pl.when(taken)
            def _():
                pltpu.make_async_copy(
                    arrived_ref.at[slot_ref[block]], tiles_buf.at[block], sems.at[block]
                ).start()

            @pl.when(jnp.logical_not(taken))
            def _():
                pltpu.make_async_copy(
                    own_ref.at[block], tiles_buf.at[block], sems.at[block]
                ).start()

        for piece in range(groups):
            for item in range(tiles):
                start(piece * tiles + item)
            for item in range(tiles):
                start(groups * tiles + item * groups + piece)

        entry = received_ref[...].astype(F32)

        def wait(block):
            pltpu.make_async_copy(own_ref.at[block], tiles_buf.at[block], sems.at[block]).wait()

        def weights(piece):
            first = [piece * tiles + item for item in range(tiles)]
            second = [groups * tiles + item * groups + piece for item in range(tiles)]
            for block in first + second:
                wait(block)
            return (
                jnp.concatenate([tiles_buf[block] for block in first], axis=1),
                jnp.concatenate([tiles_buf[block] for block in second], axis=1),
            )

        if tick > 0:
            conv_norm(vectors, entry, padded, spread, n_buf, lambda hat, inverse: None)
        result, mixed = mix(
            side,
            vectors,
            entry,
            total,
            weights,
            early_ref if tick == 0 else n_buf,
            lambda piece, hidden, pre, below, bell: None,
        )
        output = result.astype(BF16)
        y_ref[...] = output
        feature_buf[...] = output[:, :side, :]
        done = pltpu.make_async_copy(feature_buf, feature_ref, end_sem)
        done.start()
        done.wait()


def back_kernel(owner, which, side, turning, kept, sec_ref, returned_ref, *refs):
    kernel_ref, gain_ref, scale_ref, first_ref, second_ref = refs[:5]
    hat_ref, inverse_ref, slope_ref, n_ref, h_ref = refs[5:10]
    refs = refs[10 + kept :]
    dx_ref, outs, turned_ref = refs[0], refs[1:5], refs[5]
    dy_buf, dn_buf, dspread_buf, both_buf, turned_buf = refs[6:11]
    hat_buf, inverse_buf, slope_buf, n_buf, h_buf = refs[11:16]
    padded, total, conv_out, sems, piece_sems, in_sems = refs[16:]
    both_out = outs[3]
    channels = dx_ref.shape[-1]
    hid = h_buf.shape[-1]
    pieces = hid // channels

    @pl.when(sec_ref[0] == owner)
    def _():
        height, width, _ = dx_ref.shape
        rows = height * width
        ins = [
            pltpu.make_async_copy(
                slope_ref.at[which, :, columns(piece, channels)],
                slope_buf.at[:, columns(piece, channels)],
                in_sems.at[piece],
            )
            for piece in range(pieces)
        ]
        ins.append(pltpu.make_async_copy(hat_ref.at[which], hat_buf, in_sems.at[pieces]))
        ins.append(pltpu.make_async_copy(inverse_ref.at[which], inverse_buf, in_sems.at[pieces + 1]))
        for copy in ins:
            copy.start()
        dy = returned_ref[...].astype(F32)
        flat = dy.reshape(rows, channels)
        dy_buf[...] = flat.astype(BF16)
        mix_at = columns(pieces, channels)
        both_buf[:, mix_at] = (flat * scale_ref[...]).astype(BF16)
        total[...] = jnp.zeros(total.shape, F32)
        contract = (((1,), (1,)), ((), ()))
        copies = [
            pltpu.make_async_copy(buf, out.at[which], sems.at[index])
            for index, (buf, out) in enumerate(zip((dy_buf, dn_buf, dspread_buf), outs))
        ]
        copies[0].start()

        def both_copy(piece):
            at = columns(piece, channels)
            return pltpu.make_async_copy(
                both_buf.at[:, at], both_out.at[which, :, at], piece_sems.at[piece]
            )

        both_copy(pieces).start()

        def body(piece, carry):
            at = columns(piece, channels)
            dh = lax.dot_general(
                both_buf[:, mix_at], second_ref[at, :], contract, preferred_element_type=F32
            )
            pltpu.make_async_copy(
                slope_ref.at[which, :, at], slope_buf.at[:, at], in_sems.at[piece]
            ).wait()
            dpre = (dh * slope_buf[:, at].astype(F32)).astype(BF16)
            both_buf[:, at] = dpre
            both_copy(piece).start()
            total[...] += lax.dot_general(
                dpre, first_ref[:, at], contract, preferred_element_type=F32
            )
            return carry

        lax.fori_loop(0, pieces, body, 0)
        ins[pieces].wait()
        ins[pieces + 1].wait()
        dn = total[...]
        dn_buf[...] = dn.astype(BF16)
        copies[1].start()
        hat = hat_buf[...]
        dhat = dn * gain_ref[...]
        mean = jnp.mean(dhat, axis=-1, keepdims=True)
        along = jnp.mean(dhat * hat, axis=-1, keepdims=True)
        dspread = inverse_buf[:, 0:1] * (dhat - mean - hat * along)
        dspread_buf[...] = dspread
        copies[2].start()
        if owner > 0:
            fill_padded(padded, dspread.reshape(height, width, channels))

            def conv_body(chunk, carry):
                def store(out, value):
                    conv_out[out, :, lanes(chunk)] = value

                convolve(padded, chunk, kernel_ref, height, width, True, store)
                return carry

            lax.fori_loop(0, channels // TILE, conv_body, 0)
            dx = dy + conv_out[...]
            dx = jnp.where(real_columns(dx.shape, side), dx, 0.0)
            dx_ref[...] = dx.astype(BF16)
        for copy in copies:
            copy.wait()
        for piece in range(pieces + 1):
            both_copy(piece).wait()

    if turning is not None:
        low, high = turning

        @pl.when((sec_ref[0] >= low) & (sec_ref[0] < high))
        def _():
            get_n = pltpu.make_async_copy(n_ref, n_buf, sems.at[0])
            get_h = pltpu.make_async_copy(h_ref, h_buf, sems.at[1])
            get_n.start()
            get_h.start()
            get_h.wait()
            get_n.wait()
            depth = turned_buf.shape[1]

            def turn(piece, carry):
                at = columns(piece, channels)
                turned_buf[at, :] = h_buf[:, :, at].reshape(depth, channels).T
                return carry

            lax.fori_loop(0, pieces, turn, 0)
            turned_buf[columns(pieces, channels), :] = n_buf[...].reshape(depth, channels).T
            put = pltpu.make_async_copy(turned_buf, turned_ref, sems.at[2])
            put.start()
            put.wait()


def small_kernel(micro, *refs):
    (kernel_ref, bias_ref, gain_ref, shift_ref, first_bias_ref, second_bias_ref, scale_ref) = refs[:7]
    x_ref, hat_ref, mixed_ref, dy_ref, dn_ref, dspread_ref, both_ref = refs[7:14]
    outs = refs[14:21]
    padded = refs[21]
    height, width, channels = x_ref.shape[1:]

    def total(values):
        return jnp.sum(values, axis=0, keepdims=True)

    def chunk_body(chunk, carry):
        at = lanes(chunk)
        scale = scale_ref[0:1, at]
        sums = [0.0] * 5
        for item in range(micro):
            dy = dy_ref[item, :, at].astype(F32)
            dn = dn_ref[item, :, at].astype(F32)
            sums[0] += total(dspread_ref[item, :, at])
            sums[1] += total(dn * hat_ref[item, :, at])
            sums[2] += total(dn)
            sums[3] += total(dy)
            sums[4] += total(dy * mixed_ref[item, :, at])
        outs[1][0:1, at] = bias_ref[0:1, at] - learning_rate * sums[0]
        outs[2][0:1, at] = gain_ref[0:1, at] - learning_rate * sums[1]
        outs[3][0:1, at] = shift_ref[0:1, at] - learning_rate * sums[2]
        outs[5][0:1, at] = second_bias_ref[0:1, at] - learning_rate * (scale * sums[3])
        outs[6][0:1, at] = scale - learning_rate * sums[4]
        padded[...] = jnp.zeros(padded.shape, F32)
        for item in range(micro):
            padded[item, REACH : REACH + height, EDGE : EDGE + width, :] = x_ref[
                item, :, :, at
            ].astype(F32)
        for col in range(TAPS):
            for row in range(TAPS):
                acc = None
                for item in range(micro):
                    for out in range(max(0, REACH - row), min(height, height + REACH - row)):
                        term = (
                            padded[item, out + row, pl.ds(EDGE - REACH + col, width), :]
                            * dspread_ref[item, out * width : (out + 1) * width, at]
                        )
                        acc = term if acc is None else acc + term
                tap = row * TAPS + col
                outs[0][tap, 0:1, at] = kernel_ref[tap, 0:1, at] - learning_rate * total(acc)
        return carry

    lax.fori_loop(0, channels // TILE, chunk_body, 0)
    hid = first_bias_ref.shape[1]

    def bias_body(piece, carry):
        at = lanes(piece)
        acc = 0.0
        for item in range(micro):
            acc += total(both_ref[item, :, at].astype(F32))
        outs[4][0:1, at] = first_bias_ref[0:1, at] - learning_rate * acc
        return carry

    lax.fori_loop(0, hid // TILE, bias_body, 0)


def block_views(block, first_tiles, groups, channels, first_ref, second_ref, act):
    @pl.when(block < first_tiles)
    def _():
        act(first_ref.at[:, lanes(block)])

    @pl.when(block >= first_tiles)
    def _():
        place = block - first_tiles
        group = lax.rem(place, groups)
        act(second_ref.at[columns(group, channels), lanes(lax.div(place, groups))])


def update_kernel(
    first_tiles, groups, sending, order_ref, slot_ref, turned_ref, both_ref, first_ref, second_ref, *refs
):
    if sending:
        (send_ref, wide_buf, slim_buf, in_sems, out_sems) = refs
    else:
        (own_ref, new_first, new_second, wide_buf, slim_buf, in_sems, out_sems, wide_sems) = refs
    count = wide_buf.shape[0]
    channels = wide_buf.shape[1]
    micro, rows, _ = both_ref.shape
    batch = math.gcd(count, 4)

    def fetch(step, carry):
        def act(view):
            pltpu.make_async_copy(view, wide_buf.at[step], in_sems.at[step]).start()

        block_views(order_ref[step], first_tiles, groups, channels, first_ref, second_ref, act)
        return carry

    lax.fori_loop(0, count, fetch, 0)

    def slim_copy(step):
        target = send_ref.at[slot_ref[step]] if sending else own_ref.at[order_ref[step]]
        return pltpu.make_async_copy(slim_buf.at[step], target, out_sems.at[step])

    def body(turn, carry):
        steps = [turn * batch + item for item in range(batch)]
        for step in steps:
            pltpu.make_async_copy(
                first_ref.at[:, lanes(0)], wide_buf.at[step], in_sems.at[step]
            ).wait()
        for step in steps:
            block = order_ref[step]
            is_first = block < first_tiles
            place = jnp.maximum(block - first_tiles, 0)
            group = jnp.where(is_first, groups, lax.rem(place, groups))
            column = jnp.where(is_first, block, first_tiles + lax.div(place, groups))
            grad = jnp.dot(
                turned_ref[columns(group, channels), :],
                both_ref[:, :, lanes(column)].reshape(micro * rows, TILE),
                preferred_element_type=F32,
            )
            updated = wide_buf[step] - learning_rate * grad
            slim_buf[step] = updated.astype(BF16)
            if not sending:
                wide_buf[step] = updated
        for step in steps:
            slim_copy(step).start()
            if not sending:

                def act(view, step=step):
                    pltpu.make_async_copy(wide_buf.at[step], view, wide_sems.at[step]).start()

                block_views(
                    order_ref[step], first_tiles, groups, channels, new_first, new_second, act
                )
        return carry

    lax.fori_loop(0, count // batch, body, 0)

    def drain(step, carry):
        slim_copy(step).wait()
        if not sending:
            pltpu.make_async_copy(
                wide_buf.at[step], new_first.at[:, lanes(0)], wide_sems.at[step]
            ).wait()
        return carry

    lax.fori_loop(0, count, drain, 0)


def place_kernel(
    first_tiles, groups, order_ref, slot_ref, arrived_ref, old_first, old_second, new_first, new_second, *refs
):
    wide_buf, slim_buf, in_sems, out_sems = refs
    count, channels, _ = wide_buf.shape

    def fetch(step, carry):
        pltpu.make_async_copy(
            arrived_ref.at[slot_ref[step]], slim_buf.at[step], in_sems.at[step]
        ).start()
        return carry

    lax.fori_loop(0, count, fetch, 0)

    def body(step, carry):
        pltpu.make_async_copy(arrived_ref.at[0], slim_buf.at[step], in_sems.at[step]).wait()
        wide_buf[step] = slim_buf[step].astype(F32)

        def act(view):
            pltpu.make_async_copy(wide_buf.at[step], view, out_sems.at[step]).start()

        block_views(order_ref[step], first_tiles, groups, channels, new_first, new_second, act)
        return carry

    lax.fori_loop(0, count, body, 0)

    def drain(step, carry):
        pltpu.make_async_copy(
            wide_buf.at[step], new_first.at[:, lanes(0)], out_sems.at[step]
        ).wait()
        return carry

    lax.fori_loop(0, count, drain, 0)


def params_of(limit=VMEM_LIMIT):
    return pltpu.CompilerParams(vmem_limit_bytes=limit)


def cost(flops, read):
    return pl.CostEstimate(flops=flops, bytes_accessed=read, transcendentals=0)


def pinned(arrays):
    return [pltpu.with_memory_space_constraint(item, pltpu.HBM) for item in arrays]


def hbm_spec():
    return pl.BlockSpec(memory_space=pltpu.HBM)


def train_step(owner, slot, micro, side, sec, received, vectors, weights, saved):
    height, width, channels = received.shape
    rows = height * width
    hid = vectors[4].shape[1]
    saved_shapes = [
        ((height, width, channels), BF16),
        ((rows, channels), F32),
        ((rows, TILE), F32),
        ((rows, channels), BF16),
        ((rows, channels), F32),
        ((rows, hid), BF16),
        ((rows, hid), BF16),
    ]
    kept = 0 if saved is None else len(saved)
    operands = [received, *vectors, *weights] + ([] if saved is None else pinned(saved))
    in_specs = [whole(item) for item in operands[: len(operands) - kept]]
    in_specs += [hbm_spec()] * kept
    more_specs, more_shapes, more_scratch = [], [], []
    if saved is None:
        operands[8:10] = pinned(weights)
        in_specs[8:10] = [hbm_spec()] * 2
        more_specs = [whole(item) for item in weights]
        more_shapes = [shaped(item.shape, BF16) for item in weights]
        wide = pltpu.VMEM((hid // channels, channels, channels), F32)
        more_scratch = [wide, wide, pltpu.SemaphoreType.DMA((2, hid // channels))]
    outs = pl.pallas_call(
        functools.partial(train_kernel, owner, slot, side, kept),
        grid_spec=pltpu.PrefetchScalarGridSpec(
            num_scalar_prefetch=1,
            grid=(1,),
            in_specs=in_specs,
            out_specs=[whole(received)] + [hbm_spec() for _ in saved_shapes] + more_specs,
            scratch_shapes=[pltpu.VMEM(shape, dtype) for shape, dtype in saved_shapes]
            + [
                pltpu.VMEM((channels // TILE, height + 2 * REACH, width + 2 * EDGE, TILE), F32),
                pltpu.VMEM((rows, channels), F32),
                pltpu.VMEM((rows, channels), F32),
                pltpu.SemaphoreType.DMA((5,)),
                pltpu.SemaphoreType.DMA((2, hid // channels)),
            ]
            + more_scratch,
        ),
        out_shape=[shaped(received.shape, BF16)]
        + [pltpu.HBM((micro,) + shape, dtype) for shape, dtype in saved_shapes]
        + more_shapes,
        input_output_aliases={1 + len(operands) - kept + i: 1 + i for i in range(kept)},
        compiler_params=params_of(),
        cost_estimate=cost(4 * rows * channels * hid, 8 << 20),
        name=f"train_{owner}_{slot}",
    )(sec, *operands)
    return outs[0], outs[1:8], outs[8:] if saved is None else weights


def back_step(owner, which, micro, side, turning, sec, returned, params, saved, kept_out):
    height, width, channels = returned.shape
    rows = height * width
    hid = saved[2].shape[-1]
    shapes = [
        ((rows, channels), BF16),
        ((rows, channels), BF16),
        ((rows, channels), F32),
        ((rows, hid + channels), BF16),
    ]
    turned = ((hid + channels, micro * rows), BF16)
    kept = 0 if kept_out is None else len(kept_out)
    operands = [returned, *params, *pinned(saved)]
    in_specs = [whole(item) for item in operands[:6]]
    in_specs += [hbm_spec()] * (len(saved) + kept)
    base = len(operands)
    operands += [] if kept_out is None else pinned(kept_out)
    outs = pl.pallas_call(
        functools.partial(back_kernel, owner, which, side, turning, kept),
        grid_spec=pltpu.PrefetchScalarGridSpec(
            num_scalar_prefetch=1,
            grid=(1,),
            in_specs=in_specs,
            out_specs=[whole(returned)] + [hbm_spec()] * (len(shapes) + 1),
            scratch_shapes=[pltpu.VMEM(shape, dtype) for shape, dtype in shapes]
            + [
                pltpu.VMEM(*turned),
                pltpu.VMEM((rows, channels), F32),
                pltpu.VMEM((rows, TILE), F32),
                pltpu.VMEM((rows, hid), BF16),
                pltpu.VMEM((micro, rows, channels), BF16),
                pltpu.VMEM((micro, rows, hid), BF16),
                pltpu.VMEM((channels // TILE, height + 2 * REACH, width + 2 * EDGE, TILE), F32),
                pltpu.VMEM((rows, channels), F32),
                pltpu.VMEM((height, width, channels), F32),
                pltpu.SemaphoreType.DMA((3,)),
                pltpu.SemaphoreType.DMA((hid // channels + 1,)),
                pltpu.SemaphoreType.DMA((hid // channels + 2,)),
            ],
        ),
        out_shape=[shaped(returned.shape, BF16)]
        + [pltpu.HBM((micro,) + shape, dtype) for shape, dtype in shapes]
        + [pltpu.HBM(*turned)],
        input_output_aliases={1 + base + i: 1 + i for i in range(kept)},
        compiler_params=params_of(),
        cost_estimate=cost(4 * rows * channels * hid, 8 << 20),
        name=f"back_{owner}_{which}",
    )(sec, *operands)
    return outs[0], outs[1:]


def small_step(micro, vectors, grads):
    x = grads[0]
    height, width, channels = x.shape[1:]
    return pl.pallas_call(
        functools.partial(small_kernel, micro),
        grid=(1,),
        in_specs=[whole(item) for item in vectors] + [whole(item) for item in grads],
        out_specs=[whole(item) for item in vectors],
        out_shape=[shaped(item.shape, F32) for item in vectors],
        scratch_shapes=[pltpu.VMEM((micro, height + 2 * REACH, width + 2 * EDGE, TILE), F32)],
        compiler_params=params_of(),
        cost_estimate=cost(1 << 28, 8 << 20),
        name="small",
    )(*vectors, *pinned(grads))


def tables(marked, sources):
    member = lax.axis_index("member")
    members = sources.shape[1]
    blocks = marked.shape[0]
    taken = blocks // 2
    capacity = (taken + members - 2) // (members - 1)
    ids = jnp.arange(blocks, dtype=jnp.int32)
    member_ids = jnp.arange(members, dtype=jnp.int32)
    target = jnp.sum(jnp.where(sources == member, member_ids[None, :], 0), axis=1)
    anchor = jnp.sum(jnp.where(member_ids[None, :] == member, sources, 0), axis=1)
    earlier = ids[:, None] > ids[None, :]
    counted = marked[None, :] == 1
    out_rank = jnp.sum(earlier & (target[:, None] == target[None, :]) & counted, axis=1)
    in_rank = jnp.sum(earlier & (anchor[:, None] == anchor[None, :]) & counted, axis=1)
    out_slot = (target * capacity + out_rank).astype(jnp.int32)
    in_slot = (anchor * capacity + in_rank).astype(jnp.int32)
    steps = jnp.arange(taken, dtype=jnp.int32)
    top = members * capacity - 1

    def listed(flags):
        place = jnp.sum(earlier & flags[None, :], axis=1)
        hits = flags[None, :] & (place[None, :] == steps[:, None])
        return hits, jnp.sum(jnp.where(hits, ids[None, :], 0), axis=1)

    is_marked = marked == 1
    hits, marked_order = listed(is_marked)
    send_slots = jnp.clip(jnp.sum(jnp.where(hits, out_slot[None, :], 0), axis=1), 0, top)
    take_slots = jnp.clip(jnp.sum(jnp.where(hits, in_slot[None, :], 0), axis=1), 0, top)
    _, plain_order = listed(~is_marked)
    return dict(
        slots=members * capacity,
        in_slot=jnp.clip(in_slot, 0, top),
        marked_order=marked_order.astype(jnp.int32),
        plain_order=plain_order.astype(jnp.int32),
        send_slots=send_slots.astype(jnp.int32),
        take_slots=take_slots.astype(jnp.int32),
    )


def update_step(sending, order, slots, turned, both, first, second, out_shape):
    count = order.shape[0]
    channels = first.shape[0]
    first_tiles = first.shape[1] // TILE
    groups = second.shape[0] // channels
    sems = [pltpu.SemaphoreType.DMA((count,))] * (2 if sending else 3)
    return pl.pallas_call(
        functools.partial(update_kernel, first_tiles, groups, sending),
        grid_spec=pltpu.PrefetchScalarGridSpec(
            num_scalar_prefetch=2,
            grid=(1,),
            in_specs=[whole(turned), whole(both), hbm_spec(), hbm_spec()],
            out_specs=[hbm_spec() for _ in out_shape],
            scratch_shapes=[
                pltpu.VMEM((count, channels, TILE), F32),
                pltpu.VMEM((count, channels, TILE), BF16),
                *sems,
            ],
        ),
        out_shape=out_shape,
        compiler_params=params_of(),
        cost_estimate=cost(1 << 30, 8 << 20),
        name="send" if sending else "keep",
    )(order, slots, *pinned((turned, both, first, second)))


def local(
    inputs,
    cotangent,
    probe,
    dw_kernel,
    dw_bias,
    norm_gain,
    norm_bias,
    w_in,
    b_in,
    w_out,
    b_out,
    layer_scale,
    shuffle_mask,
    source_member,
):
    sections = lax.axis_size("section")
    sec = lax.axis_index("section").astype(jnp.int32).reshape(1)
    micro = inputs.shape[1]
    height, side, channels = inputs.shape[3:]
    width = (side + 15) // 16 * 16
    rows = height * width
    hid = w_in.shape[3]
    first_tiles = hid // TILE
    groups = hid // channels
    vectors = [
        dw_kernel.reshape(TAPS * TAPS, 1, channels),
        dw_bias[0],
        norm_gain[0],
        norm_bias[0],
        b_in[0],
        b_out[0],
        layer_scale[0],
    ]
    first = w_in[0, 0]
    second = w_out[0, 0]
    lowered = [first, second]

    def padded(maps):
        return jnp.pad(maps, ((0, 0), (0, 0), (0, width - side), (0, 0)))

    images = padded(inputs[0, :, 0])
    slopes = padded(cotangent[0, :, 0])
    trial = padded(probe[0])[0]
    entries = [images[item] for item in range(micro)]
    saved = None
    for owner in range(sections):
        leaving = []
        for item in range(micro):
            current, saved, lowered = train_step(
                owner, item, micro, side, sec, entries[item], vectors, lowered, saved
            )
            if owner < sections - 1:
                leaving.append(lax.ppermute(current, "section", [(owner, owner + 1)]))
        entries = leaving
    xs, hats, inverses, ns, mixes, hs, gelu_slopes = saved
    kernel, gain, scale = vectors[0], vectors[2], vectors[6]
    entries = [slopes[item] for item in range(micro)]
    grads = None
    turnings = {(sections - 1, 0): (0, sections - 1), (max(sections - 2, 0), micro - 1): (sections - 1, sections)}
    for owner in reversed(range(sections)):
        leaving = []
        for item in range(micro):
            current, grads = back_step(
                owner,
                item,
                micro,
                side,
                turnings.get((owner, item)),
                sec,
                entries[item],
                (kernel, gain, scale, *lowered),
                (hats, inverses, gelu_slopes, ns, hs),
                grads,
            )
            if owner > 0:
                leaving.append(lax.ppermute(current, "section", [(owner, owner - 1)]))
        entries = leaving
    dys, dns, dspreads, boths, turned = grads

    table = tables(shuffle_mask[0], source_member[0])
    taken = table["marked_order"].shape[0]
    blocks = shuffle_mask.shape[1]
    (outgoing,) = update_step(
        True,
        table["marked_order"],
        table["send_slots"],
        turned,
        boths,
        first,
        second,
        [pltpu.HBM((table["slots"], channels, TILE), BF16)],
    )
    arrived = lax.all_to_all(outgoing, "member", split_axis=0, concat_axis=0, tiled=True)
    own, new_first, new_second = update_step(
        False,
        table["plain_order"],
        table["plain_order"],
        turned,
        boths,
        first,
        second,
        [
            pltpu.HBM((blocks, channels, TILE), BF16),
            pltpu.HBM(first.shape, F32),
            pltpu.HBM(second.shape, F32),
        ],
    )
    vectors = small_step(micro, vectors, (xs, hats, mixes, dys, dns, dspreads, boths))

    new_first, new_second = pl.pallas_call(
        functools.partial(place_kernel, first_tiles, groups),
        grid_spec=pltpu.PrefetchScalarGridSpec(
            num_scalar_prefetch=2,
            grid=(1,),
            in_specs=[hbm_spec()] * 3,
            out_specs=[hbm_spec()] * 2,
            scratch_shapes=[
                pltpu.VMEM((taken, channels, TILE), F32),
                pltpu.VMEM((taken, channels, TILE), BF16),
                pltpu.SemaphoreType.DMA((taken,)),
                pltpu.SemaphoreType.DMA((taken,)),
            ],
        ),
        out_shape=[pltpu.HBM(first.shape, F32), pltpu.HBM(second.shape, F32)],
        input_output_aliases={3: 0, 4: 1},
        compiler_params=params_of(),
        cost_estimate=cost(0, 8 << 20),
        name="place",
    )(table["marked_order"], table["take_slots"], *pinned((arrived, new_first, new_second)))

    early = pl.pallas_call(
        early_kernel,
        grid_spec=pltpu.PrefetchScalarGridSpec(
            num_scalar_prefetch=1,
            grid=(1,),
            in_specs=[whole(trial)] + [whole(item) for item in vectors[:4]],
            out_specs=pl.BlockSpec((rows, channels), lambda i, s: (0, 0)),
            scratch_shapes=[
                pltpu.VMEM((channels // TILE, height + 2 * REACH, width + 2 * EDGE, TILE), F32),
                pltpu.VMEM((rows, channels), F32),
            ],
        ),
        out_shape=shaped((rows, channels), BF16),
        compiler_params=params_of(),
        cost_estimate=cost(1 << 26, 1 << 20),
        name="early",
    )(sec, trial, *vectors[:4])
    received = trial
    features = None
    for tick in range(sections):
        operands = [received, early, *vectors, *pinned((own, arrived))]
        in_specs = [whole(item) for item in operands[:-2]] + [hbm_spec(), hbm_spec()]
        kept = 0 if features is None else 1
        if kept:
            operands += pinned([features])
            in_specs.append(hbm_spec())
        result, features = pl.pallas_call(
            functools.partial(probe_kernel, tick, side, kept),
            grid_spec=pltpu.PrefetchScalarGridSpec(
                num_scalar_prefetch=3,
                grid=(1,),
                in_specs=in_specs,
                out_specs=[whole(trial), hbm_spec()],
                scratch_shapes=[
                    pltpu.VMEM((height, side, channels), BF16),
                    pltpu.VMEM((blocks, channels, TILE), BF16),
                    pltpu.VMEM(
                        (channels // TILE, height + 2 * REACH, width + 2 * EDGE, TILE), F32
                    ),
                    pltpu.VMEM((rows, channels), F32),
                    pltpu.VMEM((rows, channels), F32),
                    pltpu.VMEM((rows, channels), BF16),
                    pltpu.SemaphoreType.DMA((blocks,)),
                    pltpu.SemaphoreType.DMA,
                ],
            ),
            out_shape=[shaped(trial.shape, BF16), pltpu.HBM((height, side, channels), BF16)],
            input_output_aliases={2 + len(operands): 1} if kept else {},
            compiler_params=params_of(),
            cost_estimate=cost(4 * rows * channels * hid, 8 << 20),
            name=f"probe{tick}",
        )(sec, shuffle_mask[0], table["in_slot"], *operands)
        if tick < sections - 1:
            received = lax.ppermute(result, "section", [(tick, tick + 1)])
    return (new_first[None, None], new_second[None, None], features[None, None, None])


def solution(mesh):
    return jax.shard_map(
        local,
        mesh=mesh,
        in_specs=(
            P("member", None, None, None, None, None),
            P("member", None, None, None, None, None),
            P("member", None, None, None, None),
            P("member", "section", None, None, None),
            P("member", "section", None),
            P("member", "section", None),
            P("member", "section", None),
            P("member", "section", None, None),
            P("member", "section", None),
            P("member", "section", None, None),
            P("member", "section", None),
            P("member", "section", None),
            P("section", None),
            P("section", None, None),
        ),
        out_specs=(
            P("member", "section", None, None),
            P("member", "section", None, None),
            P("member", "section", None, None, None, None),
        ),
        check_vma=False,
    )
```

```python
import functools
import math

import jax
import jax.numpy as jnp
from jax import lax
from jax.experimental import pallas as pl
from jax.experimental.pallas import tpu as pltpu
from jax.sharding import PartitionSpec as P

TILE = 128
learning_rate = 0.001
norm_epsilon = 1e-06
F32 = jnp.float32
BF16 = jnp.bfloat16
EDGE = 8
REACH = 3
TAPS = 2 * REACH + 1
VMEM_LIMIT = 36 * 1024 * 1024

TURN = 0.3275911 * math.sqrt(0.5)
TERMS = (1.061405429, -1.453152027, 1.421413741, -0.284496736, 0.254829592)


def normal_below(pre):
    bell = jnp.exp2((pre * pre) * (-0.5 * math.log2(math.e)))
    turn = 1.0 / (1.0 + TURN * jnp.abs(pre))
    poly = jnp.full_like(turn, 0.5 * TERMS[0])
    for term in TERMS[1:]:
        poly = poly * turn + 0.5 * term
    tail = poly * turn * bell
    return jnp.where(pre >= 0.0, 1.0 - tail, tail), bell


def whole(array):
    rank = len(array.shape)
    return pl.BlockSpec(array.shape, lambda *args: (0,) * rank)


def lanes(index):
    return pl.ds(pl.multiple_of(index * TILE, TILE), TILE)


def shaped(shape, dtype):
    return jax.ShapeDtypeStruct(shape, dtype)


def convolve(padded, chunk, kernel_ref, height, width, flip, store):
    totals = [None] * height
    for col in range(TAPS):
        taps = []
        for row in range(TAPS):
            at = row * TAPS + col
            if flip:
                at = TAPS * TAPS - 1 - at
            taps.append(kernel_ref[at, 0:1, lanes(chunk)])
        for line in range(REACH, REACH + height):
            values = padded[chunk, line, pl.ds(EDGE - REACH + col, width), :]
            for row in range(TAPS):
                out = line - row
                if 0 <= out < height:
                    term = values * taps[row]
                    totals[out] = term if totals[out] is None else totals[out] + term
    for out in range(height):
        store(out, totals[out])


def fill_padded(padded, maps):
    height, width, channels = maps.shape
    padded[...] = jnp.zeros(padded.shape, F32)
    for chunk in range(channels // TILE):
        padded[chunk, REACH : REACH + height, EDGE : EDGE + width, :] = maps[
            :, :, chunk * TILE : (chunk + 1) * TILE
        ]


def real_columns(shape, side):
    return lax.broadcasted_iota(jnp.int32, shape, 1) < side


def normalise(spread):
    center = jnp.mean(spread, axis=-1, keepdims=True)
    offset = spread - center
    variance = jnp.mean(offset * offset, axis=-1, keepdims=True)
    inverse = lax.rsqrt(variance + norm_epsilon)
    return offset * inverse, inverse


def conv_norm(vectors, widened, padded, spread, n_ref, hat_store):
    kernel_ref, bias_ref, gain_ref, shift_ref = vectors[:4]
    height, width, channels = widened.shape
    fill_padded(padded, widened)

    def conv_body(chunk, carry):
        bias = bias_ref[0:1, lanes(chunk)]

        def store(out, value):
            spread[out * width : (out + 1) * width, lanes(chunk)] = value + bias

        convolve(padded, chunk, kernel_ref, height, width, False, store)
        return carry

    lax.fori_loop(0, channels // TILE, conv_body, 0)
    hat, inverse = normalise(spread[...])
    n_ref[...] = (hat * gain_ref[...] + shift_ref[...]).astype(BF16)
    hat_store(hat, inverse)


def mix(side, vectors, widened, total, weights, n_ref, hidden_store):
    first_bias_ref, second_bias_ref, scale_ref = vectors[4:]
    height, width, channels = widened.shape
    hid = first_bias_ref.shape[1]
    total[...] = jnp.zeros(total.shape, F32)

    def mix_body(piece, carry):
        first, second = weights(piece)
        at = columns(piece, channels)
        pre = jnp.dot(n_ref[...], first, preferred_element_type=F32) + first_bias_ref[:, at]
        below, bell = normal_below(pre)
        hidden = (pre * below).astype(BF16)
        hidden_store(piece, hidden, pre, below, bell)
        total[...] += jnp.dot(hidden, second, preferred_element_type=F32)
        return carry

    lax.fori_loop(0, hid // channels, mix_body, 0)
    mixed = total[...] + second_bias_ref[...]
    result = widened + (scale_ref[...] * mixed).reshape(height, width, channels)
    result = jnp.where(real_columns(result.shape, side), result, 0.0)
    return result, mixed


def columns(piece, channels):
    return pl.ds(pl.multiple_of(piece * channels, channels), channels)


def train_kernel(owner, slot, side, passing, kept, sec_ref, entry_ref, *refs):
    vectors, (first_ref, second_ref) = refs[:7], refs[7:9]
    refs = refs[9 + kept :]
    y_ref, outs = refs[0], refs[1:8]
    refs = refs[8:]
    leading = kept == 0
    if leading:
        low_first, low_second = refs[:2]
        refs = refs[2:]
        wide_first, wide_second, wide_sems = refs[12:]
    bufs = refs[:7]
    padded, spread, total, sems, piece_sems = refs[7:12]
    x_buf, hat_buf, inverse_buf, n_buf, mixed_buf, h_buf, slope_buf = bufs
    h_out, slope_out = outs[5:]
    channels = x_buf.shape[-1]
    pieces = h_buf.shape[-1] // channels
    active = sec_ref[0] == owner

    def wide_copies(piece):
        at = columns(piece, channels)
        return [
            pltpu.make_async_copy(first_ref.at[:, at], wide_first.at[piece], wide_sems.at[0, piece]),
            pltpu.make_async_copy(second_ref.at[at, :], wide_second.at[piece], wide_sems.at[1, piece]),
        ]

    def weights(piece):
        at = columns(piece, channels)
        if not leading:
            return first_ref[:, at], second_ref[at, :]
        for copy in wide_copies(piece):
            copy.wait()
        first = wide_first[piece].astype(BF16)
        second = wide_second[piece].astype(BF16)
        low_first[:, at] = first
        low_second[at, :] = second
        return first, second

    if leading:
        for piece in range(pieces):
            for copy in wide_copies(piece):
                copy.start()

        @pl.when(jnp.logical_not(active))
        def _():
            def body(piece, carry):
                weights(piece)
                return carry

            lax.fori_loop(0, pieces, body, 0)

    @pl.when(active)
    def _():
        entry = entry_ref[...].astype(F32)
        x_buf[...] = entry_ref[...]

        def piece_copies(piece):
            at = columns(piece, channels)
            return [
                pltpu.make_async_copy(h_buf.at[:, at], h_out.at[slot, :, at], piece_sems.at[0, piece]),
                pltpu.make_async_copy(
                    slope_buf.at[:, at], slope_out.at[slot, :, at], piece_sems.at[1, piece]
                ),
            ]

        def hidden_store(piece, hidden, pre, below, bell):
            at = columns(piece, channels)
            h_buf[:, at] = hidden
            slope_buf[:, at] = (below + pre * (bell * (1.0 / math.sqrt(2.0 * math.pi)))).astype(BF16)
            for copy in piece_copies(piece):
                copy.start()

        copies = [
            pltpu.make_async_copy(buf, out.at[slot], sems.at[index])
            for index, (buf, out) in enumerate(zip(bufs[:5], outs[:5]))
        ]

        def hat_store(hat, inverse):
            hat_buf[...] = hat
            inverse_buf[...] = jnp.broadcast_to(inverse, inverse_buf.shape)
            for copy in copies[:4]:
                copy.start()

        conv_norm(vectors, entry, padded, spread, n_buf, hat_store)
        result, mixed = mix(side, vectors, entry, total, weights, n_buf, hidden_store)
        if passing:
            y_ref[...] = result.astype(BF16)
        mixed_buf[...] = mixed
        copies[4].start()
        for copy in copies:
            copy.wait()
        for piece in range(pieces):
            for copy in piece_copies(piece):
                copy.wait()


def early_kernel(sec_ref, image_ref, *refs):
    vectors = refs[:4]
    n_ref, padded, spread = refs[4:]

    @pl.when(sec_ref[0] == 0)
    def _():
        conv_norm(
            vectors, image_ref[...].astype(F32), padded, spread, n_ref, lambda hat, inverse: None
        )


def probe_kernel(tick, side, kept, sec_ref, marked_ref, slot_ref, received_ref, early_ref, *refs):
    vectors, (own_ref, arrived_ref) = refs[:7], refs[7:9]
    refs = refs[9 + kept :]
    y_ref, feature_ref, feature_buf, tiles_buf, padded, spread, total, n_buf, sems, end_sem = refs

    @pl.when(sec_ref[0] == tick)
    def _():
        channels = y_ref.shape[-1]
        tiles = channels // TILE
        groups = vectors[4].shape[1] // channels

        def start(block):
            taken = marked_ref[block] == 1

            @pl.when(taken)
            def _():
                pltpu.make_async_copy(
                    arrived_ref.at[slot_ref[block]], tiles_buf.at[block], sems.at[block]
                ).start()

            @pl.when(jnp.logical_not(taken))
            def _():
                pltpu.make_async_copy(
                    own_ref.at[block], tiles_buf.at[block], sems.at[block]
                ).start()

        for piece in range(groups):
            for item in range(tiles):
                start(piece * tiles + item)
            for item in range(tiles):
                start(groups * tiles + item * groups + piece)

        entry = received_ref[...].astype(F32)

        def wait(block):
            pltpu.make_async_copy(own_ref.at[block], tiles_buf.at[block], sems.at[block]).wait()

        def weights(piece):
            first = [piece * tiles + item for item in range(tiles)]
            second = [groups * tiles + item * groups + piece for item in range(tiles)]
            for block in first + second:
                wait(block)
            return (
                jnp.concatenate([tiles_buf[block] for block in first], axis=1),
                jnp.concatenate([tiles_buf[block] for block in second], axis=1),
            )

        if tick > 0:
            conv_norm(vectors, entry, padded, spread, n_buf, lambda hat, inverse: None)
        result, mixed = mix(
            side,
            vectors,
            entry,
            total,
            weights,
            early_ref if tick == 0 else n_buf,
            lambda piece, hidden, pre, below, bell: None,
        )
        output = result.astype(BF16)
        y_ref[...] = output
        feature_buf[...] = output[:, :side, :]
        done = pltpu.make_async_copy(feature_buf, feature_ref, end_sem)
        done.start()
        done.wait()


def back_body(owner, which, side, returned_ref, params, saved, dx_ref, outs, bufs):
    kernel_ref, gain_ref, scale_ref, first_ref, second_ref = params
    hat_ref, inverse_ref, slope_ref = saved
    both_out = outs[3]
    dy_buf, dn_buf, dspread_buf, both_buf, hat_buf, inverse_buf, slope_buf = bufs[:7]
    padded, total, conv_out, sems, piece_sems, in_sems = bufs[7:]
    hid = slope_buf.shape[-1]
    height, width, channels = returned_ref.shape
    pieces = hid // channels
    rows = height * width
    ins = [
        pltpu.make_async_copy(
            slope_ref.at[which, :, columns(piece, channels)],
            slope_buf.at[:, columns(piece, channels)],
            in_sems.at[piece],
        )
        for piece in range(pieces)
    ]
    ins.append(pltpu.make_async_copy(hat_ref.at[which], hat_buf, in_sems.at[pieces]))
    ins.append(pltpu.make_async_copy(inverse_ref.at[which], inverse_buf, in_sems.at[pieces + 1]))
    for copy in ins:
        copy.start()
    dy = returned_ref[...].astype(F32)
    flat = dy.reshape(rows, channels)
    dy_buf[...] = flat.astype(BF16)
    mix_at = columns(pieces, channels)
    both_buf[:, mix_at] = (flat * scale_ref[...]).astype(BF16)
    total[...] = jnp.zeros(total.shape, F32)
    contract = (((1,), (1,)), ((), ()))
    copies = [
        pltpu.make_async_copy(buf, out.at[which], sems.at[index])
        for index, (buf, out) in enumerate(zip((dy_buf, dn_buf, dspread_buf), outs))
    ]
    copies[0].start()

    def both_copy(piece):
        at = columns(piece, channels)
        return pltpu.make_async_copy(
            both_buf.at[:, at], both_out.at[which, :, at], piece_sems.at[piece]
        )

    both_copy(pieces).start()

    def body(piece, carry):
        at = columns(piece, channels)
        dh = lax.dot_general(
            both_buf[:, mix_at], second_ref[at, :], contract, preferred_element_type=F32
        )
        pltpu.make_async_copy(
            slope_ref.at[which, :, at], slope_buf.at[:, at], in_sems.at[piece]
        ).wait()
        dpre = (dh * slope_buf[:, at].astype(F32)).astype(BF16)
        both_buf[:, at] = dpre
        both_copy(piece).start()
        total[...] += lax.dot_general(
            dpre, first_ref[:, at], contract, preferred_element_type=F32
        )
        return carry

    lax.fori_loop(0, pieces, body, 0)
    ins[pieces].wait()
    ins[pieces + 1].wait()
    dn = total[...]
    dn_buf[...] = dn.astype(BF16)
    copies[1].start()
    hat = hat_buf[...]
    dhat = dn * gain_ref[...]
    mean = jnp.mean(dhat, axis=-1, keepdims=True)
    along = jnp.mean(dhat * hat, axis=-1, keepdims=True)
    dspread = inverse_buf[:, 0:1] * (dhat - mean - hat * along)
    dspread_buf[...] = dspread
    copies[2].start()
    if owner > 0:
        fill_padded(padded, dspread.reshape(height, width, channels))

        def conv_body(chunk, carry):
            def store(out, value):
                conv_out[out, :, lanes(chunk)] = value

            convolve(padded, chunk, kernel_ref, height, width, True, store)
            return carry

        lax.fori_loop(0, channels // TILE, conv_body, 0)
        dx = dy + conv_out[...]
        dx = jnp.where(real_columns(dx.shape, side), dx, 0.0)
        dx_ref[...] = dx.astype(BF16)
    for copy in copies:
        copy.wait()
    for piece in range(pieces + 1):
        both_copy(piece).wait()


def back_kernel(owner, which, side, turning, kept, sec_ref, returned_ref, *refs):
    params, saved, (n_ref, h_ref) = refs[:5], refs[5:8], refs[8:10]
    refs = refs[10 + kept :]
    dx_ref, outs, turned_ref = refs[0], refs[1:5], refs[5]
    turned_buf, n_buf, h_buf = refs[6:9]
    bufs = refs[9:]
    sems = bufs[10]
    channels = returned_ref.shape[-1]
    pieces = h_buf.shape[-1] // channels

    @pl.when(sec_ref[0] == owner)
    def _():
        back_body(owner, which, side, returned_ref, params, saved, dx_ref, outs, bufs)

    if turning is not None:
        low, high = turning

        @pl.when((sec_ref[0] >= low) & (sec_ref[0] < high))
        def _():
            get_n = pltpu.make_async_copy(n_ref, n_buf, sems.at[0])
            get_h = pltpu.make_async_copy(h_ref, h_buf, sems.at[1])
            get_n.start()
            get_h.start()
            get_h.wait()
            get_n.wait()
            depth = turned_buf.shape[1]

            def turn(piece, carry):
                at = columns(piece, channels)
                turned_buf[at, :] = h_buf[:, :, at].reshape(depth, channels).T
                return carry

            lax.fori_loop(0, pieces, turn, 0)
            turned_buf[columns(pieces, channels), :] = n_buf[...].reshape(depth, channels).T
            put = pltpu.make_async_copy(turned_buf, turned_ref, sems.at[2])
            put.start()
            put.wait()


def small_kernel(micro, *refs):
    (kernel_ref, bias_ref, gain_ref, shift_ref, first_bias_ref, second_bias_ref, scale_ref) = refs[:7]
    x_ref, hat_ref, mixed_ref, dy_ref, dn_ref, dspread_ref, both_ref = refs[7:14]
    outs = refs[14:21]
    padded = refs[21]
    height, width, channels = x_ref.shape[1:]

    def total(values):
        return jnp.sum(values, axis=0, keepdims=True)

    def chunk_body(chunk, carry):
        at = lanes(chunk)
        scale = scale_ref[0:1, at]
        sums = [0.0] * 5
        for item in range(micro):
            dy = dy_ref[item, :, at].astype(F32)
            dn = dn_ref[item, :, at].astype(F32)
            sums[0] += total(dspread_ref[item, :, at])
            sums[1] += total(dn * hat_ref[item, :, at])
            sums[2] += total(dn)
            sums[3] += total(dy)
            sums[4] += total(dy * mixed_ref[item, :, at])
        outs[1][0:1, at] = bias_ref[0:1, at] - learning_rate * sums[0]
        outs[2][0:1, at] = gain_ref[0:1, at] - learning_rate * sums[1]
        outs[3][0:1, at] = shift_ref[0:1, at] - learning_rate * sums[2]
        outs[5][0:1, at] = second_bias_ref[0:1, at] - learning_rate * (scale * sums[3])
        outs[6][0:1, at] = scale - learning_rate * sums[4]
        padded[...] = jnp.zeros(padded.shape, F32)
        for item in range(micro):
            padded[item, REACH : REACH + height, EDGE : EDGE + width, :] = x_ref[
                item, :, :, at
            ].astype(F32)
        for col in range(TAPS):
            for row in range(TAPS):
                acc = None
                for item in range(micro):
                    for out in range(max(0, REACH - row), min(height, height + REACH - row)):
                        term = (
                            padded[item, out + row, pl.ds(EDGE - REACH + col, width), :]
                            * dspread_ref[item, out * width : (out + 1) * width, at]
                        )
                        acc = term if acc is None else acc + term
                tap = row * TAPS + col
                outs[0][tap, 0:1, at] = kernel_ref[tap, 0:1, at] - learning_rate * total(acc)
        return carry

    lax.fori_loop(0, channels // TILE, chunk_body, 0)
    hid = first_bias_ref.shape[1]

    def bias_body(piece, carry):
        at = lanes(piece)
        acc = 0.0
        for item in range(micro):
            acc += total(both_ref[item, :, at].astype(F32))
        outs[4][0:1, at] = first_bias_ref[0:1, at] - learning_rate * acc
        return carry

    lax.fori_loop(0, hid // TILE, bias_body, 0)


def block_views(block, first_tiles, groups, channels, first_ref, second_ref, act):
    @pl.when(block < first_tiles)
    def _():
        act(first_ref.at[:, lanes(block)])

    @pl.when(block >= first_tiles)
    def _():
        place = block - first_tiles
        group = lax.rem(place, groups)
        act(second_ref.at[columns(group, channels), lanes(lax.div(place, groups))])


def fetch_blocks(order_ref, first_tiles, groups, first_ref, second_ref, wide_buf, in_sems):
    def fetch(step, carry):
        def act(view):
            pltpu.make_async_copy(view, wide_buf.at[step], in_sems.at[step]).start()

        channels = wide_buf.shape[1]
        block_views(order_ref[step], first_tiles, groups, channels, first_ref, second_ref, act)
        return carry

    lax.fori_loop(0, wide_buf.shape[0], fetch, 0)


def update_blocks(
    first_tiles,
    groups,
    order_ref,
    turned_ref,
    both_ref,
    first_ref,
    wide_buf,
    slim_buf,
    in_sems,
    out_sems,
    slim_target,
    wide_out,
):
    count, channels, _ = wide_buf.shape
    micro, rows, _ = both_ref.shape
    batch = math.gcd(count, 4)

    def slim_copy(step):
        return pltpu.make_async_copy(slim_buf.at[step], slim_target(step), out_sems.at[step])

    def body(turn, carry):
        steps = [turn * batch + item for item in range(batch)]
        for step in steps:
            pltpu.make_async_copy(
                first_ref.at[:, lanes(0)], wide_buf.at[step], in_sems.at[step]
            ).wait()
        for step in steps:
            block = order_ref[step]
            is_first = block < first_tiles
            place = jnp.maximum(block - first_tiles, 0)
            group = jnp.where(is_first, groups, lax.rem(place, groups))
            column = jnp.where(is_first, block, first_tiles + lax.div(place, groups))
            grad = jnp.dot(
                turned_ref[columns(group, channels), :],
                both_ref[:, :, lanes(column)].reshape(micro * rows, TILE),
                preferred_element_type=F32,
            )
            updated = wide_buf[step] - learning_rate * grad
            slim_buf[step] = updated.astype(BF16)
            if wide_out is not None:
                wide_buf[step] = updated
        for step in steps:
            slim_copy(step).start()
            if wide_out is not None:
                new_first, new_second, wide_sems = wide_out

                def act(view, step=step):
                    pltpu.make_async_copy(wide_buf.at[step], view, wide_sems.at[step]).start()

                block_views(
                    order_ref[step], first_tiles, groups, channels, new_first, new_second, act
                )
        return carry

    lax.fori_loop(0, count // batch, body, 0)

    def drain(step, carry):
        slim_copy(step).wait()
        if wide_out is not None:
            new_first, new_second, wide_sems = wide_out
            pltpu.make_async_copy(
                wide_buf.at[step], new_first.at[:, lanes(0)], wide_sems.at[step]
            ).wait()
        return carry

    lax.fori_loop(0, count, drain, 0)


def keep_kernel(
    first_tiles, groups, order_ref, turned_ref, both_ref, first_ref, second_ref, *refs
):
    own_ref, new_first, new_second, wide_buf, slim_buf, in_sems, out_sems, wide_sems = refs
    fetch_blocks(order_ref, first_tiles, groups, first_ref, second_ref, wide_buf, in_sems)
    update_blocks(
        first_tiles,
        groups,
        order_ref,
        turned_ref,
        both_ref,
        first_ref,
        wide_buf,
        slim_buf,
        in_sems,
        out_sems,
        lambda step: own_ref.at[order_ref[step]],
        (new_first, new_second, wide_sems),
    )


def final_kernel(
    side, first_tiles, groups, sec_ref, order_ref, slot_ref, returned_ref, *refs
):
    params, saved, (first_ref, second_ref) = refs[:5], refs[5:8], refs[8:10]
    old_both, turned_ref = refs[13], refs[14]
    outs, send_ref = refs[15:19], refs[19]
    both_all, turned_buf, wide_buf, slim_buf, slot_sems, out_sems, more_sems = refs[20:27]
    rest = refs[27:]
    micro, rows, _ = both_all.shape
    last = micro - 1
    bufs = rest[:3] + (both_all.at[last],) + rest[3:]
    idle = [
        pltpu.make_async_copy(old_both.at[item], both_all.at[item], more_sems.at[item])
        for item in range(micro)
    ]
    get_turned = pltpu.make_async_copy(turned_ref, turned_buf, more_sems.at[micro])
    for copy in idle[:last]:
        copy.start()
    get_turned.start()
    fetch_blocks(order_ref, first_tiles, groups, first_ref, second_ref, wide_buf, slot_sems)

    @pl.when(sec_ref[0] == 0)
    def _():
        back_body(0, last, side, returned_ref, params, saved, None, outs, bufs)

    @pl.when(sec_ref[0] != 0)
    def _():
        idle[last].start()
        idle[last].wait()

    for copy in idle[:last]:
        copy.wait()
    get_turned.wait()
    update_blocks(
        first_tiles,
        groups,
        order_ref,
        turned_buf,
        both_all,
        first_ref,
        wide_buf,
        slim_buf,
        slot_sems,
        out_sems,
        lambda step: send_ref.at[slot_ref[step]],
        None,
    )


def place_kernel(
    first_tiles, groups, order_ref, slot_ref, arrived_ref, old_first, old_second, new_first, new_second, *refs
):
    wide_buf, slim_buf, in_sems, out_sems = refs
    count, channels, _ = wide_buf.shape

    def fetch(step, carry):
        pltpu.make_async_copy(
            arrived_ref.at[slot_ref[step]], slim_buf.at[step], in_sems.at[step]
        ).start()
        return carry

    lax.fori_loop(0, count, fetch, 0)

    def body(step, carry):
        pltpu.make_async_copy(arrived_ref.at[0], slim_buf.at[step], in_sems.at[step]).wait()
        wide_buf[step] = slim_buf[step].astype(F32)

        def act(view):
            pltpu.make_async_copy(wide_buf.at[step], view, out_sems.at[step]).start()

        block_views(order_ref[step], first_tiles, groups, channels, new_first, new_second, act)
        return carry

    lax.fori_loop(0, count, body, 0)

    def drain(step, carry):
        pltpu.make_async_copy(
            wide_buf.at[step], new_first.at[:, lanes(0)], out_sems.at[step]
        ).wait()
        return carry

    lax.fori_loop(0, count, drain, 0)


def params_of(limit=VMEM_LIMIT):
    return pltpu.CompilerParams(vmem_limit_bytes=limit)


def cost(flops, read):
    return pl.CostEstimate(flops=flops, bytes_accessed=read, transcendentals=0)


def pinned(arrays):
    return [pltpu.with_memory_space_constraint(item, pltpu.HBM) for item in arrays]


def hbm_spec():
    return pl.BlockSpec(memory_space=pltpu.HBM)


def train_step(owner, slot, passing, micro, side, sec, received, vectors, weights, saved):
    height, width, channels = received.shape
    rows = height * width
    hid = vectors[4].shape[1]
    saved_shapes = [
        ((height, width, channels), BF16),
        ((rows, channels), F32),
        ((rows, TILE), F32),
        ((rows, channels), BF16),
        ((rows, channels), F32),
        ((rows, hid), BF16),
        ((rows, hid), BF16),
    ]
    kept = 0 if saved is None else len(saved)
    operands = [received, *vectors, *weights] + ([] if saved is None else pinned(saved))
    if saved is None:
        operands[1:8] = pinned(vectors)
    in_specs = [whole(item) for item in operands[: len(operands) - kept]]
    in_specs += [hbm_spec()] * kept
    more_specs, more_shapes, more_scratch = [], [], []
    if saved is None:
        operands[8:10] = pinned(weights)
        in_specs[8:10] = [hbm_spec()] * 2
        more_specs = [whole(item) for item in weights]
        more_shapes = [shaped(item.shape, BF16) for item in weights]
        wide = pltpu.VMEM((hid // channels, channels, channels), F32)
        more_scratch = [wide, wide, pltpu.SemaphoreType.DMA((2, hid // channels))]
    outs = pl.pallas_call(
        functools.partial(train_kernel, owner, slot, side, passing, kept),
        grid_spec=pltpu.PrefetchScalarGridSpec(
            num_scalar_prefetch=1,
            grid=(1,),
            in_specs=in_specs,
            out_specs=[whole(received) if passing else hbm_spec()]
            + [hbm_spec() for _ in saved_shapes]
            + more_specs,
            scratch_shapes=[pltpu.VMEM(shape, dtype) for shape, dtype in saved_shapes]
            + [
                pltpu.VMEM((channels // TILE, height + 2 * REACH, width + 2 * EDGE, TILE), F32),
                pltpu.VMEM((rows, channels), F32),
                pltpu.VMEM((rows, channels), F32),
                pltpu.SemaphoreType.DMA((5,)),
                pltpu.SemaphoreType.DMA((2, hid // channels)),
            ]
            + more_scratch,
        ),
        out_shape=[shaped(received.shape, BF16)]
        + [pltpu.HBM((micro,) + shape, dtype) for shape, dtype in saved_shapes]
        + more_shapes,
        input_output_aliases={1 + len(operands) - kept + i: 1 + i for i in range(kept)},
        compiler_params=params_of(),
        cost_estimate=cost(4 * rows * channels * hid, 8 << 20),
        name=f"train_{owner}_{slot}",
    )(sec, *operands)
    return outs[0], outs[1:8], outs[8:] if saved is None else weights


def back_scratch(height, width, channels, hid):
    rows = height * width
    return [
        pltpu.VMEM((rows, channels), F32),
        pltpu.VMEM((rows, TILE), F32),
        pltpu.VMEM((rows, hid), BF16),
        pltpu.VMEM((channels // TILE, height + 2 * REACH, width + 2 * EDGE, TILE), F32),
        pltpu.VMEM((rows, channels), F32),
        pltpu.VMEM((height, width, channels), F32),
        pltpu.SemaphoreType.DMA((3,)),
        pltpu.SemaphoreType.DMA((hid // channels + 1,)),
        pltpu.SemaphoreType.DMA((hid // channels + 2,)),
    ]


def final_step(side, table, sec, returned, params, saved, weights, kept_out):
    height, width, channels = returned.shape
    rows = height * width
    first, second = weights
    hid = first.shape[1]
    turned = kept_out[4]
    micro = kept_out[3].shape[0]
    count = table["marked_order"].shape[0]
    operands = [returned, *params, *pinned((*saved, *weights, *kept_out))]
    in_specs = [whole(item) for item in operands[:6]] + [hbm_spec()] * (len(operands) - 6)
    shapes = [(item.shape, item.dtype) for item in kept_out[:4]]
    outs = pl.pallas_call(
        functools.partial(final_kernel, side, hid // TILE, hid // channels),
        grid_spec=pltpu.PrefetchScalarGridSpec(
            num_scalar_prefetch=3,
            grid=(1,),
            in_specs=in_specs,
            out_specs=[hbm_spec()] * 5,
            scratch_shapes=[
                pltpu.VMEM((micro, rows, hid + channels), BF16),
                pltpu.VMEM(turned.shape, BF16),
                pltpu.VMEM((count, channels, TILE), F32),
                pltpu.VMEM((count, channels, TILE), BF16),
                pltpu.SemaphoreType.DMA((count,)),
                pltpu.SemaphoreType.DMA((count,)),
                pltpu.SemaphoreType.DMA((micro + 1,)),
            ]
            + [pltpu.VMEM(shape[1:], dtype) for shape, dtype in shapes[:3]]
            + back_scratch(height, width, channels, hid),
        ),
        out_shape=[pltpu.HBM(shape, dtype) for shape, dtype in shapes]
        + [pltpu.HBM((table["slots"], channels, TILE), BF16)],
        input_output_aliases={3 + 11 + i: i for i in range(4)},
        compiler_params=params_of(),
        cost_estimate=cost(4 * rows * channels * hid, 8 << 20),
        name="final",
    )(sec, table["marked_order"], table["send_slots"], *operands)
    return [*outs[:4], turned], outs[4]


def back_step(owner, which, micro, side, turning, sec, returned, params, saved, kept_out):
    height, width, channels = returned.shape
    rows = height * width
    hid = saved[2].shape[-1]
    shapes = [
        ((rows, channels), BF16),
        ((rows, channels), BF16),
        ((rows, channels), F32),
        ((rows, hid + channels), BF16),
    ]
    turned = ((hid + channels, micro * rows), BF16)
    kept = 0 if kept_out is None else len(kept_out)
    operands = [returned, *params, *pinned(saved)]
    in_specs = [whole(item) for item in operands[:6]]
    in_specs += [hbm_spec()] * (len(saved) + kept)
    base = len(operands)
    operands += [] if kept_out is None else pinned(kept_out)
    outs = pl.pallas_call(
        functools.partial(back_kernel, owner, which, side, turning, kept),
        grid_spec=pltpu.PrefetchScalarGridSpec(
            num_scalar_prefetch=1,
            grid=(1,),
            in_specs=in_specs,
            out_specs=[whole(returned) if owner > 0 else hbm_spec()]
            + [hbm_spec()] * (len(shapes) + 1),
            scratch_shapes=[
                pltpu.VMEM(*turned),
                pltpu.VMEM((micro, rows, channels), BF16),
                pltpu.VMEM((micro, rows, hid), BF16),
            ]
            + [pltpu.VMEM(shape, dtype) for shape, dtype in shapes]
            + back_scratch(height, width, channels, hid),
        ),
        out_shape=[shaped(returned.shape, BF16)]
        + [pltpu.HBM((micro,) + shape, dtype) for shape, dtype in shapes]
        + [pltpu.HBM(*turned)],
        input_output_aliases={1 + base + i: 1 + i for i in range(kept)},
        compiler_params=params_of(),
        cost_estimate=cost(4 * rows * channels * hid, 8 << 20),
        name=f"back_{owner}_{which}",
    )(sec, *operands)
    return outs[0], outs[1:]


def small_step(micro, vectors, grads):
    x = grads[0]
    height, width, channels = x.shape[1:]
    return pl.pallas_call(
        functools.partial(small_kernel, micro),
        grid=(1,),
        in_specs=[whole(item) for item in vectors] + [whole(item) for item in grads],
        out_specs=[whole(item) for item in vectors],
        out_shape=[shaped(item.shape, F32) for item in vectors],
        scratch_shapes=[pltpu.VMEM((micro, height + 2 * REACH, width + 2 * EDGE, TILE), F32)],
        compiler_params=params_of(),
        cost_estimate=cost(1 << 28, 8 << 20),
        name="small",
    )(*vectors, *pinned(grads))


def tables(marked, sources):
    member = lax.axis_index("member")
    members = sources.shape[1]
    blocks = marked.shape[0]
    taken = blocks // 2
    capacity = (taken + members - 2) // (members - 1)
    ids = jnp.arange(blocks, dtype=jnp.int32)
    member_ids = jnp.arange(members, dtype=jnp.int32)
    target = jnp.sum(jnp.where(sources == member, member_ids[None, :], 0), axis=1)
    anchor = jnp.sum(jnp.where(member_ids[None, :] == member, sources, 0), axis=1)
    earlier = ids[:, None] > ids[None, :]
    counted = marked[None, :] == 1
    out_rank = jnp.sum(earlier & (target[:, None] == target[None, :]) & counted, axis=1)
    in_rank = jnp.sum(earlier & (anchor[:, None] == anchor[None, :]) & counted, axis=1)
    out_slot = (target * capacity + out_rank).astype(jnp.int32)
    in_slot = (anchor * capacity + in_rank).astype(jnp.int32)
    steps = jnp.arange(taken, dtype=jnp.int32)
    top = members * capacity - 1

    def listed(flags):
        place = jnp.sum(earlier & flags[None, :], axis=1)
        hits = flags[None, :] & (place[None, :] == steps[:, None])
        return hits, jnp.sum(jnp.where(hits, ids[None, :], 0), axis=1)

    is_marked = marked == 1
    hits, marked_order = listed(is_marked)
    send_slots = jnp.clip(jnp.sum(jnp.where(hits, out_slot[None, :], 0), axis=1), 0, top)
    take_slots = jnp.clip(jnp.sum(jnp.where(hits, in_slot[None, :], 0), axis=1), 0, top)
    _, plain_order = listed(~is_marked)
    return dict(
        slots=members * capacity,
        in_slot=jnp.clip(in_slot, 0, top),
        marked_order=marked_order.astype(jnp.int32),
        plain_order=plain_order.astype(jnp.int32),
        send_slots=send_slots.astype(jnp.int32),
        take_slots=take_slots.astype(jnp.int32),
    )


def keep_step(order, turned, both, first, second, out_shape):
    count = order.shape[0]
    channels = first.shape[0]
    first_tiles = first.shape[1] // TILE
    groups = second.shape[0] // channels
    return pl.pallas_call(
        functools.partial(keep_kernel, first_tiles, groups),
        grid_spec=pltpu.PrefetchScalarGridSpec(
            num_scalar_prefetch=1,
            grid=(1,),
            in_specs=[whole(turned), whole(both), hbm_spec(), hbm_spec()],
            out_specs=[hbm_spec() for _ in out_shape],
            scratch_shapes=[
                pltpu.VMEM((count, channels, TILE), F32),
                pltpu.VMEM((count, channels, TILE), BF16),
            ]
            + [pltpu.SemaphoreType.DMA((count,))] * 3,
        ),
        out_shape=out_shape,
        compiler_params=params_of(),
        cost_estimate=cost(1 << 30, 8 << 20),
        name="keep",
    )(order, *pinned((turned, both, first, second)))


def local(
    inputs,
    cotangent,
    probe,
    dw_kernel,
    dw_bias,
    norm_gain,
    norm_bias,
    w_in,
    b_in,
    w_out,
    b_out,
    layer_scale,
    shuffle_mask,
    source_member,
):
    sections = lax.axis_size("section")
    sec = lax.axis_index("section").astype(jnp.int32).reshape(1)
    micro = inputs.shape[1]
    height, side, channels = inputs.shape[3:]
    width = (side + 15) // 16 * 16
    rows = height * width
    hid = w_in.shape[3]
    first_tiles = hid // TILE
    groups = hid // channels
    vectors = [
        dw_kernel.reshape(TAPS * TAPS, 1, channels),
        dw_bias[0],
        norm_gain[0],
        norm_bias[0],
        b_in[0],
        b_out[0],
        layer_scale[0],
    ]
    first = w_in[0, 0]
    second = w_out[0, 0]
    lowered = [first, second]

    def padded(maps):
        return jnp.pad(maps, ((0, 0), (0, 0), (0, width - side), (0, 0)))

    images = padded(inputs[0, :, 0])
    slopes = padded(cotangent[0, :, 0])
    trial = padded(probe[0])[0]
    entries = [images[item] for item in range(micro)]
    saved = None
    for owner in range(sections):
        leaving = []
        for item in range(micro):
            current, saved, lowered = train_step(
                owner,
                item,
                owner < sections - 1,
                micro,
                side,
                sec,
                entries[item],
                vectors,
                lowered,
                saved,
            )
            if owner < sections - 1:
                leaving.append(lax.ppermute(current, "section", [(owner, owner + 1)]))
        entries = leaving
    xs, hats, inverses, ns, mixes, hs, gelu_slopes = saved
    kernel, gain, scale = vectors[0], vectors[2], vectors[6]
    entries = [slopes[item] for item in range(micro)]
    grads = None
    turnings = {(sections - 1, 0): (0, sections - 1), (max(sections - 2, 0), micro - 1): (sections - 1, sections)}
    table = tables(shuffle_mask[0], source_member[0])
    for owner in reversed(range(sections)):
        leaving = []
        for item in range(micro):
            if owner == 0 and item == micro - 1 and grads is not None:
                grads, outgoing = final_step(
                    side,
                    table,
                    sec,
                    entries[item],
                    (kernel, gain, scale, *lowered),
                    (hats, inverses, gelu_slopes),
                    (first, second),
                    grads,
                )
                continue
            current, grads = back_step(
                owner,
                item,
                micro,
                side,
                turnings.get((owner, item)),
                sec,
                entries[item],
                (kernel, gain, scale, *lowered),
                (hats, inverses, gelu_slopes, ns, hs),
                grads,
            )
            if owner > 0:
                leaving.append(lax.ppermute(current, "section", [(owner, owner - 1)]))
        entries = leaving
    dys, dns, dspreads, boths, turned = grads

    taken = table["marked_order"].shape[0]
    blocks = shuffle_mask.shape[1]
    arrived = lax.all_to_all(outgoing, "member", split_axis=0, concat_axis=0, tiled=True)
    own, new_first, new_second = keep_step(
        table["plain_order"],
        turned,
        boths,
        first,
        second,
        [
            pltpu.HBM((blocks, channels, TILE), BF16),
            pltpu.HBM(first.shape, F32),
            pltpu.HBM(second.shape, F32),
        ],
    )
    vectors = small_step(micro, vectors, (xs, hats, mixes, dys, dns, dspreads, boths))

    new_first, new_second = pl.pallas_call(
        functools.partial(place_kernel, first_tiles, groups),
        grid_spec=pltpu.PrefetchScalarGridSpec(
            num_scalar_prefetch=2,
            grid=(1,),
            in_specs=[hbm_spec()] * 3,
            out_specs=[hbm_spec()] * 2,
            scratch_shapes=[
                pltpu.VMEM((taken, channels, TILE), F32),
                pltpu.VMEM((taken, channels, TILE), BF16),
                pltpu.SemaphoreType.DMA((taken,)),
                pltpu.SemaphoreType.DMA((taken,)),
            ],
        ),
        out_shape=[pltpu.HBM(first.shape, F32), pltpu.HBM(second.shape, F32)],
        input_output_aliases={3: 0, 4: 1},
        compiler_params=params_of(),
        cost_estimate=cost(0, 8 << 20),
        name="place",
    )(table["marked_order"], table["take_slots"], *pinned((arrived, new_first, new_second)))

    early = pl.pallas_call(
        early_kernel,
        grid_spec=pltpu.PrefetchScalarGridSpec(
            num_scalar_prefetch=1,
            grid=(1,),
            in_specs=[whole(trial)] + [whole(item) for item in vectors[:4]],
            out_specs=pl.BlockSpec((rows, channels), lambda i, s: (0, 0)),
            scratch_shapes=[
                pltpu.VMEM((channels // TILE, height + 2 * REACH, width + 2 * EDGE, TILE), F32),
                pltpu.VMEM((rows, channels), F32),
            ],
        ),
        out_shape=shaped((rows, channels), BF16),
        compiler_params=params_of(),
        cost_estimate=cost(1 << 26, 1 << 20),
        name="early",
    )(sec, trial, *vectors[:4])
    received = trial
    features = None
    for tick in range(sections):
        operands = [received, early, *vectors, *pinned((own, arrived))]
        in_specs = [whole(item) for item in operands[:-2]] + [hbm_spec(), hbm_spec()]
        kept = 0 if features is None else 1
        if kept:
            operands += pinned([features])
            in_specs.append(hbm_spec())
        result, features = pl.pallas_call(
            functools.partial(probe_kernel, tick, side, kept),
            grid_spec=pltpu.PrefetchScalarGridSpec(
                num_scalar_prefetch=3,
                grid=(1,),
                in_specs=in_specs,
                out_specs=[whole(trial), hbm_spec()],
                scratch_shapes=[
                    pltpu.VMEM((height, side, channels), BF16),
                    pltpu.VMEM((blocks, channels, TILE), BF16),
                    pltpu.VMEM(
                        (channels // TILE, height + 2 * REACH, width + 2 * EDGE, TILE), F32
                    ),
                    pltpu.VMEM((rows, channels), F32),
                    pltpu.VMEM((rows, channels), F32),
                    pltpu.VMEM((rows, channels), BF16),
                    pltpu.SemaphoreType.DMA((blocks,)),
                    pltpu.SemaphoreType.DMA,
                ],
            ),
            out_shape=[shaped(trial.shape, BF16), pltpu.HBM((height, side, channels), BF16)],
            input_output_aliases={2 + len(operands): 1} if kept else {},
            compiler_params=params_of(),
            cost_estimate=cost(4 * rows * channels * hid, 8 << 20),
            name=f"probe{tick}",
        )(sec, shuffle_mask[0], table["in_slot"], *operands)
        if tick < sections - 1:
            received = lax.ppermute(result, "section", [(tick, tick + 1)])
    return (new_first[None, None], new_second[None, None], features[None, None, None])


def solution(mesh):
    return jax.shard_map(
        local,
        mesh=mesh,
        in_specs=(
            P("member", None, None, None, None, None),
            P("member", None, None, None, None, None),
            P("member", None, None, None, None),
            P("member", "section", None, None, None),
            P("member", "section", None),
            P("member", "section", None),
            P("member", "section", None),
            P("member", "section", None, None),
            P("member", "section", None),
            P("member", "section", None, None),
            P("member", "section", None),
            P("member", "section", None),
            P("section", None),
            P("section", None, None),
        ),
        out_specs=(
            P("member", "section", None, None),
            P("member", "section", None, None),
            P("member", "section", None, None, None, None),
        ),
        check_vma=False,
    )
```

```python
import functools
import math

import jax
import jax.numpy as jnp
from jax import lax
from jax.experimental import pallas as pl
from jax.experimental.pallas import tpu as pltpu
from jax.sharding import PartitionSpec as P

TILE = 128
learning_rate = 0.001
norm_epsilon = 1e-06
F32 = jnp.float32
BF16 = jnp.bfloat16
EDGE = 8
REACH = 3
TAPS = 2 * REACH + 1
VMEM_LIMIT = 36 * 1024 * 1024

TURN = 0.3275911 * math.sqrt(0.5)
TERMS = (1.061405429, -1.453152027, 1.421413741, -0.284496736, 0.254829592)


def normal_below(pre):
    bell = jnp.exp2((pre * pre) * (-0.5 * math.log2(math.e)))
    turn = 1.0 / (1.0 + TURN * jnp.abs(pre))
    poly = jnp.full_like(turn, 0.5 * TERMS[0])
    for term in TERMS[1:]:
        poly = poly * turn + 0.5 * term
    tail = poly * turn * bell
    return jnp.where(pre >= 0.0, 1.0 - tail, tail), bell


def whole(array):
    rank = len(array.shape)
    return pl.BlockSpec(array.shape, lambda *args: (0,) * rank)


def lanes(index):
    return pl.ds(pl.multiple_of(index * TILE, TILE), TILE)


def shaped(shape, dtype):
    return jax.ShapeDtypeStruct(shape, dtype)


def convolve(padded, chunk, kernel_ref, height, width, flip, store):
    totals = [None] * height
    for col in range(TAPS):
        taps = []
        for row in range(TAPS):
            at = row * TAPS + col
            if flip:
                at = TAPS * TAPS - 1 - at
            taps.append(kernel_ref[at, 0:1, lanes(chunk)])
        for line in range(REACH, REACH + height):
            values = padded[chunk, line, pl.ds(EDGE - REACH + col, width), :]
            for row in range(TAPS):
                out = line - row
                if 0 <= out < height:
                    term = values * taps[row]
                    totals[out] = term if totals[out] is None else totals[out] + term
    for out in range(height):
        store(out, totals[out])


def fill_padded(padded, maps):
    height, width, channels = maps.shape
    padded[...] = jnp.zeros(padded.shape, F32)
    for chunk in range(channels // TILE):
        padded[chunk, REACH : REACH + height, EDGE : EDGE + width, :] = maps[
            :, :, chunk * TILE : (chunk + 1) * TILE
        ]


def real_columns(shape, side):
    return lax.broadcasted_iota(jnp.int32, shape, 1) < side


def normalise(spread):
    center = jnp.mean(spread, axis=-1, keepdims=True)
    offset = spread - center
    variance = jnp.mean(offset * offset, axis=-1, keepdims=True)
    inverse = lax.rsqrt(variance + norm_epsilon)
    return offset * inverse, inverse


def conv_norm(vectors, widened, padded, spread, n_ref, hat_store):
    kernel_ref, bias_ref, gain_ref, shift_ref = vectors[:4]
    height, width, channels = widened.shape
    fill_padded(padded, widened)

    def conv_body(chunk, carry):
        bias = bias_ref[0:1, lanes(chunk)]

        def store(out, value):
            spread[out * width : (out + 1) * width, lanes(chunk)] = value + bias

        convolve(padded, chunk, kernel_ref, height, width, False, store)
        return carry

    lax.fori_loop(0, channels // TILE, conv_body, 0)
    hat, inverse = normalise(spread[...])
    n_ref[...] = (hat * gain_ref[...] + shift_ref[...]).astype(BF16)
    hat_store(hat, inverse)


def mix(side, vectors, widened, total, weights, n_ref, hidden_store):
    first_bias_ref, second_bias_ref, scale_ref = vectors[4:]
    height, width, channels = widened.shape
    hid = first_bias_ref.shape[1]
    total[...] = jnp.zeros(total.shape, F32)

    def mix_body(piece, carry):
        first, second = weights(piece)
        at = columns(piece, channels)
        pre = jnp.dot(n_ref[...], first, preferred_element_type=F32) + first_bias_ref[:, at]
        below, bell = normal_below(pre)
        hidden = (pre * below).astype(BF16)
        hidden_store(piece, hidden, pre, below, bell)
        total[...] += jnp.dot(hidden, second, preferred_element_type=F32)
        return carry

    lax.fori_loop(0, hid // channels, mix_body, 0)
    mixed = total[...] + second_bias_ref[...]
    result = widened + (scale_ref[...] * mixed).reshape(height, width, channels)
    result = jnp.where(real_columns(result.shape, side), result, 0.0)
    return result, mixed


def columns(piece, channels):
    return pl.ds(pl.multiple_of(piece * channels, channels), channels)


def train_kernel(owner, slot, side, passing, kept, sec_ref, entry_ref, *refs):
    vectors, (first_ref, second_ref) = refs[:7], refs[7:9]
    refs = refs[9 + kept :]
    y_ref, outs = refs[0], refs[1:8]
    refs = refs[8:]
    leading = kept == 0
    if leading:
        low_first, low_second = refs[:2]
        refs = refs[2:]
        wide_first, wide_second, wide_sems = refs[12:]
    bufs = refs[:7]
    padded, spread, total, sems, piece_sems = refs[7:12]
    x_buf, hat_buf, inverse_buf, n_buf, mixed_buf, h_buf, slope_buf = bufs
    h_out, slope_out = outs[5:]
    channels = x_buf.shape[-1]
    pieces = h_buf.shape[-1] // channels
    active = sec_ref[0] == owner

    def wide_copies(piece):
        at = columns(piece, channels)
        return [
            pltpu.make_async_copy(first_ref.at[:, at], wide_first.at[piece], wide_sems.at[0, piece]),
            pltpu.make_async_copy(second_ref.at[at, :], wide_second.at[piece], wide_sems.at[1, piece]),
        ]

    def weights(piece):
        at = columns(piece, channels)
        if not leading:
            return first_ref[:, at], second_ref[at, :]
        for copy in wide_copies(piece):
            copy.wait()
        first = wide_first[piece].astype(BF16)
        second = wide_second[piece].astype(BF16)
        low_first[:, at] = first
        low_second[at, :] = second
        return first, second

    if leading:
        for piece in range(pieces):
            for copy in wide_copies(piece):
                copy.start()

        @pl.when(jnp.logical_not(active))
        def _():
            def body(piece, carry):
                weights(piece)
                return carry

            lax.fori_loop(0, pieces, body, 0)

    @pl.when(active)
    def _():
        entry = entry_ref[...].astype(F32)
        x_buf[...] = entry_ref[...]

        def piece_copies(piece):
            at = columns(piece, channels)
            return [
                pltpu.make_async_copy(h_buf.at[:, at], h_out.at[slot, :, at], piece_sems.at[0, piece]),
                pltpu.make_async_copy(
                    slope_buf.at[:, at], slope_out.at[slot, :, at], piece_sems.at[1, piece]
                ),
            ]

        def hidden_store(piece, hidden, pre, below, bell):
            at = columns(piece, channels)
            h_buf[:, at] = hidden
            slope_buf[:, at] = (below + pre * (bell * (1.0 / math.sqrt(2.0 * math.pi)))).astype(BF16)
            for copy in piece_copies(piece):
                copy.start()

        copies = [
            pltpu.make_async_copy(buf, out.at[slot], sems.at[index])
            for index, (buf, out) in enumerate(zip(bufs[:5], outs[:5]))
        ]

        def hat_store(hat, inverse):
            hat_buf[...] = hat
            inverse_buf[...] = jnp.broadcast_to(inverse, inverse_buf.shape)
            for copy in copies[:4]:
                copy.start()

        conv_norm(vectors, entry, padded, spread, n_buf, hat_store)
        result, mixed = mix(side, vectors, entry, total, weights, n_buf, hidden_store)
        if passing:
            y_ref[...] = result.astype(BF16)
        mixed_buf[...] = mixed
        copies[4].start()
        for copy in copies:
            copy.wait()
        for piece in range(pieces):
            for copy in piece_copies(piece):
                copy.wait()


def early_kernel(sec_ref, image_ref, *refs):
    vectors = refs[:4]
    n_ref, padded, spread = refs[4:]

    @pl.when(sec_ref[0] == 0)
    def _():
        conv_norm(
            vectors, image_ref[...].astype(F32), padded, spread, n_ref, lambda hat, inverse: None
        )


def probe_kernel(
    tick, side, partners, kept, sec_ref, marked_ref, slot_ref, plain_ref, received_ref, early_ref, *refs
):
    vectors, own_ref, arrived = refs[:7], refs[7], refs[8 : 8 + partners]
    refs = refs[8 + partners + kept :]
    y_ref, feature_ref, feature_buf, tiles_buf, padded, spread, total, n_buf, sems, end_sem = refs

    @pl.when(sec_ref[0] == tick)
    def _():
        channels = y_ref.shape[-1]
        tiles = channels // TILE
        groups = vectors[4].shape[1] // channels

        def fetch(step, carry):
            block = marked_ref[step]

            def act(view):
                pltpu.make_async_copy(view, tiles_buf.at[block], sems.at[block]).start()

            with_slot(arrived, slot_ref[step], act)
            plain = plain_ref[step]
            pltpu.make_async_copy(own_ref.at[plain], tiles_buf.at[plain], sems.at[plain]).start()
            return carry

        lax.fori_loop(0, tiles_buf.shape[0] // 2, fetch, 0)
        entry = received_ref[...].astype(F32)

        def wait(block):
            pltpu.make_async_copy(own_ref.at[block], tiles_buf.at[block], sems.at[block]).wait()

        def weights(piece):
            first = [piece * tiles + item for item in range(tiles)]
            second = [groups * tiles + item * groups + piece for item in range(tiles)]
            for block in first + second:
                wait(block)
            return (
                jnp.concatenate([tiles_buf[block] for block in first], axis=1),
                jnp.concatenate([tiles_buf[block] for block in second], axis=1),
            )

        if tick > 0:
            conv_norm(vectors, entry, padded, spread, n_buf, lambda hat, inverse: None)
        result, mixed = mix(
            side,
            vectors,
            entry,
            total,
            weights,
            early_ref if tick == 0 else n_buf,
            lambda piece, hidden, pre, below, bell: None,
        )
        output = result.astype(BF16)
        y_ref[...] = output
        feature_buf[...] = output[:, :side, :]
        done = pltpu.make_async_copy(feature_buf, feature_ref, end_sem)
        done.start()
        done.wait()


def back_body(owner, which, side, returned_ref, params, saved, dx_ref, outs, bufs, then=None):
    kernel_ref, gain_ref, scale_ref, first_ref, second_ref = params
    hat_ref, inverse_ref, slope_ref = saved
    both_out = outs[3]
    dy_buf, dn_buf, dspread_buf, both_buf, hat_buf, inverse_buf, slope_buf = bufs[:7]
    padded, total, conv_out, sems, piece_sems, in_sems = bufs[7:]
    hid = slope_buf.shape[-1]
    height, width, channels = returned_ref.shape
    pieces = hid // channels
    rows = height * width
    ins = [
        pltpu.make_async_copy(
            slope_ref.at[which, :, columns(piece, channels)],
            slope_buf.at[:, columns(piece, channels)],
            in_sems.at[piece],
        )
        for piece in range(pieces)
    ]
    ins.append(pltpu.make_async_copy(hat_ref.at[which], hat_buf, in_sems.at[pieces]))
    ins.append(pltpu.make_async_copy(inverse_ref.at[which], inverse_buf, in_sems.at[pieces + 1]))
    for copy in ins:
        copy.start()
    if then is not None:
        then()
    dy = returned_ref[...].astype(F32)
    flat = dy.reshape(rows, channels)
    dy_buf[...] = flat.astype(BF16)
    mix_at = columns(pieces, channels)
    both_buf[:, mix_at] = (flat * scale_ref[...]).astype(BF16)
    total[...] = jnp.zeros(total.shape, F32)
    contract = (((1,), (1,)), ((), ()))
    copies = [
        pltpu.make_async_copy(buf, out.at[which], sems.at[index])
        for index, (buf, out) in enumerate(zip((dy_buf, dn_buf, dspread_buf), outs))
    ]
    copies[0].start()

    def both_copy(piece):
        at = columns(piece, channels)
        return pltpu.make_async_copy(
            both_buf.at[:, at], both_out.at[which, :, at], piece_sems.at[piece]
        )

    both_copy(pieces).start()

    def body(piece, carry):
        at = columns(piece, channels)
        dh = lax.dot_general(
            both_buf[:, mix_at], second_ref[at, :], contract, preferred_element_type=F32
        )
        pltpu.make_async_copy(
            slope_ref.at[which, :, at], slope_buf.at[:, at], in_sems.at[piece]
        ).wait()
        dpre = (dh * slope_buf[:, at].astype(F32)).astype(BF16)
        both_buf[:, at] = dpre
        both_copy(piece).start()
        total[...] += lax.dot_general(
            dpre, first_ref[:, at], contract, preferred_element_type=F32
        )
        return carry

    lax.fori_loop(0, pieces, body, 0)
    ins[pieces].wait()
    ins[pieces + 1].wait()
    dn = total[...]
    dn_buf[...] = dn.astype(BF16)
    copies[1].start()
    hat = hat_buf[...]
    dhat = dn * gain_ref[...]
    mean = jnp.mean(dhat, axis=-1, keepdims=True)
    along = jnp.mean(dhat * hat, axis=-1, keepdims=True)
    dspread = inverse_buf[:, 0:1] * (dhat - mean - hat * along)
    dspread_buf[...] = dspread
    copies[2].start()
    if owner > 0:
        fill_padded(padded, dspread.reshape(height, width, channels))

        def conv_body(chunk, carry):
            def store(out, value):
                conv_out[out, :, lanes(chunk)] = value

            convolve(padded, chunk, kernel_ref, height, width, True, store)
            return carry

        lax.fori_loop(0, channels // TILE, conv_body, 0)
        dx = dy + conv_out[...]
        dx = jnp.where(real_columns(dx.shape, side), dx, 0.0)
        dx_ref[...] = dx.astype(BF16)
    for copy in copies:
        copy.wait()
    for piece in range(pieces + 1):
        both_copy(piece).wait()


def back_kernel(owner, which, side, turning, kept, sec_ref, returned_ref, *refs):
    params, saved, (n_ref, h_ref) = refs[:5], refs[5:8], refs[8:10]
    refs = refs[10 + kept :]
    dx_ref, outs, turned_ref = refs[0], refs[1:5], refs[5]
    turned_buf, n_buf, h_buf = refs[6:9]
    bufs = refs[9:]
    sems = bufs[10]
    channels = returned_ref.shape[-1]
    pieces = h_buf.shape[-1] // channels

    @pl.when(sec_ref[0] == owner)
    def _():
        back_body(owner, which, side, returned_ref, params, saved, dx_ref, outs, bufs)

    if turning is not None:
        low, high = turning

        @pl.when((sec_ref[0] >= low) & (sec_ref[0] < high))
        def _():
            get_n = pltpu.make_async_copy(n_ref, n_buf, sems.at[0])
            get_h = pltpu.make_async_copy(h_ref, h_buf, sems.at[1])
            get_n.start()
            get_h.start()
            get_h.wait()
            get_n.wait()
            depth = turned_buf.shape[1]

            def turn(piece, carry):
                at = columns(piece, channels)
                turned_buf[at, :] = h_buf[:, :, at].reshape(depth, channels).T
                return carry

            lax.fori_loop(0, pieces, turn, 0)
            turned_buf[columns(pieces, channels), :] = n_buf[...].reshape(depth, channels).T
            put = pltpu.make_async_copy(turned_buf, turned_ref, sems.at[2])
            put.start()
            put.wait()


def small_kernel(micro, *refs):
    (kernel_ref, bias_ref, gain_ref, shift_ref, first_bias_ref, second_bias_ref, scale_ref) = refs[:7]
    x_ref, hat_ref, mixed_ref, dy_ref, dn_ref, dspread_ref, both_ref = refs[7:14]
    outs = refs[14:21]
    padded = refs[21]
    height, width, channels = x_ref.shape[1:]

    def total(values):
        return jnp.sum(values, axis=0, keepdims=True)

    def chunk_body(chunk, carry):
        at = lanes(chunk)
        scale = scale_ref[0:1, at]
        sums = [0.0] * 5
        for item in range(micro):
            dy = dy_ref[item, :, at].astype(F32)
            dn = dn_ref[item, :, at].astype(F32)
            sums[0] += total(dspread_ref[item, :, at])
            sums[1] += total(dn * hat_ref[item, :, at])
            sums[2] += total(dn)
            sums[3] += total(dy)
            sums[4] += total(dy * mixed_ref[item, :, at])
        outs[1][0:1, at] = bias_ref[0:1, at] - learning_rate * sums[0]
        outs[2][0:1, at] = gain_ref[0:1, at] - learning_rate * sums[1]
        outs[3][0:1, at] = shift_ref[0:1, at] - learning_rate * sums[2]
        outs[5][0:1, at] = second_bias_ref[0:1, at] - learning_rate * (scale * sums[3])
        outs[6][0:1, at] = scale - learning_rate * sums[4]
        padded[...] = jnp.zeros(padded.shape, F32)
        for item in range(micro):
            padded[item, REACH : REACH + height, EDGE : EDGE + width, :] = x_ref[
                item, :, :, at
            ].astype(F32)
        for col in range(TAPS):
            for row in range(TAPS):
                acc = None
                for item in range(micro):
                    for out in range(max(0, REACH - row), min(height, height + REACH - row)):
                        term = (
                            padded[item, out + row, pl.ds(EDGE - REACH + col, width), :]
                            * dspread_ref[item, out * width : (out + 1) * width, at]
                        )
                        acc = term if acc is None else acc + term
                tap = row * TAPS + col
                outs[0][tap, 0:1, at] = kernel_ref[tap, 0:1, at] - learning_rate * total(acc)
        return carry

    lax.fori_loop(0, channels // TILE, chunk_body, 0)
    hid = first_bias_ref.shape[1]

    def bias_body(piece, carry):
        at = lanes(piece)
        acc = 0.0
        for item in range(micro):
            acc += total(both_ref[item, :, at].astype(F32))
        outs[4][0:1, at] = first_bias_ref[0:1, at] - learning_rate * acc
        return carry

    lax.fori_loop(0, hid // TILE, bias_body, 0)


def block_views(block, first_tiles, groups, channels, first_ref, second_ref, act):
    @pl.when(block < first_tiles)
    def _():
        act(first_ref.at[:, lanes(block)])

    @pl.when(block >= first_tiles)
    def _():
        place = block - first_tiles
        group = lax.rem(place, groups)
        act(second_ref.at[columns(group, channels), lanes(lax.div(place, groups))])


def with_slot(arrays, slot, act):
    capacity = arrays[0].shape[0]
    for index, array in enumerate(arrays):

        @pl.when(lax.div(slot, capacity) == index)
        def _():
            act(array.at[lax.rem(slot, capacity)])


def fetch_blocks(order_ref, first_tiles, groups, first_ref, second_ref, wide_buf, in_sems):
    def fetch(step, carry):
        def act(view):
            pltpu.make_async_copy(view, wide_buf.at[step], in_sems.at[step]).start()

        channels = wide_buf.shape[1]
        block_views(order_ref[step], first_tiles, groups, channels, first_ref, second_ref, act)
        return carry

    lax.fori_loop(0, wide_buf.shape[0], fetch, 0)


def update_blocks(
    first_tiles,
    groups,
    order_ref,
    turned_ref,
    both_ref,
    first_ref,
    wide_buf,
    slim_buf,
    in_sems,
    out_sems,
    slim_target,
    slim_like,
    wide_out,
):
    count, channels, _ = wide_buf.shape
    micro, rows, _ = both_ref.shape
    batch = math.gcd(count, 4)

    def slim_copy(step, target):
        return pltpu.make_async_copy(slim_buf.at[step], target, out_sems.at[step])

    def body(turn, carry):
        steps = [turn * batch + item for item in range(batch)]
        for step in steps:
            pltpu.make_async_copy(
                first_ref.at[:, lanes(0)], wide_buf.at[step], in_sems.at[step]
            ).wait()
        for step in steps:
            block = order_ref[step]
            is_first = block < first_tiles
            place = jnp.maximum(block - first_tiles, 0)
            group = jnp.where(is_first, groups, lax.rem(place, groups))
            column = jnp.where(is_first, block, first_tiles + lax.div(place, groups))
            grad = jnp.dot(
                turned_ref[columns(group, channels), :],
                both_ref[:, :, lanes(column)].reshape(micro * rows, TILE),
                preferred_element_type=F32,
            )
            updated = wide_buf[step] - learning_rate * grad
            slim_buf[step] = updated.astype(BF16)
            if wide_out is not None:
                wide_buf[step] = updated
        for step in steps:
            slim_target(step, lambda target, step=step: slim_copy(step, target).start())
            if wide_out is not None:
                new_first, new_second, wide_sems = wide_out

                def act(view, step=step):
                    pltpu.make_async_copy(wide_buf.at[step], view, wide_sems.at[step]).start()

                block_views(
                    order_ref[step], first_tiles, groups, channels, new_first, new_second, act
                )
        return carry

    lax.fori_loop(0, count // batch, body, 0)

    def drain(step, carry):
        slim_copy(step, slim_like).wait()
        if wide_out is not None:
            new_first, new_second, wide_sems = wide_out
            pltpu.make_async_copy(
                wide_buf.at[step], new_first.at[:, lanes(0)], wide_sems.at[step]
            ).wait()
        return carry

    lax.fori_loop(0, count, drain, 0)


def keep_kernel(
    first_tiles, groups, order_ref, turned_ref, both_ref, first_ref, second_ref, *refs
):
    own_ref, new_first, new_second, wide_buf, slim_buf, in_sems, out_sems, wide_sems = refs
    fetch_blocks(order_ref, first_tiles, groups, first_ref, second_ref, wide_buf, in_sems)
    update_blocks(
        first_tiles,
        groups,
        order_ref,
        turned_ref,
        both_ref,
        first_ref,
        wide_buf,
        slim_buf,
        in_sems,
        out_sems,
        lambda step, act: act(own_ref.at[order_ref[step]]),
        own_ref.at[0],
        (new_first, new_second, wide_sems),
    )


def final_kernel(
    side, first_tiles, groups, partners, sec_ref, order_ref, slot_ref, returned_ref, *refs
):
    params, saved, (first_ref, second_ref) = refs[:5], refs[5:8], refs[8:10]
    old_both, turned_ref = refs[13], refs[14]
    outs, send_refs = refs[15:19], refs[19 : 19 + partners]
    refs = refs[19 + partners :]
    both_all, turned_buf, wide_buf, slim_buf, slot_sems, out_sems, more_sems = refs[:7]
    rest = refs[7:]
    micro, rows, _ = both_all.shape
    last = micro - 1
    bufs = rest[:3] + (both_all.at[last],) + rest[3:]
    idle = [
        pltpu.make_async_copy(old_both.at[item], both_all.at[item], more_sems.at[item])
        for item in range(micro)
    ]
    get_turned = pltpu.make_async_copy(turned_ref, turned_buf, more_sems.at[micro])

    def prefetch():
        for copy in idle[:last]:
            copy.start()
        get_turned.start()
        fetch_blocks(order_ref, first_tiles, groups, first_ref, second_ref, wide_buf, slot_sems)

    @pl.when(sec_ref[0] == 0)
    def _():
        back_body(0, last, side, returned_ref, params, saved, None, outs, bufs, prefetch)

    @pl.when(sec_ref[0] != 0)
    def _():
        idle[last].start()
        prefetch()
        idle[last].wait()

    for copy in idle[:last]:
        copy.wait()
    get_turned.wait()
    update_blocks(
        first_tiles,
        groups,
        order_ref,
        turned_buf,
        both_all,
        first_ref,
        wide_buf,
        slim_buf,
        slot_sems,
        out_sems,
        lambda step, act: with_slot(send_refs, slot_ref[step], act),
        send_refs[0].at[0],
        None,
    )


def place_kernel(
    first_tiles, groups, partners, order_ref, slot_ref, *refs
):
    arrived, (new_first, new_second) = refs[:partners], refs[partners + 2 : partners + 4]
    wide_buf, slim_buf, in_sems, out_sems = refs[partners + 4 :]
    count, channels, _ = wide_buf.shape

    def fetch(step, carry):
        def act(view):
            pltpu.make_async_copy(view, slim_buf.at[step], in_sems.at[step]).start()

        with_slot(arrived, slot_ref[step], act)
        return carry

    lax.fori_loop(0, count, fetch, 0)

    def body(step, carry):
        pltpu.make_async_copy(arrived[0].at[0], slim_buf.at[step], in_sems.at[step]).wait()
        wide_buf[step] = slim_buf[step].astype(F32)

        def act(view):
            pltpu.make_async_copy(wide_buf.at[step], view, out_sems.at[step]).start()

        block_views(order_ref[step], first_tiles, groups, channels, new_first, new_second, act)
        return carry

    lax.fori_loop(0, count, body, 0)

    def drain(step, carry):
        pltpu.make_async_copy(
            wide_buf.at[step], new_first.at[:, lanes(0)], out_sems.at[step]
        ).wait()
        return carry

    lax.fori_loop(0, count, drain, 0)


def params_of(limit=VMEM_LIMIT):
    return pltpu.CompilerParams(vmem_limit_bytes=limit)


def cost(flops, read):
    return pl.CostEstimate(flops=flops, bytes_accessed=read, transcendentals=0)


def pinned(arrays):
    return [pltpu.with_memory_space_constraint(item, pltpu.HBM) for item in arrays]


def hbm_spec():
    return pl.BlockSpec(memory_space=pltpu.HBM)


def train_step(owner, slot, passing, micro, side, sec, received, vectors, weights, saved):
    height, width, channels = received.shape
    rows = height * width
    hid = vectors[4].shape[1]
    saved_shapes = [
        ((height, width, channels), BF16),
        ((rows, channels), F32),
        ((rows, TILE), F32),
        ((rows, channels), BF16),
        ((rows, channels), F32),
        ((rows, hid), BF16),
        ((rows, hid), BF16),
    ]
    kept = 0 if saved is None else len(saved)
    operands = [received, *vectors, *weights] + ([] if saved is None else pinned(saved))
    if saved is None:
        operands[1:8] = pinned(vectors)
    in_specs = [whole(item) for item in operands[: len(operands) - kept]]
    in_specs += [hbm_spec()] * kept
    more_specs, more_shapes, more_scratch = [], [], []
    if saved is None:
        operands[8:10] = pinned(weights)
        in_specs[8:10] = [hbm_spec()] * 2
        more_specs = [whole(item) for item in weights]
        more_shapes = [shaped(item.shape, BF16) for item in weights]
        wide = pltpu.VMEM((hid // channels, channels, channels), F32)
        more_scratch = [wide, wide, pltpu.SemaphoreType.DMA((2, hid // channels))]
    outs = pl.pallas_call(
        functools.partial(train_kernel, owner, slot, side, passing, kept),
        grid_spec=pltpu.PrefetchScalarGridSpec(
            num_scalar_prefetch=1,
            grid=(1,),
            in_specs=in_specs,
            out_specs=[whole(received) if passing else hbm_spec()]
            + [hbm_spec() for _ in saved_shapes]
            + more_specs,
            scratch_shapes=[pltpu.VMEM(shape, dtype) for shape, dtype in saved_shapes]
            + [
                pltpu.VMEM((channels // TILE, height + 2 * REACH, width + 2 * EDGE, TILE), F32),
                pltpu.VMEM((rows, channels), F32),
                pltpu.VMEM((rows, channels), F32),
                pltpu.SemaphoreType.DMA((5,)),
                pltpu.SemaphoreType.DMA((2, hid // channels)),
            ]
            + more_scratch,
        ),
        out_shape=[shaped(received.shape, BF16)]
        + [pltpu.HBM((micro,) + shape, dtype) for shape, dtype in saved_shapes]
        + more_shapes,
        input_output_aliases={1 + len(operands) - kept + i: 1 + i for i in range(kept)},
        compiler_params=params_of(),
        cost_estimate=cost(4 * rows * channels * hid, 8 << 20),
        name=f"train_{owner}_{slot}",
    )(sec, *operands)
    return outs[0], outs[1:8], outs[8:] if saved is None else weights


def back_scratch(height, width, channels, hid):
    rows = height * width
    return [
        pltpu.VMEM((rows, channels), F32),
        pltpu.VMEM((rows, TILE), F32),
        pltpu.VMEM((rows, hid), BF16),
        pltpu.VMEM((channels // TILE, height + 2 * REACH, width + 2 * EDGE, TILE), F32),
        pltpu.VMEM((rows, channels), F32),
        pltpu.VMEM((height, width, channels), F32),
        pltpu.SemaphoreType.DMA((3,)),
        pltpu.SemaphoreType.DMA((hid // channels + 1,)),
        pltpu.SemaphoreType.DMA((hid // channels + 2,)),
    ]


def final_step(side, table, sec, returned, params, saved, weights, kept_out):
    height, width, channels = returned.shape
    rows = height * width
    first, second = weights
    hid = first.shape[1]
    turned = kept_out[4]
    micro = kept_out[3].shape[0]
    count = table["marked_order"].shape[0]
    operands = [returned, *params, *pinned((*saved, *weights, *kept_out))]
    in_specs = [whole(item) for item in operands[:6]] + [hbm_spec()] * (len(operands) - 6)
    shapes = [(item.shape, item.dtype) for item in kept_out[:4]]
    outs = pl.pallas_call(
        functools.partial(final_kernel, side, hid // TILE, hid // channels, table["partners"]),
        grid_spec=pltpu.PrefetchScalarGridSpec(
            num_scalar_prefetch=3,
            grid=(1,),
            in_specs=in_specs,
            out_specs=[hbm_spec()] * (4 + table["partners"]),
            scratch_shapes=[
                pltpu.VMEM((micro, rows, hid + channels), BF16),
                pltpu.VMEM(turned.shape, BF16),
                pltpu.VMEM((count, channels, TILE), F32),
                pltpu.VMEM((count, channels, TILE), BF16),
                pltpu.SemaphoreType.DMA((count,)),
                pltpu.SemaphoreType.DMA((count,)),
                pltpu.SemaphoreType.DMA((micro + 1,)),
            ]
            + [pltpu.VMEM(shape[1:], dtype) for shape, dtype in shapes[:3]]
            + back_scratch(height, width, channels, hid),
        ),
        out_shape=[pltpu.HBM(shape, dtype) for shape, dtype in shapes]
        + [pltpu.HBM((table["capacity"], channels, TILE), BF16)] * table["partners"],
        input_output_aliases={3 + 11 + i: i for i in range(4)},
        compiler_params=params_of(),
        cost_estimate=cost(4 * rows * channels * hid, 8 << 20),
        name="final",
    )(sec, table["marked_order"], table["send_slots"], *operands)
    return [*outs[:4], turned], outs[4:]


def back_step(owner, which, micro, side, turning, sec, returned, params, saved, kept_out):
    height, width, channels = returned.shape
    rows = height * width
    hid = saved[2].shape[-1]
    shapes = [
        ((rows, channels), BF16),
        ((rows, channels), BF16),
        ((rows, channels), F32),
        ((rows, hid + channels), BF16),
    ]
    turned = ((hid + channels, micro * rows), BF16)
    kept = 0 if kept_out is None else len(kept_out)
    operands = [returned, *params, *pinned(saved)]
    in_specs = [whole(item) for item in operands[:6]]
    in_specs += [hbm_spec()] * (len(saved) + kept)
    base = len(operands)
    operands += [] if kept_out is None else pinned(kept_out)
    outs = pl.pallas_call(
        functools.partial(back_kernel, owner, which, side, turning, kept),
        grid_spec=pltpu.PrefetchScalarGridSpec(
            num_scalar_prefetch=1,
            grid=(1,),
            in_specs=in_specs,
            out_specs=[whole(returned) if owner > 0 else hbm_spec()]
            + [hbm_spec()] * (len(shapes) + 1),
            scratch_shapes=[
                pltpu.VMEM(*turned),
                pltpu.VMEM((micro, rows, channels), BF16),
                pltpu.VMEM((micro, rows, hid), BF16),
            ]
            + [pltpu.VMEM(shape, dtype) for shape, dtype in shapes]
            + back_scratch(height, width, channels, hid),
        ),
        out_shape=[shaped(returned.shape, BF16)]
        + [pltpu.HBM((micro,) + shape, dtype) for shape, dtype in shapes]
        + [pltpu.HBM(*turned)],
        input_output_aliases={1 + base + i: 1 + i for i in range(kept)},
        compiler_params=params_of(),
        cost_estimate=cost(4 * rows * channels * hid, 8 << 20),
        name=f"back_{owner}_{which}",
    )(sec, *operands)
    return outs[0], outs[1:]


def small_step(micro, vectors, grads):
    x = grads[0]
    height, width, channels = x.shape[1:]
    return pl.pallas_call(
        functools.partial(small_kernel, micro),
        grid=(1,),
        in_specs=[whole(item) for item in vectors] + [whole(item) for item in grads],
        out_specs=[whole(item) for item in vectors],
        out_shape=[shaped(item.shape, F32) for item in vectors],
        scratch_shapes=[pltpu.VMEM((micro, height + 2 * REACH, width + 2 * EDGE, TILE), F32)],
        compiler_params=params_of(),
        cost_estimate=cost(1 << 28, 8 << 20),
        name="small",
    )(*vectors, *pinned(grads))


def distance(source, target, members):
    if members & (members - 1) == 0:
        return jnp.bitwise_xor(source, target)
    return (target - source) % members


def reached(source, step, members):
    return source ^ step if members & (members - 1) == 0 else (source + step) % members


def tables(marked, sources):
    member = lax.axis_index("member")
    members = sources.shape[1]
    blocks = marked.shape[0]
    taken = blocks // 2
    capacity = (taken + members - 2) // (members - 1)
    ids = jnp.arange(blocks, dtype=jnp.int32)
    member_ids = jnp.arange(members, dtype=jnp.int32)
    target = jnp.sum(jnp.where(sources == member, member_ids[None, :], 0), axis=1)
    anchor = jnp.sum(jnp.where(member_ids[None, :] == member, sources, 0), axis=1)
    earlier = ids[:, None] > ids[None, :]
    counted = marked[None, :] == 1
    out_rank = jnp.sum(earlier & (target[:, None] == target[None, :]) & counted, axis=1)
    in_rank = jnp.sum(earlier & (anchor[:, None] == anchor[None, :]) & counted, axis=1)
    out_slot = (distance(member, target, members) - 1) * capacity + out_rank
    in_slot = (distance(anchor, member, members) - 1) * capacity + in_rank
    steps = jnp.arange(taken, dtype=jnp.int32)
    top = (members - 1) * capacity - 1

    def listed(flags):
        place = jnp.sum(earlier & flags[None, :], axis=1)
        hits = flags[None, :] & (place[None, :] == steps[:, None])
        return hits, jnp.sum(jnp.where(hits, ids[None, :], 0), axis=1)

    is_marked = marked == 1
    hits, marked_order = listed(is_marked)
    send_slots = jnp.clip(jnp.sum(jnp.where(hits, out_slot[None, :], 0), axis=1), 0, top)
    take_slots = jnp.clip(jnp.sum(jnp.where(hits, in_slot[None, :], 0), axis=1), 0, top)
    _, plain_order = listed(~is_marked)
    return dict(
        partners=members - 1,
        capacity=capacity,
        marked_order=marked_order.astype(jnp.int32),
        plain_order=plain_order.astype(jnp.int32),
        send_slots=send_slots.astype(jnp.int32),
        take_slots=take_slots.astype(jnp.int32),
    )


def keep_step(order, turned, both, first, second, out_shape):
    count = order.shape[0]
    channels = first.shape[0]
    first_tiles = first.shape[1] // TILE
    groups = second.shape[0] // channels
    return pl.pallas_call(
        functools.partial(keep_kernel, first_tiles, groups),
        grid_spec=pltpu.PrefetchScalarGridSpec(
            num_scalar_prefetch=1,
            grid=(1,),
            in_specs=[whole(turned), whole(both), hbm_spec(), hbm_spec()],
            out_specs=[hbm_spec() for _ in out_shape],
            scratch_shapes=[
                pltpu.VMEM((count, channels, TILE), F32),
                pltpu.VMEM((count, channels, TILE), BF16),
            ]
            + [pltpu.SemaphoreType.DMA((count,))] * 3,
        ),
        out_shape=out_shape,
        compiler_params=params_of(),
        cost_estimate=cost(1 << 30, 8 << 20),
        name="keep",
    )(order, *pinned((turned, both, first, second)))


def local(
    inputs,
    cotangent,
    probe,
    dw_kernel,
    dw_bias,
    norm_gain,
    norm_bias,
    w_in,
    b_in,
    w_out,
    b_out,
    layer_scale,
    shuffle_mask,
    source_member,
):
    sections = lax.axis_size("section")
    sec = lax.axis_index("section").astype(jnp.int32).reshape(1)
    micro = inputs.shape[1]
    height, side, channels = inputs.shape[3:]
    width = (side + 15) // 16 * 16
    rows = height * width
    hid = w_in.shape[3]
    first_tiles = hid // TILE
    groups = hid // channels
    vectors = [
        dw_kernel.reshape(TAPS * TAPS, 1, channels),
        dw_bias[0],
        norm_gain[0],
        norm_bias[0],
        b_in[0],
        b_out[0],
        layer_scale[0],
    ]
    first = w_in[0, 0]
    second = w_out[0, 0]
    lowered = [first, second]

    def padded(maps):
        return jnp.pad(maps, ((0, 0), (0, 0), (0, width - side), (0, 0)))

    images = padded(inputs[0, :, 0])
    slopes = padded(cotangent[0, :, 0])
    trial = padded(probe[0])[0]
    entries = [images[item] for item in range(micro)]
    saved = None
    for owner in range(sections):
        leaving = []
        for item in range(micro):
            current, saved, lowered = train_step(
                owner,
                item,
                owner < sections - 1,
                micro,
                side,
                sec,
                entries[item],
                vectors,
                lowered,
                saved,
            )
            if owner < sections - 1:
                leaving.append(lax.ppermute(current, "section", [(owner, owner + 1)]))
        entries = leaving
    xs, hats, inverses, ns, mixes, hs, gelu_slopes = saved
    kernel, gain, scale = vectors[0], vectors[2], vectors[6]
    entries = [slopes[item] for item in range(micro)]
    grads = None
    turnings = {(sections - 1, 0): (0, sections - 1), (max(sections - 2, 0), micro - 1): (sections - 1, sections)}
    table = tables(shuffle_mask[0], source_member[0])
    for owner in reversed(range(sections)):
        leaving = []
        for item in range(micro):
            if owner == 0 and item == micro - 1 and grads is not None:
                grads, outgoing = final_step(
                    side,
                    table,
                    sec,
                    entries[item],
                    (kernel, gain, scale, *lowered),
                    (hats, inverses, gelu_slopes),
                    (first, second),
                    grads,
                )
                continue
            current, grads = back_step(
                owner,
                item,
                micro,
                side,
                turnings.get((owner, item)),
                sec,
                entries[item],
                (kernel, gain, scale, *lowered),
                (hats, inverses, gelu_slopes, ns, hs),
                grads,
            )
            if owner > 0:
                leaving.append(lax.ppermute(current, "section", [(owner, owner - 1)]))
        entries = leaving
    dys, dns, dspreads, boths, turned = grads

    taken = table["marked_order"].shape[0]
    blocks = shuffle_mask.shape[1]
    members = lax.axis_size("member")
    arrived = [
        lax.ppermute(
            outgoing[step], "member", [(m, reached(m, step + 1, members)) for m in range(members)]
        )
        for step in reversed(range(members - 1))
    ][::-1]
    own, new_first, new_second = keep_step(
        table["plain_order"],
        turned,
        boths,
        first,
        second,
        [
            pltpu.HBM((blocks, channels, TILE), BF16),
            pltpu.HBM(first.shape, F32),
            pltpu.HBM(second.shape, F32),
        ],
    )
    vectors = small_step(micro, vectors, (xs, hats, mixes, dys, dns, dspreads, boths))

    new_first, new_second = pl.pallas_call(
        functools.partial(place_kernel, first_tiles, groups, members - 1),
        grid_spec=pltpu.PrefetchScalarGridSpec(
            num_scalar_prefetch=2,
            grid=(1,),
            in_specs=[hbm_spec()] * (members + 1),
            out_specs=[hbm_spec()] * 2,
            scratch_shapes=[
                pltpu.VMEM((taken, channels, TILE), F32),
                pltpu.VMEM((taken, channels, TILE), BF16),
                pltpu.SemaphoreType.DMA((taken,)),
                pltpu.SemaphoreType.DMA((taken,)),
            ],
        ),
        out_shape=[pltpu.HBM(first.shape, F32), pltpu.HBM(second.shape, F32)],
        input_output_aliases={members + 1: 0, members + 2: 1},
        compiler_params=params_of(),
        cost_estimate=cost(0, 8 << 20),
        name="place",
    )(table["marked_order"], table["take_slots"], *pinned((*arrived, new_first, new_second)))

    early = pl.pallas_call(
        early_kernel,
        grid_spec=pltpu.PrefetchScalarGridSpec(
            num_scalar_prefetch=1,
            grid=(1,),
            in_specs=[whole(trial)] + [whole(item) for item in vectors[:4]],
            out_specs=pl.BlockSpec((rows, channels), lambda i, s: (0, 0)),
            scratch_shapes=[
                pltpu.VMEM((channels // TILE, height + 2 * REACH, width + 2 * EDGE, TILE), F32),
                pltpu.VMEM((rows, channels), F32),
            ],
        ),
        out_shape=shaped((rows, channels), BF16),
        compiler_params=params_of(),
        cost_estimate=cost(1 << 26, 1 << 20),
        name="early",
    )(sec, trial, *vectors[:4])
    received = trial
    features = None
    for tick in range(sections):
        operands = [received, early, *vectors, *pinned((own, *arrived))]
        in_specs = [whole(item) for item in operands[:9]] + [hbm_spec()] * members
        kept = 0 if features is None else 1
        if kept:
            operands += pinned([features])
            in_specs.append(hbm_spec())
        result, features = pl.pallas_call(
            functools.partial(probe_kernel, tick, side, members - 1, kept),
            grid_spec=pltpu.PrefetchScalarGridSpec(
                num_scalar_prefetch=4,
                grid=(1,),
                in_specs=in_specs,
                out_specs=[whole(trial), hbm_spec()],
                scratch_shapes=[
                    pltpu.VMEM((height, side, channels), BF16),
                    pltpu.VMEM((blocks, channels, TILE), BF16),
                    pltpu.VMEM(
                        (channels // TILE, height + 2 * REACH, width + 2 * EDGE, TILE), F32
                    ),
                    pltpu.VMEM((rows, channels), F32),
                    pltpu.VMEM((rows, channels), F32),
                    pltpu.VMEM((rows, channels), BF16),
                    pltpu.SemaphoreType.DMA((blocks,)),
                    pltpu.SemaphoreType.DMA,
                ],
            ),
            out_shape=[shaped(trial.shape, BF16), pltpu.HBM((height, side, channels), BF16)],
            input_output_aliases={3 + len(operands): 1} if kept else {},
            compiler_params=params_of(),
            cost_estimate=cost(4 * rows * channels * hid, 8 << 20),
            name=f"probe{tick}",
        )(sec, table["marked_order"], table["take_slots"], table["plain_order"], *operands)
        if tick < sections - 1:
            received = lax.ppermute(result, "section", [(tick, tick + 1)])
    return (new_first[None, None], new_second[None, None], features[None, None, None])


def solution(mesh):
    return jax.shard_map(
        local,
        mesh=mesh,
        in_specs=(
            P("member", None, None, None, None, None),
            P("member", None, None, None, None, None),
            P("member", None, None, None, None),
            P("member", "section", None, None, None),
            P("member", "section", None),
            P("member", "section", None),
            P("member", "section", None),
            P("member", "section", None, None),
            P("member", "section", None),
            P("member", "section", None, None),
            P("member", "section", None),
            P("member", "section", None),
            P("section", None),
            P("section", None, None),
        ),
        out_specs=(
            P("member", "section", None, None),
            P("member", "section", None, None),
            P("member", "section", None, None, None, None),
        ),
        check_vma=False,
    )
```

```python
import functools
import math

import jax
import jax.numpy as jnp
from jax import lax
from jax.experimental import pallas as pl
from jax.experimental.pallas import tpu as pltpu
from jax.sharding import PartitionSpec as P

TILE = 128
learning_rate = 0.001
norm_epsilon = 1e-06
F32 = jnp.float32
BF16 = jnp.bfloat16
EDGE = 8
REACH = 3
TAPS = 2 * REACH + 1
VMEM_LIMIT = 36 * 1024 * 1024

TURN = 0.3275911 * math.sqrt(0.5)
TERMS = (1.061405429, -1.453152027, 1.421413741, -0.284496736, 0.254829592)


def normal_below(pre):
    bell = jnp.exp2((pre * pre) * (-0.5 * math.log2(math.e)))
    turn = 1.0 / (1.0 + TURN * jnp.abs(pre))
    poly = jnp.full_like(turn, 0.5 * TERMS[0])
    for term in TERMS[1:]:
        poly = poly * turn + 0.5 * term
    tail = poly * turn * bell
    return jnp.where(pre >= 0.0, 1.0 - tail, tail), bell


def whole(array):
    rank = len(array.shape)
    return pl.BlockSpec(array.shape, lambda *args: (0,) * rank)


def lanes(index):
    return pl.ds(pl.multiple_of(index * TILE, TILE), TILE)


def shaped(shape, dtype):
    return jax.ShapeDtypeStruct(shape, dtype)


def convolve(padded, chunk, kernel_ref, height, width, flip, store):
    totals = [None] * height
    for col in range(TAPS):
        taps = []
        for row in range(TAPS):
            at = row * TAPS + col
            if flip:
                at = TAPS * TAPS - 1 - at
            taps.append(kernel_ref[at, 0:1, lanes(chunk)])
        for line in range(REACH, REACH + height):
            values = padded[chunk, line, pl.ds(EDGE - REACH + col, width), :]
            for row in range(TAPS):
                out = line - row
                if 0 <= out < height:
                    term = values * taps[row]
                    totals[out] = term if totals[out] is None else totals[out] + term
    for out in range(height):
        store(out, totals[out])


def fill_padded(padded, maps):
    height, width, channels = maps.shape
    padded[...] = jnp.zeros(padded.shape, F32)
    for chunk in range(channels // TILE):
        padded[chunk, REACH : REACH + height, EDGE : EDGE + width, :] = maps[
            :, :, chunk * TILE : (chunk + 1) * TILE
        ]


def real_columns(shape, side):
    return lax.broadcasted_iota(jnp.int32, shape, 1) < side


def normalise(spread):
    center = jnp.mean(spread, axis=-1, keepdims=True)
    offset = spread - center
    variance = jnp.mean(offset * offset, axis=-1, keepdims=True)
    inverse = lax.rsqrt(variance + norm_epsilon)
    return offset * inverse, inverse


def conv_norm(vectors, widened, padded, spread, n_ref, hat_store):
    kernel_ref, bias_ref, gain_ref, shift_ref = vectors[:4]
    height, width, channels = widened.shape
    fill_padded(padded, widened)

    def conv_body(chunk, carry):
        bias = bias_ref[0:1, lanes(chunk)]

        def store(out, value):
            spread[out * width : (out + 1) * width, lanes(chunk)] = value + bias

        convolve(padded, chunk, kernel_ref, height, width, False, store)
        return carry

    lax.fori_loop(0, channels // TILE, conv_body, 0)
    hat, inverse = normalise(spread[...])
    n_ref[...] = (hat * gain_ref[...] + shift_ref[...]).astype(BF16)
    hat_store(hat, inverse)


def mix(side, vectors, widened, total, weights, n_ref, hidden_store):
    first_bias_ref, second_bias_ref, scale_ref = vectors[4:]
    height, width, channels = widened.shape
    hid = first_bias_ref.shape[1]
    total[...] = jnp.zeros(total.shape, F32)

    def mix_body(piece, carry):
        first, second = weights(piece)
        at = columns(piece, channels)
        pre = jnp.dot(n_ref[...], first, preferred_element_type=F32) + first_bias_ref[:, at]
        below, bell = normal_below(pre)
        hidden = (pre * below).astype(BF16)
        hidden_store(piece, hidden, pre, below, bell)
        total[...] += jnp.dot(hidden, second, preferred_element_type=F32)
        return carry

    lax.fori_loop(0, hid // channels, mix_body, 0)
    mixed = total[...] + second_bias_ref[...]
    result = widened + (scale_ref[...] * mixed).reshape(height, width, channels)
    result = jnp.where(real_columns(result.shape, side), result, 0.0)
    return result, mixed


def columns(piece, channels):
    return pl.ds(pl.multiple_of(piece * channels, channels), channels)


def train_kernel(owner, slot, side, passing, kept, sec_ref, entry_ref, *refs):
    vectors, (first_ref, second_ref) = refs[:7], refs[7:9]
    refs = refs[9 + kept :]
    y_ref, outs = refs[0], refs[1:8]
    refs = refs[8:]
    leading = kept == 0
    if leading:
        low_first, low_second = refs[:2]
        refs = refs[2:]
        wide_first, wide_second, wide_sems = refs[12:]
    bufs = refs[:7]
    padded, spread, total, sems, piece_sems = refs[7:12]
    x_buf, hat_buf, inverse_buf, n_buf, mixed_buf, h_buf, slope_buf = bufs
    h_out, slope_out = outs[5:]
    channels = x_buf.shape[-1]
    pieces = h_buf.shape[-1] // channels
    active = sec_ref[0] == owner

    def wide_copies(piece):
        at = columns(piece, channels)
        return [
            pltpu.make_async_copy(first_ref.at[:, at], wide_first.at[piece], wide_sems.at[0, piece]),
            pltpu.make_async_copy(second_ref.at[at, :], wide_second.at[piece], wide_sems.at[1, piece]),
        ]

    def weights(piece):
        at = columns(piece, channels)
        if not leading:
            return first_ref[:, at], second_ref[at, :]
        for copy in wide_copies(piece):
            copy.wait()
        first = wide_first[piece].astype(BF16)
        second = wide_second[piece].astype(BF16)
        low_first[:, at] = first
        low_second[at, :] = second
        return first, second

    if leading:
        for piece in range(pieces):
            for copy in wide_copies(piece):
                copy.start()

        @pl.when(jnp.logical_not(active))
        def _():
            def body(piece, carry):
                weights(piece)
                return carry

            lax.fori_loop(0, pieces, body, 0)

    @pl.when(active)
    def _():
        entry = entry_ref[...].astype(F32)
        x_buf[...] = entry_ref[...]

        def piece_copies(piece):
            at = columns(piece, channels)
            return [
                pltpu.make_async_copy(h_buf.at[:, at], h_out.at[slot, :, at], piece_sems.at[0, piece]),
                pltpu.make_async_copy(
                    slope_buf.at[:, at], slope_out.at[slot, :, at], piece_sems.at[1, piece]
                ),
            ]

        def hidden_store(piece, hidden, pre, below, bell):
            at = columns(piece, channels)
            h_buf[:, at] = hidden
            slope_buf[:, at] = (below + pre * (bell * (1.0 / math.sqrt(2.0 * math.pi)))).astype(BF16)
            for copy in piece_copies(piece):
                copy.start()

        copies = [
            pltpu.make_async_copy(buf, out.at[slot], sems.at[index])
            for index, (buf, out) in enumerate(zip(bufs[:5], outs[:5]))
        ]

        def hat_store(hat, inverse):
            hat_buf[...] = hat
            inverse_buf[...] = jnp.broadcast_to(inverse, inverse_buf.shape)
            for copy in copies[:4]:
                copy.start()

        conv_norm(vectors, entry, padded, spread, n_buf, hat_store)
        result, mixed = mix(side, vectors, entry, total, weights, n_buf, hidden_store)
        if passing:
            y_ref[...] = result.astype(BF16)
        mixed_buf[...] = mixed
        copies[4].start()
        for copy in copies:
            copy.wait()
        for piece in range(pieces):
            for copy in piece_copies(piece):
                copy.wait()


def early_kernel(sec_ref, image_ref, *refs):
    vectors = refs[:4]
    n_ref, padded, spread = refs[4:]

    @pl.when(sec_ref[0] == 0)
    def _():
        conv_norm(
            vectors, image_ref[...].astype(F32), padded, spread, n_ref, lambda hat, inverse: None
        )


def probe_kernel(
    tick, side, passing, partners, kept, sec_ref, marked_ref, slot_ref, plain_ref, received_ref, early_ref, *refs
):
    vectors, own_ref, arrived = refs[:7], refs[7], refs[8 : 8 + partners]
    refs = refs[8 + partners + kept :]
    y_ref, feature_ref, feature_buf, tiles_buf, padded, spread, total, n_buf, sems, end_sem = refs

    @pl.when(sec_ref[0] == tick)
    def _():
        channels = y_ref.shape[-1]
        tiles = channels // TILE
        groups = vectors[4].shape[1] // channels

        def fetch(step, carry):
            block = marked_ref[step]

            def act(view):
                pltpu.make_async_copy(view, tiles_buf.at[block], sems.at[block]).start()

            with_slot(arrived, slot_ref[step], act)
            plain = plain_ref[step]
            pltpu.make_async_copy(own_ref.at[plain], tiles_buf.at[plain], sems.at[plain]).start()
            return carry

        lax.fori_loop(0, tiles_buf.shape[0] // 2, fetch, 0)
        entry = received_ref[...].astype(F32)

        def wait(block):
            pltpu.make_async_copy(own_ref.at[block], tiles_buf.at[block], sems.at[block]).wait()

        def weights(piece):
            first = [piece * tiles + item for item in range(tiles)]
            second = [groups * tiles + item * groups + piece for item in range(tiles)]
            for block in first + second:
                wait(block)
            return (
                jnp.concatenate([tiles_buf[block] for block in first], axis=1),
                jnp.concatenate([tiles_buf[block] for block in second], axis=1),
            )

        if tick > 0:
            conv_norm(vectors, entry, padded, spread, n_buf, lambda hat, inverse: None)
        result, mixed = mix(
            side,
            vectors,
            entry,
            total,
            weights,
            early_ref if tick == 0 else n_buf,
            lambda piece, hidden, pre, below, bell: None,
        )
        output = result.astype(BF16)
        if passing:
            y_ref[...] = output
        feature_buf[...] = output[:, :side, :]
        done = pltpu.make_async_copy(feature_buf, feature_ref, end_sem)
        done.start()
        done.wait()


def back_body(owner, which, side, returned_ref, params, saved, dx_ref, outs, bufs, then=None):
    kernel_ref, gain_ref, scale_ref, first_ref, second_ref = params
    hat_ref, inverse_ref, slope_ref = saved
    both_out = outs[3]
    dy_buf, dn_buf, dspread_buf, both_buf, hat_buf, inverse_buf, slope_buf = bufs[:7]
    padded, total, conv_out, sems, piece_sems, in_sems = bufs[7:]
    hid = slope_buf.shape[-1]
    height, width, channels = returned_ref.shape
    pieces = hid // channels
    rows = height * width
    ins = [
        pltpu.make_async_copy(
            slope_ref.at[which, :, columns(piece, channels)],
            slope_buf.at[:, columns(piece, channels)],
            in_sems.at[piece],
        )
        for piece in range(pieces)
    ]
    ins.append(pltpu.make_async_copy(hat_ref.at[which], hat_buf, in_sems.at[pieces]))
    ins.append(pltpu.make_async_copy(inverse_ref.at[which], inverse_buf, in_sems.at[pieces + 1]))
    for copy in ins:
        copy.start()
    if then is not None:
        then()
    dy = returned_ref[...].astype(F32)
    flat = dy.reshape(rows, channels)
    dy_buf[...] = flat.astype(BF16)
    mix_at = columns(pieces, channels)
    both_buf[:, mix_at] = (flat * scale_ref[...]).astype(BF16)
    total[...] = jnp.zeros(total.shape, F32)
    contract = (((1,), (1,)), ((), ()))
    copies = [
        pltpu.make_async_copy(buf, out.at[which], sems.at[index])
        for index, (buf, out) in enumerate(zip((dy_buf, dn_buf, dspread_buf), outs))
    ]
    copies[0].start()

    def both_copy(piece):
        at = columns(piece, channels)
        return pltpu.make_async_copy(
            both_buf.at[:, at], both_out.at[which, :, at], piece_sems.at[piece]
        )

    both_copy(pieces).start()

    def body(piece, carry):
        at = columns(piece, channels)
        dh = lax.dot_general(
            both_buf[:, mix_at], second_ref[at, :], contract, preferred_element_type=F32
        )
        pltpu.make_async_copy(
            slope_ref.at[which, :, at], slope_buf.at[:, at], in_sems.at[piece]
        ).wait()
        dpre = (dh * slope_buf[:, at].astype(F32)).astype(BF16)
        both_buf[:, at] = dpre
        both_copy(piece).start()
        total[...] += lax.dot_general(
            dpre, first_ref[:, at], contract, preferred_element_type=F32
        )
        return carry

    lax.fori_loop(0, pieces, body, 0)
    ins[pieces].wait()
    ins[pieces + 1].wait()
    dn = total[...]
    dn_buf[...] = dn.astype(BF16)
    copies[1].start()
    hat = hat_buf[...]
    dhat = dn * gain_ref[...]
    mean = jnp.mean(dhat, axis=-1, keepdims=True)
    along = jnp.mean(dhat * hat, axis=-1, keepdims=True)
    dspread = inverse_buf[:, 0:1] * (dhat - mean - hat * along)
    dspread_buf[...] = dspread
    copies[2].start()
    if owner > 0:
        fill_padded(padded, dspread.reshape(height, width, channels))

        def conv_body(chunk, carry):
            def store(out, value):
                conv_out[out, :, lanes(chunk)] = value

            convolve(padded, chunk, kernel_ref, height, width, True, store)
            return carry

        lax.fori_loop(0, channels // TILE, conv_body, 0)
        dx = dy + conv_out[...]
        dx = jnp.where(real_columns(dx.shape, side), dx, 0.0)
        dx_ref[...] = dx.astype(BF16)
    for copy in copies:
        copy.wait()
    for piece in range(pieces + 1):
        both_copy(piece).wait()


def back_kernel(owner, which, side, turning, kept, sec_ref, returned_ref, *refs):
    params, saved, (n_ref, h_ref) = refs[:5], refs[5:8], refs[8:10]
    refs = refs[10 + kept :]
    dx_ref, outs, turned_ref = refs[0], refs[1:5], refs[5]
    turned_buf, n_buf, h_buf = refs[6:9]
    bufs = refs[9:]
    sems = bufs[10]
    channels = returned_ref.shape[-1]
    pieces = h_buf.shape[-1] // channels

    @pl.when(sec_ref[0] == owner)
    def _():
        back_body(owner, which, side, returned_ref, params, saved, dx_ref, outs, bufs)

    if turning is not None:
        low, high = turning

        @pl.when((sec_ref[0] >= low) & (sec_ref[0] < high))
        def _():
            get_n = pltpu.make_async_copy(n_ref, n_buf, sems.at[0])
            get_h = pltpu.make_async_copy(h_ref, h_buf, sems.at[1])
            get_n.start()
            get_h.start()
            get_h.wait()
            get_n.wait()
            depth = turned_buf.shape[1]

            def turn(piece, carry):
                at = columns(piece, channels)
                turned_buf[at, :] = h_buf[:, :, at].reshape(depth, channels).T
                return carry

            lax.fori_loop(0, pieces, turn, 0)
            turned_buf[columns(pieces, channels), :] = n_buf[...].reshape(depth, channels).T
            put = pltpu.make_async_copy(turned_buf, turned_ref, sems.at[2])
            put.start()
            put.wait()


def small_kernel(micro, *refs):
    (kernel_ref, bias_ref, gain_ref, shift_ref, first_bias_ref, second_bias_ref, scale_ref) = refs[:7]
    x_ref, hat_ref, mixed_ref, dy_ref, dn_ref, dspread_ref, both_ref = refs[7:14]
    outs = refs[14:21]
    padded = refs[21]
    height, width, channels = x_ref.shape[1:]

    def total(values):
        return jnp.sum(values, axis=0, keepdims=True)

    def chunk_body(chunk, carry):
        at = lanes(chunk)
        scale = scale_ref[0:1, at]
        sums = [0.0] * 5
        for item in range(micro):
            dy = dy_ref[item, :, at].astype(F32)
            dn = dn_ref[item, :, at].astype(F32)
            sums[0] += total(dspread_ref[item, :, at])
            sums[1] += total(dn * hat_ref[item, :, at])
            sums[2] += total(dn)
            sums[3] += total(dy)
            sums[4] += total(dy * mixed_ref[item, :, at])
        outs[1][0:1, at] = bias_ref[0:1, at] - learning_rate * sums[0]
        outs[2][0:1, at] = gain_ref[0:1, at] - learning_rate * sums[1]
        outs[3][0:1, at] = shift_ref[0:1, at] - learning_rate * sums[2]
        outs[5][0:1, at] = second_bias_ref[0:1, at] - learning_rate * (scale * sums[3])
        outs[6][0:1, at] = scale - learning_rate * sums[4]
        padded[...] = jnp.zeros(padded.shape, F32)
        for item in range(micro):
            padded[item, REACH : REACH + height, EDGE : EDGE + width, :] = x_ref[
                item, :, :, at
            ].astype(F32)
        for col in range(TAPS):
            for row in range(TAPS):
                acc = None
                for item in range(micro):
                    for out in range(max(0, REACH - row), min(height, height + REACH - row)):
                        term = (
                            padded[item, out + row, pl.ds(EDGE - REACH + col, width), :]
                            * dspread_ref[item, out * width : (out + 1) * width, at]
                        )
                        acc = term if acc is None else acc + term
                tap = row * TAPS + col
                outs[0][tap, 0:1, at] = kernel_ref[tap, 0:1, at] - learning_rate * total(acc)
        return carry

    lax.fori_loop(0, channels // TILE, chunk_body, 0)
    hid = first_bias_ref.shape[1]

    def bias_body(piece, carry):
        at = lanes(piece)
        acc = 0.0
        for item in range(micro):
            acc += total(both_ref[item, :, at].astype(F32))
        outs[4][0:1, at] = first_bias_ref[0:1, at] - learning_rate * acc
        return carry

    lax.fori_loop(0, hid // TILE, bias_body, 0)


def block_views(block, first_tiles, groups, channels, first_ref, second_ref, act):
    @pl.when(block < first_tiles)
    def _():
        act(first_ref.at[:, lanes(block)])

    @pl.when(block >= first_tiles)
    def _():
        place = block - first_tiles
        group = lax.rem(place, groups)
        act(second_ref.at[columns(group, channels), lanes(lax.div(place, groups))])


def with_slot(arrays, slot, act):
    capacity = arrays[0].shape[0]
    for index, array in enumerate(arrays):

        @pl.when(lax.div(slot, capacity) == index)
        def _():
            act(array.at[lax.rem(slot, capacity)])


def fetch_blocks(order_ref, first_tiles, groups, first_ref, second_ref, wide_buf, in_sems):
    def fetch(step, carry):
        def act(view):
            pltpu.make_async_copy(view, wide_buf.at[step], in_sems.at[step]).start()

        channels = wide_buf.shape[1]
        block_views(order_ref[step], first_tiles, groups, channels, first_ref, second_ref, act)
        return carry

    lax.fori_loop(0, wide_buf.shape[0], fetch, 0)


def update_blocks(
    first_tiles,
    groups,
    order_ref,
    turned_ref,
    both_ref,
    first_ref,
    wide_buf,
    slim_buf,
    in_sems,
    out_sems,
    slim_target,
    slim_like,
    wide_out,
):
    count, channels, _ = wide_buf.shape
    micro, rows, _ = both_ref.shape
    batch = math.gcd(count, 4)

    def slim_copy(step, target):
        return pltpu.make_async_copy(slim_buf.at[step], target, out_sems.at[step])

    def body(turn, carry):
        steps = [turn * batch + item for item in range(batch)]
        for step in steps:
            pltpu.make_async_copy(
                first_ref.at[:, lanes(0)], wide_buf.at[step], in_sems.at[step]
            ).wait()
        for step in steps:
            block = order_ref[step]
            is_first = block < first_tiles
            place = jnp.maximum(block - first_tiles, 0)
            group = jnp.where(is_first, groups, lax.rem(place, groups))
            column = jnp.where(is_first, block, first_tiles + lax.div(place, groups))
            grad = jnp.dot(
                turned_ref[columns(group, channels), :],
                both_ref[:, :, lanes(column)].reshape(micro * rows, TILE),
                preferred_element_type=F32,
            )
            updated = wide_buf[step] - learning_rate * grad
            slim_buf[step] = updated.astype(BF16)
            if wide_out is not None:
                wide_buf[step] = updated
        for step in steps:
            slim_target(step, lambda target, step=step: slim_copy(step, target).start())
            if wide_out is not None:
                new_first, new_second, wide_sems = wide_out

                def act(view, step=step):
                    pltpu.make_async_copy(wide_buf.at[step], view, wide_sems.at[step]).start()

                block_views(
                    order_ref[step], first_tiles, groups, channels, new_first, new_second, act
                )
        return carry

    lax.fori_loop(0, count // batch, body, 0)

    def drain(step, carry):
        slim_copy(step, slim_like).wait()
        if wide_out is not None:
            new_first, new_second, wide_sems = wide_out
            pltpu.make_async_copy(
                wide_buf.at[step], new_first.at[:, lanes(0)], wide_sems.at[step]
            ).wait()
        return carry

    lax.fori_loop(0, count, drain, 0)


def keep_kernel(
    first_tiles, groups, order_ref, turned_ref, both_ref, first_ref, second_ref, *refs
):
    own_ref, new_first, new_second, wide_buf, slim_buf, in_sems, out_sems, wide_sems = refs
    fetch_blocks(order_ref, first_tiles, groups, first_ref, second_ref, wide_buf, in_sems)
    update_blocks(
        first_tiles,
        groups,
        order_ref,
        turned_ref,
        both_ref,
        first_ref,
        wide_buf,
        slim_buf,
        in_sems,
        out_sems,
        lambda step, act: act(own_ref.at[order_ref[step]]),
        own_ref.at[0],
        (new_first, new_second, wide_sems),
    )


def final_kernel(
    side, first_tiles, groups, partners, sec_ref, order_ref, slot_ref, returned_ref, *refs
):
    params, saved, (first_ref, second_ref) = refs[:5], refs[5:8], refs[8:10]
    old_both, turned_ref = refs[13], refs[14]
    outs, send_refs = refs[15:19], refs[19 : 19 + partners]
    refs = refs[19 + partners :]
    both_all, turned_buf, wide_buf, slim_buf, slot_sems, out_sems, more_sems = refs[:7]
    rest = refs[7:]
    micro, rows, _ = both_all.shape
    last = micro - 1
    bufs = rest[:3] + (both_all.at[last],) + rest[3:]
    idle = [
        pltpu.make_async_copy(old_both.at[item], both_all.at[item], more_sems.at[item])
        for item in range(micro)
    ]
    get_turned = pltpu.make_async_copy(turned_ref, turned_buf, more_sems.at[micro])

    def prefetch():
        for copy in idle[:last]:
            copy.start()
        get_turned.start()
        fetch_blocks(order_ref, first_tiles, groups, first_ref, second_ref, wide_buf, slot_sems)

    @pl.when(sec_ref[0] == 0)
    def _():
        back_body(0, last, side, returned_ref, params, saved, None, outs, bufs, prefetch)

    @pl.when(sec_ref[0] != 0)
    def _():
        idle[last].start()
        prefetch()
        idle[last].wait()

    for copy in idle[:last]:
        copy.wait()
    get_turned.wait()
    update_blocks(
        first_tiles,
        groups,
        order_ref,
        turned_buf,
        both_all,
        first_ref,
        wide_buf,
        slim_buf,
        slot_sems,
        out_sems,
        lambda step, act: with_slot(send_refs, slot_ref[step], act),
        send_refs[0].at[0],
        None,
    )


def place_kernel(
    first_tiles, groups, partners, order_ref, slot_ref, *refs
):
    arrived, (new_first, new_second) = refs[:partners], refs[partners + 2 : partners + 4]
    wide_buf, slim_buf, in_sems, out_sems = refs[partners + 4 :]
    count, channels, _ = wide_buf.shape

    def fetch(step, carry):
        def act(view):
            pltpu.make_async_copy(view, slim_buf.at[step], in_sems.at[step]).start()

        with_slot(arrived, slot_ref[step], act)
        return carry

    lax.fori_loop(0, count, fetch, 0)

    def body(step, carry):
        pltpu.make_async_copy(arrived[0].at[0], slim_buf.at[step], in_sems.at[step]).wait()
        wide_buf[step] = slim_buf[step].astype(F32)

        def act(view):
            pltpu.make_async_copy(wide_buf.at[step], view, out_sems.at[step]).start()

        block_views(order_ref[step], first_tiles, groups, channels, new_first, new_second, act)
        return carry

    lax.fori_loop(0, count, body, 0)

    def drain(step, carry):
        pltpu.make_async_copy(
            wide_buf.at[step], new_first.at[:, lanes(0)], out_sems.at[step]
        ).wait()
        return carry

    lax.fori_loop(0, count, drain, 0)


def params_of(limit=VMEM_LIMIT):
    return pltpu.CompilerParams(vmem_limit_bytes=limit)


def cost(flops, read):
    return pl.CostEstimate(flops=flops, bytes_accessed=read, transcendentals=0)


def pinned(arrays):
    return [pltpu.with_memory_space_constraint(item, pltpu.HBM) for item in arrays]


def hbm_spec():
    return pl.BlockSpec(memory_space=pltpu.HBM)


def train_step(owner, slot, passing, micro, side, sec, received, vectors, weights, saved):
    height, width, channels = received.shape
    rows = height * width
    hid = vectors[4].shape[1]
    saved_shapes = [
        ((height, width, channels), BF16),
        ((rows, channels), F32),
        ((rows, TILE), F32),
        ((rows, channels), BF16),
        ((rows, channels), F32),
        ((rows, hid), BF16),
        ((rows, hid), BF16),
    ]
    kept = 0 if saved is None else len(saved)
    operands = [received, *vectors, *weights] + ([] if saved is None else pinned(saved))
    if saved is None:
        operands[1:8] = pinned(vectors)
    in_specs = [whole(item) for item in operands[: len(operands) - kept]]
    in_specs += [hbm_spec()] * kept
    more_specs, more_shapes, more_scratch = [], [], []
    if saved is None:
        operands[8:10] = pinned(weights)
        in_specs[8:10] = [hbm_spec()] * 2
        more_specs = [whole(item) for item in weights]
        more_shapes = [shaped(item.shape, BF16) for item in weights]
        wide = pltpu.VMEM((hid // channels, channels, channels), F32)
        more_scratch = [wide, wide, pltpu.SemaphoreType.DMA((2, hid // channels))]
    outs = pl.pallas_call(
        functools.partial(train_kernel, owner, slot, side, passing, kept),
        grid_spec=pltpu.PrefetchScalarGridSpec(
            num_scalar_prefetch=1,
            grid=(1,),
            in_specs=in_specs,
            out_specs=[whole(received) if passing else hbm_spec()]
            + [hbm_spec() for _ in saved_shapes]
            + more_specs,
            scratch_shapes=[pltpu.VMEM(shape, dtype) for shape, dtype in saved_shapes]
            + [
                pltpu.VMEM((channels // TILE, height + 2 * REACH, width + 2 * EDGE, TILE), F32),
                pltpu.VMEM((rows, channels), F32),
                pltpu.VMEM((rows, channels), F32),
                pltpu.SemaphoreType.DMA((5,)),
                pltpu.SemaphoreType.DMA((2, hid // channels)),
            ]
            + more_scratch,
        ),
        out_shape=[shaped(received.shape, BF16)]
        + [pltpu.HBM((micro,) + shape, dtype) for shape, dtype in saved_shapes]
        + more_shapes,
        input_output_aliases={1 + len(operands) - kept + i: 1 + i for i in range(kept)},
        compiler_params=params_of(),
        cost_estimate=cost(4 * rows * channels * hid, 8 << 20),
        name=f"train_{owner}_{slot}",
    )(sec, *operands)
    return outs[0], outs[1:8], outs[8:] if saved is None else weights


def back_scratch(height, width, channels, hid):
    rows = height * width
    return [
        pltpu.VMEM((rows, channels), F32),
        pltpu.VMEM((rows, TILE), F32),
        pltpu.VMEM((rows, hid), BF16),
        pltpu.VMEM((channels // TILE, height + 2 * REACH, width + 2 * EDGE, TILE), F32),
        pltpu.VMEM((rows, channels), F32),
        pltpu.VMEM((height, width, channels), F32),
        pltpu.SemaphoreType.DMA((3,)),
        pltpu.SemaphoreType.DMA((hid // channels + 1,)),
        pltpu.SemaphoreType.DMA((hid // channels + 2,)),
    ]


def final_step(side, table, sec, returned, params, saved, weights, kept_out):
    height, width, channels = returned.shape
    rows = height * width
    first, second = weights
    hid = first.shape[1]
    turned = kept_out[4]
    micro = kept_out[3].shape[0]
    count = table["marked_order"].shape[0]
    operands = [returned, *params, *pinned((*saved, *weights, *kept_out))]
    in_specs = [whole(item) for item in operands[:6]] + [hbm_spec()] * (len(operands) - 6)
    shapes = [(item.shape, item.dtype) for item in kept_out[:4]]
    outs = pl.pallas_call(
        functools.partial(final_kernel, side, hid // TILE, hid // channels, table["partners"]),
        grid_spec=pltpu.PrefetchScalarGridSpec(
            num_scalar_prefetch=3,
            grid=(1,),
            in_specs=in_specs,
            out_specs=[hbm_spec()] * (4 + table["partners"]),
            scratch_shapes=[
                pltpu.VMEM((micro, rows, hid + channels), BF16),
                pltpu.VMEM(turned.shape, BF16),
                pltpu.VMEM((count, channels, TILE), F32),
                pltpu.VMEM((count, channels, TILE), BF16),
                pltpu.SemaphoreType.DMA((count,)),
                pltpu.SemaphoreType.DMA((count,)),
                pltpu.SemaphoreType.DMA((micro + 1,)),
            ]
            + [pltpu.VMEM(shape[1:], dtype) for shape, dtype in shapes[:3]]
            + back_scratch(height, width, channels, hid),
        ),
        out_shape=[pltpu.HBM(shape, dtype) for shape, dtype in shapes]
        + [pltpu.HBM((table["capacity"], channels, TILE), BF16)] * table["partners"],
        input_output_aliases={3 + 11 + i: i for i in range(4)},
        compiler_params=params_of(),
        cost_estimate=cost(4 * rows * channels * hid, 8 << 20),
        name="final",
    )(sec, table["marked_order"], table["send_slots"], *operands)
    return [*outs[:4], turned], outs[4:]


def back_step(owner, which, micro, side, turning, sec, returned, params, saved, kept_out):
    height, width, channels = returned.shape
    rows = height * width
    hid = saved[2].shape[-1]
    shapes = [
        ((rows, channels), BF16),
        ((rows, channels), BF16),
        ((rows, channels), F32),
        ((rows, hid + channels), BF16),
    ]
    turned = ((hid + channels, micro * rows), BF16)
    kept = 0 if kept_out is None else len(kept_out)
    operands = [returned, *params, *pinned(saved)]
    in_specs = [whole(item) for item in operands[:6]]
    in_specs += [hbm_spec()] * (len(saved) + kept)
    base = len(operands)
    operands += [] if kept_out is None else pinned(kept_out)
    outs = pl.pallas_call(
        functools.partial(back_kernel, owner, which, side, turning, kept),
        grid_spec=pltpu.PrefetchScalarGridSpec(
            num_scalar_prefetch=1,
            grid=(1,),
            in_specs=in_specs,
            out_specs=[whole(returned) if owner > 0 else hbm_spec()]
            + [hbm_spec()] * (len(shapes) + 1),
            scratch_shapes=[
                pltpu.VMEM(*turned),
                pltpu.VMEM((micro, rows, channels), BF16),
                pltpu.VMEM((micro, rows, hid), BF16),
            ]
            + [pltpu.VMEM(shape, dtype) for shape, dtype in shapes]
            + back_scratch(height, width, channels, hid),
        ),
        out_shape=[shaped(returned.shape, BF16)]
        + [pltpu.HBM((micro,) + shape, dtype) for shape, dtype in shapes]
        + [pltpu.HBM(*turned)],
        input_output_aliases={1 + base + i: 1 + i for i in range(kept)},
        compiler_params=params_of(),
        cost_estimate=cost(4 * rows * channels * hid, 8 << 20),
        name=f"back_{owner}_{which}",
    )(sec, *operands)
    return outs[0], outs[1:]


def small_step(micro, vectors, grads):
    x = grads[0]
    height, width, channels = x.shape[1:]
    return pl.pallas_call(
        functools.partial(small_kernel, micro),
        grid=(1,),
        in_specs=[whole(item) for item in vectors] + [whole(item) for item in grads],
        out_specs=[whole(item) for item in vectors],
        out_shape=[shaped(item.shape, F32) for item in vectors],
        scratch_shapes=[pltpu.VMEM((micro, height + 2 * REACH, width + 2 * EDGE, TILE), F32)],
        compiler_params=params_of(),
        cost_estimate=cost(1 << 28, 8 << 20),
        name="small",
    )(*vectors, *pinned(grads))


def distance(source, target, members):
    if members & (members - 1) == 0:
        return jnp.bitwise_xor(source, target)
    return (target - source) % members


def reached(source, step, members):
    return source ^ step if members & (members - 1) == 0 else (source + step) % members


def tables(marked, sources):
    member = lax.axis_index("member")
    members = sources.shape[1]
    blocks = marked.shape[0]
    taken = blocks // 2
    capacity = (taken + members - 2) // (members - 1)
    ids = jnp.arange(blocks, dtype=jnp.int32)
    member_ids = jnp.arange(members, dtype=jnp.int32)
    target = jnp.sum(jnp.where(sources == member, member_ids[None, :], 0), axis=1)
    anchor = jnp.sum(jnp.where(member_ids[None, :] == member, sources, 0), axis=1)
    earlier = ids[:, None] > ids[None, :]
    counted = marked[None, :] == 1
    out_rank = jnp.sum(earlier & (target[:, None] == target[None, :]) & counted, axis=1)
    in_rank = jnp.sum(earlier & (anchor[:, None] == anchor[None, :]) & counted, axis=1)
    out_slot = (members - 1 - distance(member, target, members)) * capacity + out_rank
    in_slot = (members - 1 - distance(anchor, member, members)) * capacity + in_rank
    steps = jnp.arange(taken, dtype=jnp.int32)
    top = (members - 1) * capacity - 1

    def listed(flags):
        place = jnp.sum(earlier & flags[None, :], axis=1)
        hits = flags[None, :] & (place[None, :] == steps[:, None])
        return hits, jnp.sum(jnp.where(hits, ids[None, :], 0), axis=1)

    is_marked = marked == 1
    hits, marked_order = listed(is_marked)
    send_slots = jnp.clip(jnp.sum(jnp.where(hits, out_slot[None, :], 0), axis=1), 0, top)
    take_slots = jnp.clip(jnp.sum(jnp.where(hits, in_slot[None, :], 0), axis=1), 0, top)
    _, plain_order = listed(~is_marked)
    return dict(
        partners=members - 1,
        capacity=capacity,
        marked_order=marked_order.astype(jnp.int32),
        plain_order=plain_order.astype(jnp.int32),
        send_slots=send_slots.astype(jnp.int32),
        take_slots=take_slots.astype(jnp.int32),
    )


def keep_step(order, turned, both, first, second, out_shape):
    count = order.shape[0]
    channels = first.shape[0]
    first_tiles = first.shape[1] // TILE
    groups = second.shape[0] // channels
    return pl.pallas_call(
        functools.partial(keep_kernel, first_tiles, groups),
        grid_spec=pltpu.PrefetchScalarGridSpec(
            num_scalar_prefetch=1,
            grid=(1,),
            in_specs=[whole(turned), whole(both), hbm_spec(), hbm_spec()],
            out_specs=[hbm_spec() for _ in out_shape],
            scratch_shapes=[
                pltpu.VMEM((count, channels, TILE), F32),
                pltpu.VMEM((count, channels, TILE), BF16),
            ]
            + [pltpu.SemaphoreType.DMA((count,))] * 3,
        ),
        out_shape=out_shape,
        compiler_params=params_of(),
        cost_estimate=cost(1 << 30, 8 << 20),
        name="keep",
    )(order, *pinned((turned, both, first, second)))


def local(
    inputs,
    cotangent,
    probe,
    dw_kernel,
    dw_bias,
    norm_gain,
    norm_bias,
    w_in,
    b_in,
    w_out,
    b_out,
    layer_scale,
    shuffle_mask,
    source_member,
):
    sections = lax.axis_size("section")
    sec = lax.axis_index("section").astype(jnp.int32).reshape(1)
    micro = inputs.shape[1]
    height, side, channels = inputs.shape[3:]
    width = (side + 15) // 16 * 16
    rows = height * width
    hid = w_in.shape[3]
    first_tiles = hid // TILE
    groups = hid // channels
    vectors = [
        dw_kernel.reshape(TAPS * TAPS, 1, channels),
        dw_bias[0],
        norm_gain[0],
        norm_bias[0],
        b_in[0],
        b_out[0],
        layer_scale[0],
    ]
    first = w_in[0, 0]
    second = w_out[0, 0]
    lowered = [first, second]

    def padded(maps):
        return jnp.pad(maps, ((0, 0), (0, 0), (0, width - side), (0, 0)))

    images = padded(inputs[0, :, 0])
    slopes = padded(cotangent[0, :, 0])
    trial = padded(probe[0])[0]
    entries = [images[item] for item in range(micro)]
    saved = None
    for owner in range(sections):
        leaving = []
        for item in range(micro):
            current, saved, lowered = train_step(
                owner,
                item,
                owner < sections - 1,
                micro,
                side,
                sec,
                entries[item],
                vectors,
                lowered,
                saved,
            )
            if owner < sections - 1:
                leaving.append(lax.ppermute(current, "section", [(owner, owner + 1)]))
        entries = leaving
    xs, hats, inverses, ns, mixes, hs, gelu_slopes = saved
    kernel, gain, scale = vectors[0], vectors[2], vectors[6]
    entries = [slopes[item] for item in range(micro)]
    grads = None
    turnings = {(sections - 1, 0): (0, sections - 1), (max(sections - 2, 0), micro - 1): (sections - 1, sections)}
    table = tables(shuffle_mask[0], source_member[0])
    for owner in reversed(range(sections)):
        leaving = []
        for item in range(micro):
            if owner == 0 and item == micro - 1 and grads is not None:
                grads, outgoing = final_step(
                    side,
                    table,
                    sec,
                    entries[item],
                    (kernel, gain, scale, *lowered),
                    (hats, inverses, gelu_slopes),
                    (first, second),
                    grads,
                )
                continue
            current, grads = back_step(
                owner,
                item,
                micro,
                side,
                turnings.get((owner, item)),
                sec,
                entries[item],
                (kernel, gain, scale, *lowered),
                (hats, inverses, gelu_slopes, ns, hs),
                grads,
            )
            if owner > 0:
                leaving.append(lax.ppermute(current, "section", [(owner, owner - 1)]))
        entries = leaving
    dys, dns, dspreads, boths, turned = grads

    taken = table["marked_order"].shape[0]
    blocks = shuffle_mask.shape[1]
    members = lax.axis_size("member")
    arrived = [
        lax.ppermute(
            part, "member", [(m, reached(m, members - 1 - index, members)) for m in range(members)]
        )
        for index, part in enumerate(outgoing)
    ]
    own, new_first, new_second = keep_step(
        table["plain_order"],
        turned,
        boths,
        first,
        second,
        [
            pltpu.HBM((blocks, channels, TILE), BF16),
            pltpu.HBM(first.shape, F32),
            pltpu.HBM(second.shape, F32),
        ],
    )
    vectors = small_step(micro, vectors, (xs, hats, mixes, dys, dns, dspreads, boths))

    new_first, new_second = pl.pallas_call(
        functools.partial(place_kernel, first_tiles, groups, members - 1),
        grid_spec=pltpu.PrefetchScalarGridSpec(
            num_scalar_prefetch=2,
            grid=(1,),
            in_specs=[hbm_spec()] * (members + 1),
            out_specs=[hbm_spec()] * 2,
            scratch_shapes=[
                pltpu.VMEM((taken, channels, TILE), F32),
                pltpu.VMEM((taken, channels, TILE), BF16),
                pltpu.SemaphoreType.DMA((taken,)),
                pltpu.SemaphoreType.DMA((taken,)),
            ],
        ),
        out_shape=[pltpu.HBM(first.shape, F32), pltpu.HBM(second.shape, F32)],
        input_output_aliases={members + 1: 0, members + 2: 1},
        compiler_params=params_of(),
        cost_estimate=cost(0, 8 << 20),
        name="place",
    )(table["marked_order"], table["take_slots"], *pinned((*arrived, new_first, new_second)))

    early = pl.pallas_call(
        early_kernel,
        grid_spec=pltpu.PrefetchScalarGridSpec(
            num_scalar_prefetch=1,
            grid=(1,),
            in_specs=[whole(trial)] + [whole(item) for item in vectors[:4]],
            out_specs=pl.BlockSpec((rows, channels), lambda i, s: (0, 0)),
            scratch_shapes=[
                pltpu.VMEM((channels // TILE, height + 2 * REACH, width + 2 * EDGE, TILE), F32),
                pltpu.VMEM((rows, channels), F32),
            ],
        ),
        out_shape=shaped((rows, channels), BF16),
        compiler_params=params_of(),
        cost_estimate=cost(1 << 26, 1 << 20),
        name="early",
    )(sec, trial, *vectors[:4])
    received = trial
    features = None
    for tick in range(sections):
        operands = [received, early, *vectors, *pinned((own, *arrived))]
        in_specs = [whole(item) for item in operands[:9]] + [hbm_spec()] * members
        kept = 0 if features is None else 1
        if kept:
            operands += pinned([features])
            in_specs.append(hbm_spec())
        result, features = pl.pallas_call(
            functools.partial(probe_kernel, tick, side, tick < sections - 1, members - 1, kept),
            grid_spec=pltpu.PrefetchScalarGridSpec(
                num_scalar_prefetch=4,
                grid=(1,),
                in_specs=in_specs,
                out_specs=[whole(trial) if tick < sections - 1 else hbm_spec(), hbm_spec()],
                scratch_shapes=[
                    pltpu.VMEM((height, side, channels), BF16),
                    pltpu.VMEM((blocks, channels, TILE), BF16),
                    pltpu.VMEM(
                        (channels // TILE, height + 2 * REACH, width + 2 * EDGE, TILE), F32
                    ),
                    pltpu.VMEM((rows, channels), F32),
                    pltpu.VMEM((rows, channels), F32),
                    pltpu.VMEM((rows, channels), BF16),
                    pltpu.SemaphoreType.DMA((blocks,)),
                    pltpu.SemaphoreType.DMA,
                ],
            ),
            out_shape=[shaped(trial.shape, BF16), pltpu.HBM((height, side, channels), BF16)],
            input_output_aliases={3 + len(operands): 1} if kept else {},
            compiler_params=params_of(),
            cost_estimate=cost(4 * rows * channels * hid, 8 << 20),
            name=f"probe{tick}",
        )(sec, table["marked_order"], table["take_slots"], table["plain_order"], *operands)
        if tick < sections - 1:
            received = lax.ppermute(result, "section", [(tick, tick + 1)])
    return (new_first[None, None], new_second[None, None], features[None, None, None])


def solution(mesh):
    return jax.shard_map(
        local,
        mesh=mesh,
        in_specs=(
            P("member", None, None, None, None, None),
            P("member", None, None, None, None, None),
            P("member", None, None, None, None),
            P("member", "section", None, None, None),
            P("member", "section", None),
            P("member", "section", None),
            P("member", "section", None),
            P("member", "section", None, None),
            P("member", "section", None),
            P("member", "section", None, None),
            P("member", "section", None),
            P("member", "section", None),
            P("section", None),
            P("section", None, None),
        ),
        out_specs=(
            P("member", "section", None, None),
            P("member", "section", None, None),
            P("member", "section", None, None, None, None),
        ),
        check_vma=False,
    )
```

```python
import functools
import math

import jax
import jax.numpy as jnp
from jax import lax
from jax.experimental import pallas as pl
from jax.experimental.pallas import tpu as pltpu
from jax.sharding import PartitionSpec as P

TILE = 128
learning_rate = 0.001
norm_epsilon = 1e-06
F32 = jnp.float32
BF16 = jnp.bfloat16
EDGE = 8
REACH = 3
TAPS = 2 * REACH + 1
VMEM_LIMIT = 36 * 1024 * 1024

TURN = 0.3275911 * math.sqrt(0.5)
TERMS = (1.061405429, -1.453152027, 1.421413741, -0.284496736, 0.254829592)


def normal_below(pre):
    bell = jnp.exp2((pre * pre) * (-0.5 * math.log2(math.e)))
    turn = 1.0 / (1.0 + TURN * jnp.abs(pre))
    poly = jnp.full_like(turn, 0.5 * TERMS[0])
    for term in TERMS[1:]:
        poly = poly * turn + 0.5 * term
    tail = poly * turn * bell
    return jnp.where(pre >= 0.0, 1.0 - tail, tail), bell


def whole(array):
    rank = len(array.shape)
    return pl.BlockSpec(array.shape, lambda *args: (0,) * rank)


def lanes(index):
    return pl.ds(pl.multiple_of(index * TILE, TILE), TILE)


def shaped(shape, dtype):
    return jax.ShapeDtypeStruct(shape, dtype)


def convolve(padded, chunk, kernel_ref, height, width, flip, store):
    totals = [None] * height
    for col in range(TAPS):
        taps = []
        for row in range(TAPS):
            at = row * TAPS + col
            if flip:
                at = TAPS * TAPS - 1 - at
            taps.append(kernel_ref[at, 0:1, lanes(chunk)])
        for line in range(REACH, REACH + height):
            values = padded[chunk, line, pl.ds(EDGE - REACH + col, width), :]
            for row in range(TAPS):
                out = line - row
                if 0 <= out < height:
                    term = values * taps[row]
                    totals[out] = term if totals[out] is None else totals[out] + term
    for out in range(height):
        store(out, totals[out])


def fill_padded(padded, maps):
    height, width, channels = maps.shape
    padded[...] = jnp.zeros(padded.shape, F32)
    for chunk in range(channels // TILE):
        padded[chunk, REACH : REACH + height, EDGE : EDGE + width, :] = maps[
            :, :, chunk * TILE : (chunk + 1) * TILE
        ]


def real_columns(shape, side):
    return lax.broadcasted_iota(jnp.int32, shape, 1) < side


def normalise(spread):
    center = jnp.mean(spread, axis=-1, keepdims=True)
    offset = spread - center
    variance = jnp.mean(offset * offset, axis=-1, keepdims=True)
    inverse = lax.rsqrt(variance + norm_epsilon)
    return offset * inverse, inverse


def conv_norm(vectors, widened, padded, spread, n_ref, hat_store):
    kernel_ref, bias_ref, gain_ref, shift_ref = vectors[:4]
    height, width, channels = widened.shape
    fill_padded(padded, widened)

    def conv_body(chunk, carry):
        bias = bias_ref[0:1, lanes(chunk)]

        def store(out, value):
            spread[out * width : (out + 1) * width, lanes(chunk)] = value + bias

        convolve(padded, chunk, kernel_ref, height, width, False, store)
        return carry

    lax.fori_loop(0, channels // TILE, conv_body, 0)
    hat, inverse = normalise(spread[...])
    n_ref[...] = (hat * gain_ref[...] + shift_ref[...]).astype(BF16)
    hat_store(hat, inverse)


def mix(side, vectors, widened, total, weights, n_ref, hidden_store):
    first_bias_ref, second_bias_ref, scale_ref = vectors[4:]
    height, width, channels = widened.shape
    hid = first_bias_ref.shape[1]
    total[...] = jnp.zeros(total.shape, F32)

    def mix_body(piece, carry):
        first, second = weights(piece)
        at = columns(piece, channels)
        pre = jnp.dot(n_ref[...], first, preferred_element_type=F32) + first_bias_ref[:, at]
        below, bell = normal_below(pre)
        hidden = (pre * below).astype(BF16)
        hidden_store(piece, hidden, pre, below, bell)
        total[...] += jnp.dot(hidden, second, preferred_element_type=F32)
        return carry

    lax.fori_loop(0, hid // channels, mix_body, 0)
    mixed = total[...] + second_bias_ref[...]
    result = widened + (scale_ref[...] * mixed).reshape(height, width, channels)
    result = jnp.where(real_columns(result.shape, side), result, 0.0)
    return result, mixed


def columns(piece, channels):
    return pl.ds(pl.multiple_of(piece * channels, channels), channels)


def train_kernel(owner, slot, side, passing, kept, sec_ref, entry_ref, *refs):
    vectors, (first_ref, second_ref) = refs[:7], refs[7:9]
    refs = refs[9 + kept :]
    y_ref, outs = refs[0], refs[1:8]
    refs = refs[8:]
    leading = kept == 0
    if leading:
        low_first, low_second = refs[:2]
        refs = refs[2:]
        wide_first, wide_second, wide_sems = refs[12:]
    bufs = refs[:7]
    padded, spread, total, sems, piece_sems = refs[7:12]
    x_buf, hat_buf, inverse_buf, n_buf, mixed_buf, h_buf, slope_buf = bufs
    h_out, slope_out = outs[5:]
    channels = x_buf.shape[-1]
    pieces = h_buf.shape[-1] // channels
    active = sec_ref[0] == owner

    def wide_copies(piece):
        at = columns(piece, channels)
        return [
            pltpu.make_async_copy(first_ref.at[:, at], wide_first.at[piece], wide_sems.at[0, piece]),
            pltpu.make_async_copy(second_ref.at[at, :], wide_second.at[piece], wide_sems.at[1, piece]),
        ]

    def weights(piece):
        at = columns(piece, channels)
        if not leading:
            return first_ref[:, at], second_ref[at, :]
        for copy in wide_copies(piece):
            copy.wait()
        first = wide_first[piece].astype(BF16)
        second = wide_second[piece].astype(BF16)
        low_first[:, at] = first
        low_second[at, :] = second
        return first, second

    if leading:
        for piece in range(pieces):
            for copy in wide_copies(piece):
                copy.start()

        @pl.when(jnp.logical_not(active))
        def _():
            def body(piece, carry):
                weights(piece)
                return carry

            lax.fori_loop(0, pieces, body, 0)

    @pl.when(active)
    def _():
        entry = entry_ref[...].astype(F32)
        x_buf[...] = entry_ref[...]

        def piece_copies(piece):
            at = columns(piece, channels)
            return [
                pltpu.make_async_copy(h_buf.at[:, at], h_out.at[slot, :, at], piece_sems.at[0, piece]),
                pltpu.make_async_copy(
                    slope_buf.at[:, at], slope_out.at[slot, :, at], piece_sems.at[1, piece]
                ),
            ]

        def hidden_store(piece, hidden, pre, below, bell):
            at = columns(piece, channels)
            h_buf[:, at] = hidden
            slope_buf[:, at] = (below + pre * (bell * (1.0 / math.sqrt(2.0 * math.pi)))).astype(BF16)
            for copy in piece_copies(piece):
                copy.start()

        copies = [
            pltpu.make_async_copy(buf, out.at[slot], sems.at[index])
            for index, (buf, out) in enumerate(zip(bufs[:5], outs[:5]))
        ]

        def hat_store(hat, inverse):
            hat_buf[...] = hat
            inverse_buf[...] = jnp.broadcast_to(inverse, inverse_buf.shape)
            for copy in copies[:4]:
                copy.start()

        conv_norm(vectors, entry, padded, spread, n_buf, hat_store)
        result, mixed = mix(side, vectors, entry, total, weights, n_buf, hidden_store)
        if passing:
            y_ref[...] = result.astype(BF16)
        mixed_buf[...] = mixed
        copies[4].start()
        for copy in copies:
            copy.wait()
        for piece in range(pieces):
            for copy in piece_copies(piece):
                copy.wait()


def early_kernel(sec_ref, image_ref, *refs):
    vectors = refs[:4]
    n_ref, padded, spread = refs[4:]

    @pl.when(sec_ref[0] == 0)
    def _():
        conv_norm(
            vectors, image_ref[...].astype(F32), padded, spread, n_ref, lambda hat, inverse: None
        )


def probe_kernel(
    tick, side, passing, partners, kept, sec_ref, marked_ref, slot_ref, plain_ref, received_ref, early_ref, *refs
):
    vectors, own_ref, arrived = refs[:7], refs[7], refs[8 : 8 + partners]
    refs = refs[8 + partners + kept :]
    y_ref, feature_ref, feature_buf, tiles_buf, padded, spread, total, n_buf, sems, end_sem = refs

    @pl.when(sec_ref[0] == tick)
    def _():
        channels = y_ref.shape[-1]
        tiles = channels // TILE
        groups = vectors[4].shape[1] // channels

        def fetch(step, carry):
            block = marked_ref[step]

            def act(view):
                pltpu.make_async_copy(view, tiles_buf.at[block], sems.at[block]).start()

            with_slot(arrived, slot_ref[step], act)
            plain = plain_ref[step]
            pltpu.make_async_copy(own_ref.at[plain], tiles_buf.at[plain], sems.at[plain]).start()
            return carry

        lax.fori_loop(0, tiles_buf.shape[0] // 2, fetch, 0)
        entry = received_ref[...].astype(F32)

        def wait(block):
            pltpu.make_async_copy(own_ref.at[block], tiles_buf.at[block], sems.at[block]).wait()

        def weights(piece):
            first = [piece * tiles + item for item in range(tiles)]
            second = [groups * tiles + item * groups + piece for item in range(tiles)]
            for block in first + second:
                wait(block)
            return (
                jnp.concatenate([tiles_buf[block] for block in first], axis=1),
                jnp.concatenate([tiles_buf[block] for block in second], axis=1),
            )

        if tick > 0:
            conv_norm(vectors, entry, padded, spread, n_buf, lambda hat, inverse: None)
        result, mixed = mix(
            side,
            vectors,
            entry,
            total,
            weights,
            early_ref if tick == 0 else n_buf,
            lambda piece, hidden, pre, below, bell: None,
        )
        output = result.astype(BF16)
        if passing:
            y_ref[...] = output
        feature_buf[...] = output[:, :side, :]
        done = pltpu.make_async_copy(feature_buf, feature_ref, end_sem)
        done.start()
        done.wait()


def back_body(owner, which, side, returned_ref, params, saved, dx_ref, outs, bufs, then=None):
    kernel_ref, gain_ref, scale_ref, first_ref, second_ref = params
    hat_ref, inverse_ref, slope_ref = saved
    both_out = outs[3]
    dy_buf, dn_buf, dspread_buf, both_buf, hat_buf, inverse_buf, slope_buf = bufs[:7]
    padded, total, conv_out, sems, piece_sems, in_sems = bufs[7:]
    hid = slope_buf.shape[-1]
    height, width, channels = returned_ref.shape
    pieces = hid // channels
    rows = height * width
    ins = [
        pltpu.make_async_copy(
            slope_ref.at[which, :, columns(piece, channels)],
            slope_buf.at[:, columns(piece, channels)],
            in_sems.at[piece],
        )
        for piece in range(pieces)
    ]
    ins.append(pltpu.make_async_copy(hat_ref.at[which], hat_buf, in_sems.at[pieces]))
    ins.append(pltpu.make_async_copy(inverse_ref.at[which], inverse_buf, in_sems.at[pieces + 1]))
    for copy in ins:
        copy.start()
    if then is not None:
        then()
    dy = returned_ref[...].astype(F32)
    flat = dy.reshape(rows, channels)
    dy_buf[...] = flat.astype(BF16)
    mix_at = columns(pieces, channels)
    both_buf[:, mix_at] = (flat * scale_ref[...]).astype(BF16)
    total[...] = jnp.zeros(total.shape, F32)
    contract = (((1,), (1,)), ((), ()))
    copies = [
        pltpu.make_async_copy(buf, out.at[which], sems.at[index])
        for index, (buf, out) in enumerate(zip((dy_buf, dn_buf, dspread_buf), outs))
    ]
    copies[0].start()

    def both_copy(piece):
        at = columns(piece, channels)
        return pltpu.make_async_copy(
            both_buf.at[:, at], both_out.at[which, :, at], piece_sems.at[piece]
        )

    both_copy(pieces).start()

    def body(piece, carry):
        at = columns(piece, channels)
        dh = lax.dot_general(
            both_buf[:, mix_at], second_ref[at, :], contract, preferred_element_type=F32
        )
        pltpu.make_async_copy(
            slope_ref.at[which, :, at], slope_buf.at[:, at], in_sems.at[piece]
        ).wait()
        dpre = (dh * slope_buf[:, at].astype(F32)).astype(BF16)
        both_buf[:, at] = dpre
        both_copy(piece).start()
        total[...] += lax.dot_general(
            dpre, first_ref[:, at], contract, preferred_element_type=F32
        )
        return carry

    lax.fori_loop(0, pieces, body, 0)
    ins[pieces].wait()
    ins[pieces + 1].wait()
    dn = total[...]
    dn_buf[...] = dn.astype(BF16)
    copies[1].start()
    hat = hat_buf[...]
    dhat = dn * gain_ref[...]
    mean = jnp.mean(dhat, axis=-1, keepdims=True)
    along = jnp.mean(dhat * hat, axis=-1, keepdims=True)
    dspread = inverse_buf[:, 0:1] * (dhat - mean - hat * along)
    dspread_buf[...] = dspread
    copies[2].start()
    if owner > 0:
        fill_padded(padded, dspread.reshape(height, width, channels))

        def conv_body(chunk, carry):
            def store(out, value):
                conv_out[out, :, lanes(chunk)] = value

            convolve(padded, chunk, kernel_ref, height, width, True, store)
            return carry

        lax.fori_loop(0, channels // TILE, conv_body, 0)
        dx = dy + conv_out[...]
        dx = jnp.where(real_columns(dx.shape, side), dx, 0.0)
        dx_ref[...] = dx.astype(BF16)
    for copy in copies:
        copy.wait()
    for piece in range(pieces + 1):
        both_copy(piece).wait()


def back_kernel(owner, which, side, turning, kept, sec_ref, returned_ref, *refs):
    params, saved, (n_ref, h_ref) = refs[:5], refs[5:8], refs[8:10]
    refs = refs[10 + kept :]
    dx_ref, outs, turned_ref = refs[0], refs[1:5], refs[5]
    turned_buf, n_buf, h_buf = refs[6:9]
    bufs = refs[9:]
    sems = bufs[10]
    channels = returned_ref.shape[-1]
    pieces = h_buf.shape[-1] // channels

    @pl.when(sec_ref[0] == owner)
    def _():
        back_body(owner, which, side, returned_ref, params, saved, dx_ref, outs, bufs)

    if turning is not None:
        low, high = turning

        @pl.when((sec_ref[0] >= low) & (sec_ref[0] < high))
        def _():
            get_n = pltpu.make_async_copy(n_ref, n_buf, sems.at[0])
            get_h = pltpu.make_async_copy(h_ref, h_buf, sems.at[1])
            get_n.start()
            get_h.start()
            get_h.wait()
            get_n.wait()
            depth = turned_buf.shape[1]

            def turn(piece, carry):
                at = columns(piece, channels)
                turned_buf[at, :] = h_buf[:, :, at].reshape(depth, channels).T
                return carry

            lax.fori_loop(0, pieces, turn, 0)
            turned_buf[columns(pieces, channels), :] = n_buf[...].reshape(depth, channels).T
            put = pltpu.make_async_copy(turned_buf, turned_ref, sems.at[2])
            put.start()
            put.wait()


def small_kernel(micro, *refs):
    (kernel_ref, bias_ref, gain_ref, shift_ref, first_bias_ref, second_bias_ref, scale_ref) = refs[:7]
    x_ref, hat_ref, mixed_ref, dy_ref, dn_ref, dspread_ref, both_ref = refs[7:14]
    outs = refs[14:21]
    padded = refs[21]
    height, width, channels = x_ref.shape[1:]

    def total(values):
        return jnp.sum(values, axis=0, keepdims=True)

    def chunk_body(chunk, carry):
        at = lanes(chunk)
        scale = scale_ref[0:1, at]
        sums = [0.0] * 5
        for item in range(micro):
            dy = dy_ref[item, :, at].astype(F32)
            dn = dn_ref[item, :, at].astype(F32)
            sums[0] += total(dspread_ref[item, :, at])
            sums[1] += total(dn * hat_ref[item, :, at])
            sums[2] += total(dn)
            sums[3] += total(dy)
            sums[4] += total(dy * mixed_ref[item, :, at])
        outs[1][0:1, at] = bias_ref[0:1, at] - learning_rate * sums[0]
        outs[2][0:1, at] = gain_ref[0:1, at] - learning_rate * sums[1]
        outs[3][0:1, at] = shift_ref[0:1, at] - learning_rate * sums[2]
        outs[5][0:1, at] = second_bias_ref[0:1, at] - learning_rate * (scale * sums[3])
        outs[6][0:1, at] = scale - learning_rate * sums[4]
        padded[...] = jnp.zeros(padded.shape, F32)
        for item in range(micro):
            padded[item, REACH : REACH + height, EDGE : EDGE + width, :] = x_ref[
                item, :, :, at
            ].astype(F32)
        for col in range(TAPS):
            for row in range(TAPS):
                acc = None
                for item in range(micro):
                    for out in range(max(0, REACH - row), min(height, height + REACH - row)):
                        term = (
                            padded[item, out + row, pl.ds(EDGE - REACH + col, width), :]
                            * dspread_ref[item, out * width : (out + 1) * width, at]
                        )
                        acc = term if acc is None else acc + term
                tap = row * TAPS + col
                outs[0][tap, 0:1, at] = kernel_ref[tap, 0:1, at] - learning_rate * total(acc)
        return carry

    lax.fori_loop(0, channels // TILE, chunk_body, 0)
    hid = first_bias_ref.shape[1]

    def bias_body(piece, carry):
        at = lanes(piece)
        acc = 0.0
        for item in range(micro):
            acc += total(both_ref[item, :, at].astype(F32))
        outs[4][0:1, at] = first_bias_ref[0:1, at] - learning_rate * acc
        return carry

    lax.fori_loop(0, hid // TILE, bias_body, 0)


def block_views(block, first_tiles, groups, channels, first_ref, second_ref, act):
    @pl.when(block < first_tiles)
    def _():
        act(first_ref.at[:, lanes(block)])

    @pl.when(block >= first_tiles)
    def _():
        place = block - first_tiles
        group = lax.rem(place, groups)
        act(second_ref.at[columns(group, channels), lanes(lax.div(place, groups))])


def slot_bits(capacity):
    return (capacity - 1).bit_length()


def with_slot(arrays, slot, act):
    bits = slot_bits(arrays[0].shape[0])
    owner = lax.shift_right_logical(slot, bits)
    place = lax.bitwise_and(slot, (1 << bits) - 1)
    for index, array in enumerate(arrays):

        @pl.when(owner == index)
        def _():
            act(array.at[place])


def fetch_blocks(order_ref, first_tiles, groups, first_ref, second_ref, wide_buf, in_sems):
    def fetch(step, carry):
        def act(view):
            pltpu.make_async_copy(view, wide_buf.at[step], in_sems.at[step]).start()

        channels = wide_buf.shape[1]
        block_views(order_ref[step], first_tiles, groups, channels, first_ref, second_ref, act)
        return carry

    lax.fori_loop(0, wide_buf.shape[0], fetch, 0)


def update_blocks(
    first_tiles,
    groups,
    order_ref,
    turned_ref,
    both_ref,
    first_ref,
    wide_buf,
    slim_buf,
    in_sems,
    out_sems,
    slim_target,
    slim_like,
    wide_out,
):
    count, channels, _ = wide_buf.shape
    micro, rows, _ = both_ref.shape
    batch = math.gcd(count, 4)

    def slim_copy(step, target):
        return pltpu.make_async_copy(slim_buf.at[step], target, out_sems.at[step])

    def body(turn, carry):
        steps = [turn * batch + item for item in range(batch)]
        for step in steps:
            pltpu.make_async_copy(
                first_ref.at[:, lanes(0)], wide_buf.at[step], in_sems.at[step]
            ).wait()
        for step in steps:
            block = order_ref[step]
            is_first = block < first_tiles
            place = jnp.maximum(block - first_tiles, 0)
            group = jnp.where(is_first, groups, lax.rem(place, groups))
            column = jnp.where(is_first, block, first_tiles + lax.div(place, groups))
            grad = jnp.dot(
                turned_ref[columns(group, channels), :],
                both_ref[:, :, lanes(column)].reshape(micro * rows, TILE),
                preferred_element_type=F32,
            )
            updated = wide_buf[step] - learning_rate * grad
            slim_buf[step] = updated.astype(BF16)
            if wide_out is not None:
                wide_buf[step] = updated
        for step in steps:
            slim_target(step, lambda target, step=step: slim_copy(step, target).start())
            if wide_out is not None:
                new_first, new_second, wide_sems = wide_out

                def act(view, step=step):
                    pltpu.make_async_copy(wide_buf.at[step], view, wide_sems.at[step]).start()

                block_views(
                    order_ref[step], first_tiles, groups, channels, new_first, new_second, act
                )
        return carry

    lax.fori_loop(0, count // batch, body, 0)

    def drain(step, carry):
        slim_copy(step, slim_like).wait()
        if wide_out is not None:
            new_first, new_second, wide_sems = wide_out
            pltpu.make_async_copy(
                wide_buf.at[step], new_first.at[:, lanes(0)], wide_sems.at[step]
            ).wait()
        return carry

    lax.fori_loop(0, count, drain, 0)


def keep_kernel(
    first_tiles, groups, order_ref, turned_ref, both_ref, first_ref, second_ref, *refs
):
    own_ref, new_first, new_second, wide_buf, slim_buf, in_sems, out_sems, wide_sems = refs
    fetch_blocks(order_ref, first_tiles, groups, first_ref, second_ref, wide_buf, in_sems)
    update_blocks(
        first_tiles,
        groups,
        order_ref,
        turned_ref,
        both_ref,
        first_ref,
        wide_buf,
        slim_buf,
        in_sems,
        out_sems,
        lambda step, act: act(own_ref.at[order_ref[step]]),
        own_ref.at[0],
        (new_first, new_second, wide_sems),
    )


def final_kernel(
    side, first_tiles, groups, partners, sec_ref, order_ref, slot_ref, returned_ref, *refs
):
    params, saved, (first_ref, second_ref) = refs[:5], refs[5:8], refs[8:10]
    old_both, turned_ref = refs[13], refs[14]
    outs, send_refs = refs[15:19], refs[19 : 19 + partners]
    refs = refs[19 + partners :]
    both_all, turned_buf, wide_buf, slim_buf, slot_sems, out_sems, more_sems = refs[:7]
    rest = refs[7:]
    micro, rows, _ = both_all.shape
    last = micro - 1
    bufs = rest[:3] + (both_all.at[last],) + rest[3:]
    idle = [
        pltpu.make_async_copy(old_both.at[item], both_all.at[item], more_sems.at[item])
        for item in range(micro)
    ]
    get_turned = pltpu.make_async_copy(turned_ref, turned_buf, more_sems.at[micro])

    def prefetch():
        for copy in idle[:last]:
            copy.start()
        get_turned.start()
        fetch_blocks(order_ref, first_tiles, groups, first_ref, second_ref, wide_buf, slot_sems)

    @pl.when(sec_ref[0] == 0)
    def _():
        back_body(0, last, side, returned_ref, params, saved, None, outs, bufs, prefetch)

    @pl.when(sec_ref[0] != 0)
    def _():
        idle[last].start()
        prefetch()
        idle[last].wait()

    for copy in idle[:last]:
        copy.wait()
    get_turned.wait()
    update_blocks(
        first_tiles,
        groups,
        order_ref,
        turned_buf,
        both_all,
        first_ref,
        wide_buf,
        slim_buf,
        slot_sems,
        out_sems,
        lambda step, act: with_slot(send_refs, slot_ref[step], act),
        send_refs[0].at[0],
        None,
    )


def place_kernel(
    first_tiles, groups, partners, order_ref, slot_ref, *refs
):
    arrived, (new_first, new_second) = refs[:partners], refs[partners + 2 : partners + 4]
    wide_buf, slim_buf, in_sems, out_sems = refs[partners + 4 :]
    count, channels, _ = wide_buf.shape

    def fetch(step, carry):
        def act(view):
            pltpu.make_async_copy(view, slim_buf.at[step], in_sems.at[step]).start()

        with_slot(arrived, slot_ref[step], act)
        return carry

    lax.fori_loop(0, count, fetch, 0)

    def body(step, carry):
        pltpu.make_async_copy(arrived[0].at[0], slim_buf.at[step], in_sems.at[step]).wait()
        wide_buf[step] = slim_buf[step].astype(F32)

        def act(view):
            pltpu.make_async_copy(wide_buf.at[step], view, out_sems.at[step]).start()

        block_views(order_ref[step], first_tiles, groups, channels, new_first, new_second, act)
        return carry

    lax.fori_loop(0, count, body, 0)

    def drain(step, carry):
        pltpu.make_async_copy(
            wide_buf.at[step], new_first.at[:, lanes(0)], out_sems.at[step]
        ).wait()
        return carry

    lax.fori_loop(0, count, drain, 0)


def params_of(limit=VMEM_LIMIT):
    return pltpu.CompilerParams(vmem_limit_bytes=limit)


def cost(flops, read):
    return pl.CostEstimate(flops=flops, bytes_accessed=read, transcendentals=0)


def pinned(arrays):
    return [pltpu.with_memory_space_constraint(item, pltpu.HBM) for item in arrays]


def hbm_spec():
    return pl.BlockSpec(memory_space=pltpu.HBM)


def train_step(owner, slot, passing, micro, side, sec, received, vectors, weights, saved):
    height, width, channels = received.shape
    rows = height * width
    hid = vectors[4].shape[1]
    saved_shapes = [
        ((height, width, channels), BF16),
        ((rows, channels), F32),
        ((rows, TILE), F32),
        ((rows, channels), BF16),
        ((rows, channels), F32),
        ((rows, hid), BF16),
        ((rows, hid), BF16),
    ]
    kept = 0 if saved is None else len(saved)
    operands = [received, *vectors, *weights] + ([] if saved is None else pinned(saved))
    if saved is None:
        operands[1:8] = pinned(vectors)
    in_specs = [whole(item) for item in operands[: len(operands) - kept]]
    in_specs += [hbm_spec()] * kept
    more_specs, more_shapes, more_scratch = [], [], []
    if saved is None:
        operands[8:10] = pinned(weights)
        in_specs[8:10] = [hbm_spec()] * 2
        more_specs = [whole(item) for item in weights]
        more_shapes = [shaped(item.shape, BF16) for item in weights]
        wide = pltpu.VMEM((hid // channels, channels, channels), F32)
        more_scratch = [wide, wide, pltpu.SemaphoreType.DMA((2, hid // channels))]
    outs = pl.pallas_call(
        functools.partial(train_kernel, owner, slot, side, passing, kept),
        grid_spec=pltpu.PrefetchScalarGridSpec(
            num_scalar_prefetch=1,
            grid=(1,),
            in_specs=in_specs,
            out_specs=[whole(received) if passing else hbm_spec()]
            + [hbm_spec() for _ in saved_shapes]
            + more_specs,
            scratch_shapes=[pltpu.VMEM(shape, dtype) for shape, dtype in saved_shapes]
            + [
                pltpu.VMEM((channels // TILE, height + 2 * REACH, width + 2 * EDGE, TILE), F32),
                pltpu.VMEM((rows, channels), F32),
                pltpu.VMEM((rows, channels), F32),
                pltpu.SemaphoreType.DMA((5,)),
                pltpu.SemaphoreType.DMA((2, hid // channels)),
            ]
            + more_scratch,
        ),
        out_shape=[shaped(received.shape, BF16)]
        + [pltpu.HBM((micro,) + shape, dtype) for shape, dtype in saved_shapes]
        + more_shapes,
        input_output_aliases={1 + len(operands) - kept + i: 1 + i for i in range(kept)},
        compiler_params=params_of(),
        cost_estimate=cost(4 * rows * channels * hid, 8 << 20),
        name=f"train_{owner}_{slot}",
    )(sec, *operands)
    return outs[0], outs[1:8], outs[8:] if saved is None else weights


def back_scratch(height, width, channels, hid):
    rows = height * width
    return [
        pltpu.VMEM((rows, channels), F32),
        pltpu.VMEM((rows, TILE), F32),
        pltpu.VMEM((rows, hid), BF16),
        pltpu.VMEM((channels // TILE, height + 2 * REACH, width + 2 * EDGE, TILE), F32),
        pltpu.VMEM((rows, channels), F32),
        pltpu.VMEM((height, width, channels), F32),
        pltpu.SemaphoreType.DMA((3,)),
        pltpu.SemaphoreType.DMA((hid // channels + 1,)),
        pltpu.SemaphoreType.DMA((hid // channels + 2,)),
    ]


def final_step(side, table, sec, returned, params, saved, weights, kept_out):
    height, width, channels = returned.shape
    rows = height * width
    first, second = weights
    hid = first.shape[1]
    turned = kept_out[4]
    micro = kept_out[3].shape[0]
    count = table["marked_order"].shape[0]
    operands = [returned, *params, *pinned((*saved, *weights, *kept_out))]
    in_specs = [whole(item) for item in operands[:6]] + [hbm_spec()] * (len(operands) - 6)
    shapes = [(item.shape, item.dtype) for item in kept_out[:4]]
    outs = pl.pallas_call(
        functools.partial(final_kernel, side, hid // TILE, hid // channels, table["partners"]),
        grid_spec=pltpu.PrefetchScalarGridSpec(
            num_scalar_prefetch=3,
            grid=(1,),
            in_specs=in_specs,
            out_specs=[hbm_spec()] * (4 + table["partners"]),
            scratch_shapes=[
                pltpu.VMEM((micro, rows, hid + channels), BF16),
                pltpu.VMEM(turned.shape, BF16),
                pltpu.VMEM((count, channels, TILE), F32),
                pltpu.VMEM((count, channels, TILE), BF16),
                pltpu.SemaphoreType.DMA((count,)),
                pltpu.SemaphoreType.DMA((count,)),
                pltpu.SemaphoreType.DMA((micro + 1,)),
            ]
            + [pltpu.VMEM(shape[1:], dtype) for shape, dtype in shapes[:3]]
            + back_scratch(height, width, channels, hid),
        ),
        out_shape=[pltpu.HBM(shape, dtype) for shape, dtype in shapes]
        + [pltpu.HBM((table["capacity"], channels, TILE), BF16)] * table["partners"],
        input_output_aliases={3 + 11 + i: i for i in range(4)},
        compiler_params=params_of(),
        cost_estimate=cost(4 * rows * channels * hid, 8 << 20),
        name="final",
    )(sec, table["marked_order"], table["send_slots"], *operands)
    return [*outs[:4], turned], outs[4:]


def back_step(owner, which, micro, side, turning, sec, returned, params, saved, kept_out):
    height, width, channels = returned.shape
    rows = height * width
    hid = saved[2].shape[-1]
    shapes = [
        ((rows, channels), BF16),
        ((rows, channels), BF16),
        ((rows, channels), F32),
        ((rows, hid + channels), BF16),
    ]
    turned = ((hid + channels, micro * rows), BF16)
    kept = 0 if kept_out is None else len(kept_out)
    operands = [returned, *params, *pinned(saved)]
    in_specs = [whole(item) for item in operands[:6]]
    in_specs += [hbm_spec()] * (len(saved) + kept)
    base = len(operands)
    operands += [] if kept_out is None else pinned(kept_out)
    outs = pl.pallas_call(
        functools.partial(back_kernel, owner, which, side, turning, kept),
        grid_spec=pltpu.PrefetchScalarGridSpec(
            num_scalar_prefetch=1,
            grid=(1,),
            in_specs=in_specs,
            out_specs=[whole(returned) if owner > 0 else hbm_spec()]
            + [hbm_spec()] * (len(shapes) + 1),
            scratch_shapes=[
                pltpu.VMEM(*turned),
                pltpu.VMEM((micro, rows, channels), BF16),
                pltpu.VMEM((micro, rows, hid), BF16),
            ]
            + [pltpu.VMEM(shape, dtype) for shape, dtype in shapes]
            + back_scratch(height, width, channels, hid),
        ),
        out_shape=[shaped(returned.shape, BF16)]
        + [pltpu.HBM((micro,) + shape, dtype) for shape, dtype in shapes]
        + [pltpu.HBM(*turned)],
        input_output_aliases={1 + base + i: 1 + i for i in range(kept)},
        compiler_params=params_of(),
        cost_estimate=cost(4 * rows * channels * hid, 8 << 20),
        name=f"back_{owner}_{which}",
    )(sec, *operands)
    return outs[0], outs[1:]


def small_step(micro, vectors, grads):
    x = grads[0]
    height, width, channels = x.shape[1:]
    return pl.pallas_call(
        functools.partial(small_kernel, micro),
        grid=(1,),
        in_specs=[whole(item) for item in vectors] + [whole(item) for item in grads],
        out_specs=[whole(item) for item in vectors],
        out_shape=[shaped(item.shape, F32) for item in vectors],
        scratch_shapes=[pltpu.VMEM((micro, height + 2 * REACH, width + 2 * EDGE, TILE), F32)],
        compiler_params=params_of(),
        cost_estimate=cost(1 << 28, 8 << 20),
        name="small",
    )(*vectors, *pinned(grads))


def distance(source, target, members):
    if members & (members - 1) == 0:
        return jnp.bitwise_xor(source, target)
    return (target - source) % members


def reached(source, step, members):
    return source ^ step if members & (members - 1) == 0 else (source + step) % members


def tables(marked, sources):
    member = lax.axis_index("member")
    members = sources.shape[1]
    blocks = marked.shape[0]
    taken = blocks // 2
    capacity = (taken + members - 2) // (members - 1)
    ids = jnp.arange(blocks, dtype=jnp.int32)
    member_ids = jnp.arange(members, dtype=jnp.int32)
    target = jnp.sum(jnp.where(sources == member, member_ids[None, :], 0), axis=1)
    anchor = jnp.sum(jnp.where(member_ids[None, :] == member, sources, 0), axis=1)
    earlier = ids[:, None] > ids[None, :]
    counted = marked[None, :] == 1
    out_rank = jnp.sum(earlier & (target[:, None] == target[None, :]) & counted, axis=1)
    in_rank = jnp.sum(earlier & (anchor[:, None] == anchor[None, :]) & counted, axis=1)
    stride = 1 << slot_bits(capacity)
    out_slot = (members - 1 - distance(member, target, members)) * stride + out_rank
    in_slot = (members - 1 - distance(anchor, member, members)) * stride + in_rank
    steps = jnp.arange(taken, dtype=jnp.int32)
    top = (members - 2) * stride + capacity - 1

    def listed(flags):
        place = jnp.sum(earlier & flags[None, :], axis=1)
        hits = flags[None, :] & (place[None, :] == steps[:, None])
        return hits, jnp.sum(jnp.where(hits, ids[None, :], 0), axis=1)

    is_marked = marked == 1
    hits, marked_order = listed(is_marked)
    send_slots = jnp.clip(jnp.sum(jnp.where(hits, out_slot[None, :], 0), axis=1), 0, top)
    take_slots = jnp.clip(jnp.sum(jnp.where(hits, in_slot[None, :], 0), axis=1), 0, top)
    _, plain_order = listed(~is_marked)
    return dict(
        partners=members - 1,
        capacity=capacity,
        marked_order=marked_order.astype(jnp.int32),
        plain_order=plain_order.astype(jnp.int32),
        send_slots=send_slots.astype(jnp.int32),
        take_slots=take_slots.astype(jnp.int32),
    )


def keep_step(order, turned, both, first, second, out_shape):
    count = order.shape[0]
    channels = first.shape[0]
    first_tiles = first.shape[1] // TILE
    groups = second.shape[0] // channels
    return pl.pallas_call(
        functools.partial(keep_kernel, first_tiles, groups),
        grid_spec=pltpu.PrefetchScalarGridSpec(
            num_scalar_prefetch=1,
            grid=(1,),
            in_specs=[whole(turned), whole(both), hbm_spec(), hbm_spec()],
            out_specs=[hbm_spec() for _ in out_shape],
            scratch_shapes=[
                pltpu.VMEM((count, channels, TILE), F32),
                pltpu.VMEM((count, channels, TILE), BF16),
            ]
            + [pltpu.SemaphoreType.DMA((count,))] * 3,
        ),
        out_shape=out_shape,
        compiler_params=params_of(),
        cost_estimate=cost(1 << 30, 8 << 20),
        name="keep",
    )(order, *pinned((turned, both, first, second)))


def local(
    inputs,
    cotangent,
    probe,
    dw_kernel,
    dw_bias,
    norm_gain,
    norm_bias,
    w_in,
    b_in,
    w_out,
    b_out,
    layer_scale,
    shuffle_mask,
    source_member,
):
    sections = lax.axis_size("section")
    sec = lax.axis_index("section").astype(jnp.int32).reshape(1)
    micro = inputs.shape[1]
    height, side, channels = inputs.shape[3:]
    width = (side + 15) // 16 * 16
    rows = height * width
    hid = w_in.shape[3]
    first_tiles = hid // TILE
    groups = hid // channels
    vectors = [
        dw_kernel.reshape(TAPS * TAPS, 1, channels),
        dw_bias[0],
        norm_gain[0],
        norm_bias[0],
        b_in[0],
        b_out[0],
        layer_scale[0],
    ]
    first = w_in[0, 0]
    second = w_out[0, 0]
    lowered = [first, second]

    def padded(maps):
        return jnp.pad(maps, ((0, 0), (0, 0), (0, width - side), (0, 0)))

    images = padded(inputs[0, :, 0])
    slopes = padded(cotangent[0, :, 0])
    trial = padded(probe[0])[0]
    entries = [images[item] for item in range(micro)]
    saved = None
    for owner in range(sections):
        leaving = []
        for item in range(micro):
            current, saved, lowered = train_step(
                owner,
                item,
                owner < sections - 1,
                micro,
                side,
                sec,
                entries[item],
                vectors,
                lowered,
                saved,
            )
            if owner < sections - 1:
                leaving.append(lax.ppermute(current, "section", [(owner, owner + 1)]))
        entries = leaving
    xs, hats, inverses, ns, mixes, hs, gelu_slopes = saved
    kernel, gain, scale = vectors[0], vectors[2], vectors[6]
    entries = [slopes[item] for item in range(micro)]
    grads = None
    turnings = {(sections - 1, 0): (0, sections - 1), (max(sections - 2, 0), micro - 1): (sections - 1, sections)}
    table = tables(shuffle_mask[0], source_member[0])
    for owner in reversed(range(sections)):
        leaving = []
        for item in range(micro):
            if owner == 0 and item == micro - 1 and grads is not None:
                grads, outgoing = final_step(
                    side,
                    table,
                    sec,
                    entries[item],
                    (kernel, gain, scale, *lowered),
                    (hats, inverses, gelu_slopes),
                    (first, second),
                    grads,
                )
                continue
            current, grads = back_step(
                owner,
                item,
                micro,
                side,
                turnings.get((owner, item)),
                sec,
                entries[item],
                (kernel, gain, scale, *lowered),
                (hats, inverses, gelu_slopes, ns, hs),
                grads,
            )
            if owner > 0:
                leaving.append(lax.ppermute(current, "section", [(owner, owner - 1)]))
        entries = leaving
    dys, dns, dspreads, boths, turned = grads

    taken = table["marked_order"].shape[0]
    blocks = shuffle_mask.shape[1]
    members = lax.axis_size("member")
    arrived = [
        lax.ppermute(
            part, "member", [(m, reached(m, members - 1 - index, members)) for m in range(members)]
        )
        for index, part in enumerate(outgoing)
    ]
    own, new_first, new_second = keep_step(
        table["plain_order"],
        turned,
        boths,
        first,
        second,
        [
            pltpu.HBM((blocks, channels, TILE), BF16),
            pltpu.HBM(first.shape, F32),
            pltpu.HBM(second.shape, F32),
        ],
    )
    vectors = small_step(micro, vectors, (xs, hats, mixes, dys, dns, dspreads, boths))

    new_first, new_second = pl.pallas_call(
        functools.partial(place_kernel, first_tiles, groups, members - 1),
        grid_spec=pltpu.PrefetchScalarGridSpec(
            num_scalar_prefetch=2,
            grid=(1,),
            in_specs=[hbm_spec()] * (members + 1),
            out_specs=[hbm_spec()] * 2,
            scratch_shapes=[
                pltpu.VMEM((taken, channels, TILE), F32),
                pltpu.VMEM((taken, channels, TILE), BF16),
                pltpu.SemaphoreType.DMA((taken,)),
                pltpu.SemaphoreType.DMA((taken,)),
            ],
        ),
        out_shape=[pltpu.HBM(first.shape, F32), pltpu.HBM(second.shape, F32)],
        input_output_aliases={members + 1: 0, members + 2: 1},
        compiler_params=params_of(),
        cost_estimate=cost(0, 8 << 20),
        name="place",
    )(table["marked_order"], table["take_slots"], *pinned((*arrived, new_first, new_second)))

    early = pl.pallas_call(
        early_kernel,
        grid_spec=pltpu.PrefetchScalarGridSpec(
            num_scalar_prefetch=1,
            grid=(1,),
            in_specs=[whole(trial)] + [whole(item) for item in vectors[:4]],
            out_specs=pl.BlockSpec((rows, channels), lambda i, s: (0, 0)),
            scratch_shapes=[
                pltpu.VMEM((channels // TILE, height + 2 * REACH, width + 2 * EDGE, TILE), F32),
                pltpu.VMEM((rows, channels), F32),
            ],
        ),
        out_shape=shaped((rows, channels), BF16),
        compiler_params=params_of(),
        cost_estimate=cost(1 << 26, 1 << 20),
        name="early",
    )(sec, trial, *vectors[:4])
    received = trial
    features = None
    for tick in range(sections):
        operands = [received, early, *vectors, *pinned((own, *arrived))]
        in_specs = [whole(item) for item in operands[:9]] + [hbm_spec()] * members
        kept = 0 if features is None else 1
        if kept:
            operands += pinned([features])
            in_specs.append(hbm_spec())
        result, features = pl.pallas_call(
            functools.partial(probe_kernel, tick, side, tick < sections - 1, members - 1, kept),
            grid_spec=pltpu.PrefetchScalarGridSpec(
                num_scalar_prefetch=4,
                grid=(1,),
                in_specs=in_specs,
                out_specs=[whole(trial) if tick < sections - 1 else hbm_spec(), hbm_spec()],
                scratch_shapes=[
                    pltpu.VMEM((height, side, channels), BF16),
                    pltpu.VMEM((blocks, channels, TILE), BF16),
                    pltpu.VMEM(
                        (channels // TILE, height + 2 * REACH, width + 2 * EDGE, TILE), F32
                    ),
                    pltpu.VMEM((rows, channels), F32),
                    pltpu.VMEM((rows, channels), F32),
                    pltpu.VMEM((rows, channels), BF16),
                    pltpu.SemaphoreType.DMA((blocks,)),
                    pltpu.SemaphoreType.DMA,
                ],
            ),
            out_shape=[shaped(trial.shape, BF16), pltpu.HBM((height, side, channels), BF16)],
            input_output_aliases={3 + len(operands): 1} if kept else {},
            compiler_params=params_of(),
            cost_estimate=cost(4 * rows * channels * hid, 8 << 20),
            name=f"probe{tick}",
        )(sec, table["marked_order"], table["take_slots"], table["plain_order"], *operands)
        if tick < sections - 1:
            received = lax.ppermute(result, "section", [(tick, tick + 1)])
    return (new_first[None, None], new_second[None, None], features[None, None, None])


def solution(mesh):
    return jax.shard_map(
        local,
        mesh=mesh,
        in_specs=(
            P("member", None, None, None, None, None),
            P("member", None, None, None, None, None),
            P("member", None, None, None, None),
            P("member", "section", None, None, None),
            P("member", "section", None),
            P("member", "section", None),
            P("member", "section", None),
            P("member", "section", None, None),
            P("member", "section", None),
            P("member", "section", None, None),
            P("member", "section", None),
            P("member", "section", None),
            P("section", None),
            P("section", None, None),
        ),
        out_specs=(
            P("member", "section", None, None),
            P("member", "section", None, None),
            P("member", "section", None, None, None, None),
        ),
        check_vma=False,
    )
```
